32 devices in a mesh: gx: 4 (over z), gy: 4 (over y, core), gz: 2 (over x).
Axes of the slice: x: 2, y: 2, z: 4, core: 2. Of those that a mesh axis runs over, the one named last changes fastest.
Arguments:
- populations: float32 [19, 16, 32, 256], P(None, 'gx', 'gy', 'gz'), may hold values from 0.015 to 0.49, as said below
- grain_velocity: float32 [3, 1024, 128], P(None, ('gx', 'gy', 'gz')), may hold values from -1.2 to 1.2
- grain_volume: float32 [1024, 128], P(('gx', 'gy', 'gz')), may hold values from 0.05 to 0.4
- slots: int32 [1024, 128], P(('gx', 'gy', 'gz')), may hold values 0 or 1
- contacts: int32 [1024, 32], P(('gx', 'gy', 'gz')), may hold values 0 or 1
- bin_cell: int32 [1024], P(('gx', 'gy', 'gz')), may hold values from 0 to 1023, as said below
Outputs:
- fluid: float32 [19, 16, 32, 256], P(None, 'gx', 'gy', 'gz')
- grains: float32 [3, 1024, 128], P(None, ('gx', 'gy', 'gz'))
The draws below stay inside these ranges and needn't reach their ends.
Inputs may be any that keep to these rules, and one draw needn't show every extreme that they name: `populations`: each part of the grid of one device holds distributions near w_i times a factor of order one. bin_cell[b] is a column index as in the reference program. A bin's column lies in the cells of the same index of gz as the device that holds the bin. Of the 32 bins that one device holds, at most 8 have columns in the cells of any one device, and in every draw every holder reaches 8 for some device.
All inputs are finite; a program needn't handle non-finite values. No bound on the sum of `slots` or of `contacts` on one device may be relied on, other than what follows from the above.
Results may differ from the reference program's by a relative error of at most 0.0001.
Values sent between devices are 32-bit elements; how exact they have to be, the bound alone decides.
No kernel may reach another device: no remote copies, remote signals or barrier semaphores. Data moves between devices by JAX's collectives and lax.ppermute only.
A program may use at most 64 MiB of HBM per device.

```python
import math
import jax
import jax.numpy as jnp
import numpy as np
from jax import lax

CX = 4
CY = 8
CZ = 128
GRAINS = 128
BIN_DEV = 32
SUBSTEPS = 4
NX = 16
NY = 32
NZ = 256
NBINS = 1024


LATTICE_WEIGHTS = np.array([1.0 / 3.0] + [1.0 / 18.0] * 6 + [1.0 / 36.0] * 12)


def draw_populations(key, part):
    weights = jnp.asarray(LATTICE_WEIGHTS, jnp.float32).reshape(19, 1, 1, 1)
    factor = jax.random.uniform(key, (19, NX, NY, NZ), jnp.float32, 0.6, 1.4)
    return weights * factor


def draw_bin_cell(key, part):
    n_gx = NX // CX
    n_gy = NY // CY
    n_gz = NZ // CZ
    sources = n_gx * n_gy
    owners = sources * n_gz
    zblocks = CZ // GRAINS
    capacity = max(2, 4 * BIN_DEV // sources)
    keys = jax.random.split(key, 5)
    perms = jax.vmap(partial_perm(sources))(jax.random.split(keys[0], owners))
    orders = jax.vmap(partial_perm(BIN_DEV))(jax.random.split(keys[1], owners))
    place = jnp.arange(BIN_DEV, dtype=jnp.int32)
    group = jnp.where(place < capacity, 0, 1 + (place - capacity) % (sources - 1))
    group = group[orders]
    source = jnp.take_along_axis(perms, group, axis=1)
    owner_gz = (jnp.arange(owners, dtype=jnp.int32) % n_gz)[:, None]
    xcell = source // n_gy * CX + jax.random.randint(keys[2], (owners, BIN_DEV), 0, CX)
    ycell = source % n_gy * CY + jax.random.randint(keys[3], (owners, BIN_DEV), 0, CY)
    zblock = owner_gz * zblocks + jax.random.randint(keys[4], (owners, BIN_DEV), 0, zblocks)
    column = (xcell * NY + ycell) * (NZ // GRAINS) + zblock
    return column.reshape(-1).astype(jnp.int32)


def partial_perm(count):

    def permute(subkey):
        return jax.random.permutation(subkey, count).astype(jnp.int32)
    return permute


def touch_ends(values, rng, least, high):
    spot = [jax.random.randint(jax.random.fold_in(rng, axis), (), 0, length) for axis, length in enumerate(values.shape)]
    main_axis = values.shape.index(max(values.shape))
    next_to = spot[:main_axis] + [(spot[main_axis] + 1) % values.shape[main_axis]] + spot[main_axis + 1:]
    return values.at[tuple(spot)].set(least).at[tuple(next_to)].set(high)


def steps_of(stream_key, extent, pieces, low, largest):
    factor_of = 1.0
    for dim, shards_of in pieces:
        steps = jax.random.uniform(jax.random.fold_in(jax.random.fold_in(stream_key, 6), dim), (shards_of,), jnp.float32, low / len(pieces), largest / len(pieces))
        factor_of = factor_of * jnp.repeat(jnp.exp(steps), extent[dim] // shards_of).reshape((-1,) + (1,) * (len(extent) - 1 - dim))
    return factor_of


def noise(own_key, shape, scale, reach, shards=(), kind=jnp.bfloat16):
    values = scale * jax.random.normal(own_key, shape, jnp.float32)
    if shards:
        values = values * steps_of(own_key, shape, shards, -0.22, 0.18)
    return jnp.clip(values, -reach, reach).astype(kind)


def setup_inputs(seed: int = 0) -> dict:
    key_of = jax.random.split(jax.random.key(seed), 7)
    return {
        "populations": draw_populations(jax.random.fold_in(key_of[6], 71), 0),
        "grain_velocity": noise(key_of[1], (3, NBINS, GRAINS), 0.2, 1.2, ((1, 32),), jnp.float32),
        "grain_volume": jnp.clip(jnp.exp(math.log(0.4) - 2.0794415 * jax.random.uniform(key_of[2], (NBINS, GRAINS), jnp.float32) ** steps_of(key_of[2], (NBINS, GRAINS), ((0, 32),), -0.2, 0.2)), 0.05, 0.4),
        "slots": touch_ends((jax.random.randint(key_of[3], (NBINS, GRAINS), 0, 4) < 3).astype(jnp.int32), jax.random.fold_in(key_of[3], 1), 0, 1),
        "contacts": touch_ends((jax.random.randint(key_of[4], (NBINS, BIN_DEV), 0, 16) < 1).astype(jnp.int32), jax.random.fold_in(key_of[4], 1), 0, 1),
        "bin_cell": draw_bin_cell(jax.random.fold_in(key_of[6], 71), 0),
    }


VELOCITIES = np.array([[0, 0, 0], [1, 0, 0], [-1, 0, 0], [0, 1, 0], [0, -1, 0], [0, 0, 1], [0, 0, -1],
                       [1, 1, 0], [-1, -1, 0], [1, -1, 0], [-1, 1, 0],
                       [1, 0, 1], [-1, 0, -1], [1, 0, -1], [-1, 0, 1],
                       [0, 1, 1], [0, -1, -1], [0, 1, -1], [0, -1, 1]])
WEIGHTS = np.array([1.0 / 3.0] + [1.0 / 18.0] * 6 + [1.0 / 36.0] * 12)
OPPOSITE = [0, 2, 1, 4, 3, 6, 5, 8, 7, 10, 9, 12, 11, 14, 13, 16, 15, 18, 17]
relax_time = 0.8
contact_stiffness = 0.1
drag_factor = 2.0
gravity = 0.01


def moments(popul):
    density = jnp.sum(popul, axis=0)
    speed = []
    for axis in range(3):
        rising = np.array([i for i in range(19) if VELOCITIES[i, axis] == 1])
        falling = np.array([i for i in range(19) if VELOCITIES[i, axis] == -1])
        momentum = jnp.sum(popul[rising], axis=0) - jnp.sum(popul[falling], axis=0)
        speed.append(momentum / density)
    return density, speed


def grain_step(block, velocity, live, volume, links):
    grains = velocity.shape[2]
    bins = links.shape[1]
    groups = velocity.shape[1] // bins
    rate = drag_factor * volume * live
    drag = rate[None] * (block[:3] - velocity)
    moving = (velocity * live[None]).reshape(3, groups, bins, grains)
    pairs = links.reshape(groups, bins, bins)
    near = jnp.einsum('gkj,cgjs->cgks', pairs, moving, precision=lax.Precision.HIGHEST).reshape(3, -1, grains)
    count = jnp.einsum('gkj,gjs->gks', pairs, live.reshape(groups, bins, grains), precision=lax.Precision.HIGHEST).reshape(-1, grains)
    push = contact_stiffness * live[None] * (near - count[None] * velocity)
    fall = jnp.asarray([0.0, 0.0, gravity], jnp.float32).reshape(3, 1, 1) * live[None]
    updated = velocity + drag + push - fall
    forces = jnp.concatenate([-drag, (volume * live)[None]], axis=0)
    return updated, forces


def collide(popul, density, speed, field):
    scale = 1.0 / (1.0 + field[3])
    target = [scale * (speed[a] + relax_time * field[a] / density) for a in range(3)]
    square = target[0] * target[0] + target[1] * target[1] + target[2] * target[2]
    rows = []
    for i in range(19):
        along = jnp.zeros_like(density)
        for a in range(3):
            if VELOCITIES[i, a] != 0:
                along = along + float(VELOCITIES[i, a]) * target[a]
        equil = float(WEIGHTS[i]) * density * (1.0 + 3.0 * along + 4.5 * along * along - 1.5 * square)
        rows.append(popul[i] - (popul[i] - equil) / relax_time)
    return jnp.stack(rows)


def stream(post):
    depth = post.shape[3]
    zpos = jnp.arange(depth)
    rows = []
    for i in range(19):
        cx, cy, cz = int(VELOCITIES[i, 0]), int(VELOCITIES[i, 1]), int(VELOCITIES[i, 2])
        moved = jnp.roll(post[i], (cx, cy, cz), axis=(0, 1, 2))
        if cz == 1:
            moved = jnp.where(zpos == 0, post[OPPOSITE[i]], moved)
        elif cz == -1:
            moved = jnp.where(zpos == depth - 1, post[OPPOSITE[i]], moved)
        rows.append(moved)
    return jnp.stack(rows)


def reference(populations, grain_velocity, grain_volume, slots, contacts, bin_cell):
    live = slots.astype(jnp.float32)
    links = contacts.astype(jnp.float32)
    fluid = populations
    velocity = grain_velocity
    for step in range(SUBSTEPS):
        density, speed = moments(fluid)
        flow = jnp.stack(speed + [density]).reshape(4, -1, GRAINS)
        block = jnp.take(flow, bin_cell, axis=1)
        velocity, forces = grain_step(block, velocity, live, grain_volume, links)
        field = jnp.zeros_like(flow).at[:, bin_cell].add(forces).reshape(4, NX, NY, NZ)
        post = collide(fluid, density, speed, field)
        fluid = stream(post)
    return fluid, velocity
```

```python
import jax
import jax.numpy as jnp
import numpy as np
from jax import lax
from jax.experimental import pallas as pl
from jax.experimental.pallas import tpu as pltpu
from jax.sharding import PartitionSpec as P

SUBSTEPS = 4


VELOCITIES = np.array(
    [
        [0, 0, 0],
        [1, 0, 0],
        [-1, 0, 0],
        [0, 1, 0],
        [0, -1, 0],
        [0, 0, 1],
        [0, 0, -1],
        [1, 1, 0],
        [-1, -1, 0],
        [1, -1, 0],
        [-1, 1, 0],
        [1, 0, 1],
        [-1, 0, -1],
        [1, 0, -1],
        [-1, 0, 1],
        [0, 1, 1],
        [0, -1, -1],
        [0, 1, -1],
        [0, -1, 1],
    ]
)
WEIGHTS = np.array([1.0 / 3.0] + [1.0 / 18.0] * 6 + [1.0 / 36.0] * 12)
OPPOSITE = [0, 2, 1, 4, 3, 6, 5, 8, 7, 10, 9, 12, 11, 14, 13, 16, 15, 18, 17]
relax_time = 0.8
contact_stiffness = 0.1
drag_factor = 2.0
gravity = 0.01


def passed_along(x, axis, by):
    length = lax.axis_size(axis)
    return lax.ppermute(x, axis, [(i, (i + by) % length) for i in range(length)])


def passed_along_2(value, axis, steps):
    count = lax.axis_size(axis)
    leading, last = (max(0, -steps), min(count, count - steps))
    return lax.ppermute(value, axis, [(source, source + steps) for source in range(leading, last)])


def moments(popul):
    density = jnp.sum(popul, axis=0)
    speed = []
    for axis in range(3):
        rising = np.array([i for i in range(19) if VELOCITIES[i, axis] == 1])
        falling = np.array([i for i in range(19) if VELOCITIES[i, axis] == -1])
        momentum = jnp.sum(popul[rising], axis=0) - jnp.sum(popul[falling], axis=0)
        speed.append(momentum / density)
    return (density, speed)


def grain_step(block, velocity, live, volume, links):
    grains = velocity.shape[2]
    bins = links.shape[1]
    groups = velocity.shape[1] // bins
    rate = drag_factor * volume * live
    drag = rate[None] * (block[:3] - velocity)
    moving = (velocity * live[None]).reshape(3, groups, bins, grains)
    pairs = links.reshape(groups, bins, bins)
    near = jnp.einsum("gkj,cgjs->cgks", pairs, moving, precision=lax.Precision.HIGHEST).reshape(
        3, -1, grains
    )
    count = jnp.einsum(
        "gkj,gjs->gks", pairs, live.reshape(groups, bins, grains), precision=lax.Precision.HIGHEST
    ).reshape(-1, grains)
    push = contact_stiffness * live[None] * (near - count[None] * velocity)
    fall = jnp.asarray([0.0, 0.0, gravity], jnp.float32).reshape(3, 1, 1) * live[None]
    updated = velocity + drag + push - fall
    forces = jnp.concatenate([-drag, (volume * live)[None]], axis=0)
    return (updated, forces)


def collide(popul, density, speed, field):
    scale = 1.0 / (1.0 + field[3])
    target = [scale * (speed[a] + relax_time * field[a] / density) for a in range(3)]
    square = target[0] * target[0] + target[1] * target[1] + target[2] * target[2]
    rows = []
    for i in range(19):
        along = jnp.zeros_like(density)
        for a in range(3):
            if VELOCITIES[i, a] != 0:
                along = along + float(VELOCITIES[i, a]) * target[a]
        equil = (
            float(WEIGHTS[i]) * density * (1.0 + 3.0 * along + 4.5 * along * along - 1.5 * square)
        )
        rows.append(popul[i] - (popul[i] - equil) / relax_time)
    return jnp.stack(rows)


def walls(moved, post):
    depth = post.shape[3]
    zpos = jnp.arange(depth)
    bottom = (zpos == 0) & (lax.axis_index("gz") == 0)
    top = (zpos == depth - 1) & (lax.axis_index("gz") == lax.axis_size("gz") - 1)
    rows = []
    for i in range(19):
        layer = moved[i]
        if VELOCITIES[i, 2] == 1:
            layer = jnp.where(bottom, post[OPPOSITE[i]], layer)
        elif VELOCITIES[i, 2] == -1:
            layer = jnp.where(top, post[OPPOSITE[i]], layer)
        rows.append(layer)
    return jnp.stack(rows)


def leaving(axis):
    rising = np.array([i for i in range(19) if VELOCITIES[i, axis] == 1])
    falling = np.array([i for i in range(19) if VELOCITIES[i, axis] == -1])
    return (rising, falling)


def stream(post):
    moved = post
    rising, falling = leaving(0)
    upper = moved[rising]
    lower = moved[falling]
    edge_up = passed_along(upper[:, -1:], "gx", 1)
    edge_down = passed_along(lower[:, :1], "gx", -1)
    moved = moved.at[rising].set(jnp.concatenate([edge_up, upper[:, :-1]], axis=1))
    moved = moved.at[falling].set(jnp.concatenate([lower[:, 1:], edge_down], axis=1))
    rising, falling = leaving(1)
    upper = moved[rising]
    lower = moved[falling]
    edge_up = passed_along(upper[:, :, -1:], "gy", 1)
    edge_down = passed_along(lower[:, :, :1], "gy", -1)
    moved = moved.at[rising].set(jnp.concatenate([edge_up, upper[:, :, :-1]], axis=2))
    moved = moved.at[falling].set(jnp.concatenate([lower[:, :, 1:], edge_down], axis=2))
    rising, falling = leaving(2)
    upper = moved[rising]
    lower = moved[falling]
    edge_up = passed_along_2(upper[:, :, :, -1:], "gz", 1)
    edge_down = passed_along_2(lower[:, :, :, :1], "gz", -1)
    moved = moved.at[rising].set(jnp.concatenate([edge_up, upper[:, :, :, :-1]], axis=3))
    moved = moved.at[falling].set(jnp.concatenate([lower[:, :, :, 1:], edge_down], axis=3))
    return walls(moved, post)


def carry_flow(outgoing):
    result = lax.all_to_all(outgoing, ("gx", "gy"), split_axis=1, concat_axis=1, tiled=True)
    return result


def carry_force(outgoing):
    result = lax.all_to_all(outgoing, ("gx", "gy"), split_axis=1, concat_axis=1, tiled=True)
    return result


def rank_within(source):
    count = source.shape[-1]
    before = jnp.arange(count)[None, :] < jnp.arange(count)[:, None]
    same = source[..., :, None] == source[..., None, :]
    return jnp.sum((same & before).astype(jnp.int32), axis=-1)


def columns_body(populations, grain_velocity, grain_volume, slots, contacts, bin_cell):
    n_gx = lax.axis_size("gx")
    n_gy = lax.axis_size("gy")
    n_gz = lax.axis_size("gz")
    sources = n_gx * n_gy
    bins = contacts.shape[1]
    grains = grain_velocity.shape[2]
    depth_x, depth_y, depth_z = (populations.shape[1], populations.shape[2], populations.shape[3])
    zblocks = depth_z // grains
    capacity = max(2, 4 * bins // sources)
    width_y = depth_y * n_gy
    column_blocks = depth_z * n_gz // grains

    def locate(cells):
        xcell = cells // (width_y * column_blocks)
        ycell = cells // column_blocks % width_y
        zblock = cells % column_blocks
        source = xcell // depth_x * n_gy + ycell // depth_y
        local = (xcell % depth_x * depth_y + ycell % depth_y) * zblocks + zblock % zblocks
        return (source, local)

    own_source, own_local = locate(bin_cell)
    own_row = own_source * capacity + rank_within(own_source)
    every = lax.all_gather(bin_cell, ("gx", "gy"), axis=0, tiled=True).reshape(sources, bins)
    all_source, all_local = locate(every)
    all_rank = rank_within(all_source)
    here = lax.axis_index("gx") * n_gy + lax.axis_index("gy")
    slot_ids = jnp.arange(capacity, dtype=jnp.int32)
    picked = (all_source == here)[:, None, :] & (all_rank[:, None, :] == slot_ids[None, :, None])
    send_column = jnp.sum(jnp.where(picked, all_local[:, None, :], 0), axis=2).reshape(-1)
    send_mask = jnp.any(picked, axis=2).reshape(-1).astype(jnp.float32)
    live = slots.astype(jnp.float32)
    links = contacts.astype(jnp.float32)
    fluid = populations
    velocity = grain_velocity
    for step in range(SUBSTEPS):
        density, speed = moments(fluid)
        flow = jnp.stack(speed + [density]).reshape(4, -1, grains)
        outgoing = jnp.take(flow, send_column, axis=1) * send_mask[None, :, None]
        incoming = carry_flow(outgoing)
        block = jnp.take(incoming, own_row, axis=1)
        velocity, forces = grain_step(block, velocity, live, grain_volume, links)
        back = jnp.zeros((4, sources * capacity, grains), jnp.float32).at[:, own_row].set(forces)
        returned = carry_force(back)
        field = jnp.zeros_like(flow).at[:, send_column].add(returned * send_mask[None, :, None])
        field = field.reshape(4, depth_x, depth_y, depth_z)
        post = collide(fluid, density, speed, field)
        fluid = stream(post)
    return (fluid, velocity)


LANES = 128
SUBLANES = 8
VMEM = pl.BlockSpec(memory_space=pltpu.VMEM)
SMEM = pl.BlockSpec(memory_space=pltpu.SMEM)


class Plan:
    def __init__(self, n_gx, n_gy, n_gz, populations, contacts, grains):
        self.n_gx, self.n_gy, self.n_gz = n_gx, n_gy, n_gz
        self.dx, self.dy, self.depth = populations.shape[1:]
        self.grains = grains
        self.bins = contacts.shape[1]
        self.sources = n_gx * n_gy
        self.group = self.dx * self.dy
        self.halo = SUBSTEPS
        self.own = self.depth // self.sources
        self.rows = self.own + 2 * self.halo
        self.columns = self.sources * self.group
        self.per_tile = max(1, LANES // self.group)
        self.fields = 24
        self.tiles = self.fields // self.per_tile
        self.width = self.fields * self.group

    def fits(self):
        group = self.group
        return (
            self.sources > 1
            and self.depth == LANES
            and self.grains == LANES
            and self.depth % self.sources == 0
            and self.own % SUBLANES == 0
            and self.rows == 2 * SUBLANES
            and group == self.bins
            and group * group == SUBLANES * LANES
            and self.sources % self.per_tile == 0
        )


def swap_groups(parts, group):
    parts = list(parts)
    lane = lax.broadcasted_iota(jnp.int32, parts[0].shape, 1)
    step = len(parts) // 2
    while step:
        low = lane // (group * step) % 2 == 0
        for a in range(len(parts)):
            if a // step % 2 == 0:
                first, second = parts[a], parts[a + step]
                shift = group * step
                parts[a] = jnp.where(low, first, pltpu.roll(second, shift, 1))
                parts[a + step] = jnp.where(low, pltpu.roll(first, LANES - shift, 1), second)
        step //= 2
    return parts


def prepare_kernel(plan, pop_ref, vel_ref, vol_ref, slot_ref, cell_ref, link_ref, turned_ref, edge_ref):
    group, bins = plan.group, plan.bins
    rate = vol_ref[...] * slot_ref[...].astype(jnp.float32)
    whole = 19 * group // LANES
    for t in range(whole):
        turned_ref[:, t * LANES : (t + 1) * LANES] = pop_ref[t * LANES : (t + 1) * LANES, :].T
    tail = jnp.concatenate(
        [pop_ref[whole * LANES :, :], vel_ref[...], rate, jnp.zeros((bins, LANES), jnp.float32)], axis=0
    )
    for t in range(whole, plan.tiles):
        part = tail[(t - whole) * LANES : (t - whole + 1) * LANES, :].T
        if t == plan.tiles - 1:
            lane = lax.broadcasted_iota(jnp.int32, part.shape, 1)
            part = jnp.where(lane >= LANES - bins, cell_ref[...], part)
        turned_ref[:, t * LANES : (t + 1) * LANES] = part
    halo = plan.halo
    edge_ref[0:halo, : plan.width] = turned_ref[plan.depth - halo :, :]
    edge_ref[halo:, : plan.width] = turned_ref[0:halo, :]
    edge_ref[:, plan.width :] = link_ref[...]


def windows_kernel(plan, turned_ref, lower_ref, upper_ref, link_ref, out_ref, whole_ref):
    halo, own, rows, width = plan.halo, plan.own, plan.rows, plan.width
    whole_ref[0:halo, :] = lower_ref[0:halo, :width]
    whole_ref[halo : halo + plan.depth, :] = turned_ref[...]
    whole_ref[halo + plan.depth :, :] = upper_ref[halo:, :width]
    for p in range(plan.sources):
        out_ref[p, :, :width] = whole_ref[p * own : p * own + rows, :]
        out_ref[p, :SUBLANES, width:] = link_ref[...]
        if p == 0:
            other = lower_ref[:, width:]
        elif p == plan.sources - 1:
            other = upper_ref[:, width:]
        else:
            other = link_ref[...]
        out_ref[p, SUBLANES:, width:] = other


def three_parts(x):
    high = x.astype(jnp.bfloat16)
    rest = x - high.astype(jnp.float32)
    middle = rest.astype(jnp.bfloat16)
    low = (rest - middle.astype(jnp.float32)).astype(jnp.bfloat16)
    return high, middle, low


def exact_dot(parts, matrix, contract):
    stacked = jnp.concatenate([piece for x in parts for piece in three_parts(x)], axis=0)
    out = lax.dot_general(
        stacked, matrix, (((1,), (contract,)), ((), ())), preferred_element_type=jnp.float32
    )
    rows = parts[0].shape[0]
    result = []
    for i in range(len(parts)):
        at = 3 * i * rows
        result.append(
            (out[at + 2 * rows : at + 3 * rows] + out[at + rows : at + 2 * rows]) + out[at : at + rows]
        )
    return result


def shifted(plan, x, axis, by):
    size = plan.columns
    lane = lax.broadcasted_iota(jnp.int32, x.shape, 1)
    group, dx, dy = plan.group, plan.dx, plan.dy

    def back(amount):
        return pltpu.roll(x, (by * amount) % size, 1) if amount % size else x

    if axis == 0:
        place = lane % group // dy
        edge = place == (0 if by == 1 else dx - 1)
        return jnp.where(edge, back(plan.n_gy * group - (dx - 1) * dy), back(dy))
    place = lane % dy
    holder = lane // group % plan.n_gy
    edge = place == (0 if by == 1 else dy - 1)
    last = holder == (0 if by == 1 else plan.n_gy - 1)
    across = jnp.where(last, back(-((plan.n_gy - 1) * group + dy - 1)), back(group - dy + 1))
    return jnp.where(edge, across, back(1))


def substeps_kernel(plan, where_ref, in_ref, out_ref, f_ref, post_ref, u_ref, force_ref, v_ref, aux_ref,
                    column_ref, link_ref):
    rows, columns, group, per = plan.rows, plan.columns, plan.group, plan.per_tile
    halo, own = plan.halo, plan.own
    quads = plan.sources // per
    first, last = where_ref[0] == 1, where_ref[1] == 1
    ground, ceiling = where_ref[2] == 1, where_ref[3] == 1

    for t in range(plan.tiles):
        for q in range(quads):
            lanes = slice(q * LANES, (q + 1) * LANES)
            parts = [in_ref[q * per + s, :, t * LANES : (t + 1) * LANES] for s in range(per)]
            for j, part in enumerate(swap_groups(parts, group)):
                field = t * per + j
                if field < 19:
                    f_ref[field, :, lanes] = part
                elif field < 22:
                    v_ref[field - 19, :, lanes] = part
                else:
                    aux_ref[field - 22, :, lanes] = part

    rate = aux_ref[0]
    live = (rate > 0.0).astype(jnp.float32)
    cells = aux_ref[1]
    other_cells = jnp.where(first, cells[0:1, :], cells[rows - 1 : rows, :])
    which = lax.broadcasted_iota(jnp.int32, (columns, columns), 0).astype(jnp.float32)
    for k, chosen in enumerate((cells[halo : halo + 1, :], other_cells)):
        column_ref[k] = (which == chosen).astype(jnp.float32).astype(jnp.bfloat16)
    lane = lax.broadcasted_iota(jnp.int32, (SUBLANES, LANES), 1)
    for k in range(2):
        for s in range(plan.sources):
            packed = in_ref[s, k * SUBLANES : (k + 1) * SUBLANES, plan.width :]
            place = s % per
            pieces = []
            for g in range(per):
                moved = packed if g == place else pltpu.roll(packed, (place - g) * group % LANES, 1)
                pieces.append(jnp.where(lane // group == place, moved, 0.0))
            link_ref[k, s * group : (s + 1) * group, :] = jnp.concatenate(pieces, axis=0).astype(jnp.bfloat16)

    row = lax.broadcasted_iota(jnp.int32, (rows, columns), 0)
    foreign = (first & (row < halo)) | (last & (row >= halo + own))

    def choose(mine, others):
        return [jnp.where(foreign, b, a) for a, b in zip(mine, others)]

    def on_columns(parts, contract):
        return choose(
            exact_dot(parts, column_ref[0], contract), exact_dot(parts, column_ref[1], contract)
        )

    def near(parts):
        both = []
        for k in range(2):
            blocks = [
                exact_dot(
                    [x[:, q * LANES : (q + 1) * LANES] for x in parts],
                    link_ref[k, q * LANES : (q + 1) * LANES, :],
                    1,
                )
                for q in range(quads)
            ]
            both.append([jnp.concatenate([b[i] for b in blocks], axis=1) for i in range(len(parts))])
        return choose(*both)

    force_ref[3] = on_columns([rate], 1)[0]
    count = near([live])[0]
    aux_ref[1] = count

    def step(_, carry):
        for q in range(quads):
            lanes = slice(q * LANES, (q + 1) * LANES)
            popul = [f_ref[i, :, lanes] for i in range(19)]
            density = popul[0]
            for i in range(1, 19):
                density = density + popul[i]
            u_ref[3, :, lanes] = density
            for a in range(3):
                rising = [popul[i] for i in range(19) if VELOCITIES[i, a] == 1]
                falling = [popul[i] for i in range(19) if VELOCITIES[i, a] == -1]
                u_ref[a, :, lanes] = (sum(rising[1:], rising[0]) - sum(falling[1:], falling[0])) / density
        rate = aux_ref[0]
        count = aux_ref[1]
        live = (rate > 0.0).astype(jnp.float32)
        speed = on_columns([u_ref[a] for a in range(3)], 0)
        velocity = [v_ref[a] for a in range(3)]
        touching = near([velocity[a] * live for a in range(3)])
        drags = [drag_factor * rate * (speed[a] - velocity[a]) for a in range(3)]
        for a, force in enumerate(on_columns([-d for d in drags], 1)):
            force_ref[a] = force
        for a in range(3):
            push = contact_stiffness * live * (touching[a] - count * velocity[a])
            updated = velocity[a] + drags[a] + push
            if a == 2:
                updated = updated - gravity * live
            v_ref[a] = updated
        for q in range(quads):
            lanes = slice(q * LANES, (q + 1) * LANES)
            density = u_ref[3, :, lanes]
            scale = 1.0 / (1.0 + force_ref[3, :, lanes])
            target = [
                scale * (u_ref[a, :, lanes] + relax_time * force_ref[a, :, lanes] / density)
                for a in range(3)
            ]
            square = target[0] * target[0] + target[1] * target[1] + target[2] * target[2]
            base = 1.0 - 1.5 * square
            for i in range(19):
                along = None
                for a in range(3):
                    if VELOCITIES[i, a] != 0:
                        term = target[a] if VELOCITIES[i, a] == 1 else -target[a]
                        along = term if along is None else along + term
                shape = base if along is None else base + along * (3.0 + 4.5 * along)
                equil = (float(WEIGHTS[i]) * density) * shape
                popul = f_ref[i, :, lanes]
                post_ref[i, :, lanes] = popul - (popul - equil) * (1.0 / relax_time)
        bottom = ground & (row == halo)
        top = ceiling & (row == halo + own - 1)
        for i in range(19):
            moved = post_ref[i]
            for axis in range(2):
                if VELOCITIES[i, axis] != 0:
                    moved = shifted(plan, moved, axis, int(VELOCITIES[i, axis]))
            if VELOCITIES[i, 2] == 1:
                moved = jnp.where(bottom, post_ref[OPPOSITE[i]], pltpu.roll(moved, 1, 0))
            elif VELOCITIES[i, 2] == -1:
                moved = jnp.where(top, post_ref[OPPOSITE[i]], pltpu.roll(moved, rows - 1, 0))
            f_ref[i] = moved
        return carry

    lax.fori_loop(0, SUBSTEPS, step, 0)

    for t in range(plan.tiles):
        for q in range(quads):
            lanes = slice(q * LANES, (q + 1) * LANES)
            parts = []
            for j in range(per):
                field = t * per + j
                if field < 19:
                    part = f_ref[field, halo : halo + own, lanes]
                elif field < 22:
                    part = v_ref[field - 19, halo : halo + own, lanes]
                else:
                    part = jnp.zeros((own, LANES), jnp.float32)
                parts.append(part)
            for s, part in enumerate(swap_groups(parts, group)):
                out_ref[q * per + s, :, t * LANES : (t + 1) * LANES] = part


def finish_kernel(plan, in_ref, pop_ref, vel_ref):
    group = plan.group
    whole = 19 * group // LANES
    rest = 19 * group - whole * LANES
    tail = []
    for t in range(plan.tiles):
        part = in_ref[:, t * LANES : (t + 1) * LANES].T
        if t < whole:
            pop_ref[t * LANES : (t + 1) * LANES, :] = part
        else:
            tail.append(part)
    tail = jnp.concatenate(tail, axis=0)
    pop_ref[whole * LANES :, :] = tail[:rest, :]
    vel_ref[...] = tail[rest : rest + 3 * plan.bins, :]


def windows_body(plan, populations, grain_velocity, grain_volume, slots, contacts, bin_cell):
    group, bins, sources = plan.group, plan.bins, plan.sources
    n_gx, n_gy, n_gz = plan.n_gx, plan.n_gy, plan.n_gz
    wide = plan.width + LANES
    column_blocks = n_gz
    width_y = plan.dy * n_gy
    xcell = bin_cell // (width_y * column_blocks)
    ycell = bin_cell // column_blocks % width_y
    source = xcell // plan.dx * n_gy + ycell // plan.dy
    place = source * group + xcell % plan.dx * plan.dy + ycell % plan.dy
    cell_row = jnp.pad(place.astype(jnp.float32), (LANES - bins, 0)).reshape(1, LANES)
    links = contacts.reshape(-1, SUBLANES, bins).transpose(1, 0, 2).reshape(SUBLANES, LANES)
    links = links.astype(jnp.float32)
    f32 = jnp.float32

    def call(kernel, shapes, inputs, scratch=(), specs=None):
        return pl.pallas_call(
            lambda *refs: kernel(plan, *refs),
            out_shape=shapes,
            in_specs=specs or [VMEM] * len(inputs),
            out_specs=jax.tree.map(lambda _: VMEM, shapes),
            scratch_shapes=list(scratch),
        )(*inputs)

    turned, edge = call(
        prepare_kernel,
        (
            jax.ShapeDtypeStruct((plan.depth, plan.width), f32),
            jax.ShapeDtypeStruct((2 * plan.halo, wide), f32),
        ),
        (
            populations.reshape(19 * group, LANES),
            grain_velocity.reshape(3 * bins, LANES),
            grain_volume,
            slots,
            cell_row,
            links,
        ),
    )
    if n_gz == 1:
        lower = upper = edge
    elif n_gz == 2:
        lower = upper = lax.ppermute(edge, "gz", [(0, 1), (1, 0)])
    else:
        lower = passed_along(edge, "gz", 1)
        upper = passed_along(edge, "gz", -1)
    outgoing = call(
        windows_kernel,
        jax.ShapeDtypeStruct((sources, plan.rows, wide), f32),
        (turned, lower, upper, links),
        (pltpu.VMEM((plan.depth + 2 * plan.halo, plan.width), f32),),
    )
    incoming = lax.all_to_all(outgoing, ("gx", "gy"), split_axis=0, concat_axis=0, tiled=True)
    here = lax.axis_index("gx") * n_gy + lax.axis_index("gy")
    layer = lax.axis_index("gz")
    first, last = here == 0, here == sources - 1
    place = jnp.stack([first, last, first & (layer == 0), last & (layer == n_gz - 1)]).astype(jnp.int32)
    rows, columns = plan.rows, plan.columns
    back = call(
        substeps_kernel,
        jax.ShapeDtypeStruct((sources, plan.own, plan.width), f32),
        (place, incoming),
        (
            pltpu.VMEM((19, rows, columns), f32),
            pltpu.VMEM((19, rows, columns), f32),
            pltpu.VMEM((4, rows, columns), f32),
            pltpu.VMEM((4, rows, columns), f32),
            pltpu.VMEM((3, rows, columns), f32),
            pltpu.VMEM((2, rows, columns), f32),
            pltpu.VMEM((2, columns, columns), jnp.bfloat16),
            pltpu.VMEM((2, columns, LANES), jnp.bfloat16),
        ),
        [SMEM, VMEM],
    )
    result = lax.all_to_all(back, ("gx", "gy"), split_axis=0, concat_axis=0, tiled=True)
    fluid, velocity = call(
        finish_kernel,
        (
            jax.ShapeDtypeStruct((19 * group, LANES), f32),
            jax.ShapeDtypeStruct((3 * bins, LANES), f32),
        ),
        (result.reshape(plan.depth, plan.width),),
    )
    return (fluid.reshape(populations.shape), velocity.reshape(grain_velocity.shape))


def body(populations, grain_velocity, grain_volume, slots, contacts, bin_cell):
    plan = Plan(
        lax.axis_size("gx"),
        lax.axis_size("gy"),
        lax.axis_size("gz"),
        populations,
        contacts,
        grain_velocity.shape[2],
    )
    arrays = (populations, grain_velocity, grain_volume, slots, contacts, bin_cell)
    if plan.fits() and contacts.shape[0] == contacts.shape[1]:
        return windows_body(plan, *arrays)
    return columns_body(*arrays)


def solution(mesh):
    placed = (
        P(None, "gx", "gy", "gz"),
        P(None, ("gx", "gy", "gz"), None),
        P(("gx", "gy", "gz"), None),
        P(("gx", "gy", "gz"), None),
        P(("gx", "gy", "gz"), None),
        P(("gx", "gy", "gz")),
    )
    return jax.shard_map(
        body,
        mesh=mesh,
        in_specs=placed,
        out_specs=(P(None, "gx", "gy", "gz"), P(None, ("gx", "gy", "gz"), None)),
        check_vma=False,
    )
```

```python
import jax
import jax.numpy as jnp
import numpy as np
from jax import lax
from jax.experimental import pallas as pl
from jax.experimental.pallas import tpu as pltpu
from jax.sharding import PartitionSpec as P

SUBSTEPS = 4


VELOCITIES = np.array(
    [
        [0, 0, 0],
        [1, 0, 0],
        [-1, 0, 0],
        [0, 1, 0],
        [0, -1, 0],
        [0, 0, 1],
        [0, 0, -1],
        [1, 1, 0],
        [-1, -1, 0],
        [1, -1, 0],
        [-1, 1, 0],
        [1, 0, 1],
        [-1, 0, -1],
        [1, 0, -1],
        [-1, 0, 1],
        [0, 1, 1],
        [0, -1, -1],
        [0, 1, -1],
        [0, -1, 1],
    ]
)
WEIGHTS = np.array([1.0 / 3.0] + [1.0 / 18.0] * 6 + [1.0 / 36.0] * 12)
OPPOSITE = [0, 2, 1, 4, 3, 6, 5, 8, 7, 10, 9, 12, 11, 14, 13, 16, 15, 18, 17]
relax_time = 0.8
contact_stiffness = 0.1
drag_factor = 2.0
gravity = 0.01


def passed_along(x, axis, by):
    length = lax.axis_size(axis)
    return lax.ppermute(x, axis, [(i, (i + by) % length) for i in range(length)])


def passed_along_2(value, axis, steps):
    count = lax.axis_size(axis)
    leading, last = (max(0, -steps), min(count, count - steps))
    return lax.ppermute(value, axis, [(source, source + steps) for source in range(leading, last)])


def moments(popul):
    density = jnp.sum(popul, axis=0)
    speed = []
    for axis in range(3):
        rising = np.array([i for i in range(19) if VELOCITIES[i, axis] == 1])
        falling = np.array([i for i in range(19) if VELOCITIES[i, axis] == -1])
        momentum = jnp.sum(popul[rising], axis=0) - jnp.sum(popul[falling], axis=0)
        speed.append(momentum / density)
    return (density, speed)


def grain_step(block, velocity, live, volume, links):
    grains = velocity.shape[2]
    bins = links.shape[1]
    groups = velocity.shape[1] // bins
    rate = drag_factor * volume * live
    drag = rate[None] * (block[:3] - velocity)
    moving = (velocity * live[None]).reshape(3, groups, bins, grains)
    pairs = links.reshape(groups, bins, bins)
    near = jnp.einsum("gkj,cgjs->cgks", pairs, moving, precision=lax.Precision.HIGHEST).reshape(
        3, -1, grains
    )
    count = jnp.einsum(
        "gkj,gjs->gks", pairs, live.reshape(groups, bins, grains), precision=lax.Precision.HIGHEST
    ).reshape(-1, grains)
    push = contact_stiffness * live[None] * (near - count[None] * velocity)
    fall = jnp.asarray([0.0, 0.0, gravity], jnp.float32).reshape(3, 1, 1) * live[None]
    updated = velocity + drag + push - fall
    forces = jnp.concatenate([-drag, (volume * live)[None]], axis=0)
    return (updated, forces)


def collide(popul, density, speed, field):
    scale = 1.0 / (1.0 + field[3])
    target = [scale * (speed[a] + relax_time * field[a] / density) for a in range(3)]
    square = target[0] * target[0] + target[1] * target[1] + target[2] * target[2]
    rows = []
    for i in range(19):
        along = jnp.zeros_like(density)
        for a in range(3):
            if VELOCITIES[i, a] != 0:
                along = along + float(VELOCITIES[i, a]) * target[a]
        equil = (
            float(WEIGHTS[i]) * density * (1.0 + 3.0 * along + 4.5 * along * along - 1.5 * square)
        )
        rows.append(popul[i] - (popul[i] - equil) / relax_time)
    return jnp.stack(rows)


def walls(moved, post):
    depth = post.shape[3]
    zpos = jnp.arange(depth)
    bottom = (zpos == 0) & (lax.axis_index("gz") == 0)
    top = (zpos == depth - 1) & (lax.axis_index("gz") == lax.axis_size("gz") - 1)
    rows = []
    for i in range(19):
        layer = moved[i]
        if VELOCITIES[i, 2] == 1:
            layer = jnp.where(bottom, post[OPPOSITE[i]], layer)
        elif VELOCITIES[i, 2] == -1:
            layer = jnp.where(top, post[OPPOSITE[i]], layer)
        rows.append(layer)
    return jnp.stack(rows)


def leaving(axis):
    rising = np.array([i for i in range(19) if VELOCITIES[i, axis] == 1])
    falling = np.array([i for i in range(19) if VELOCITIES[i, axis] == -1])
    return (rising, falling)


def stream(post):
    moved = post
    rising, falling = leaving(0)
    upper = moved[rising]
    lower = moved[falling]
    edge_up = passed_along(upper[:, -1:], "gx", 1)
    edge_down = passed_along(lower[:, :1], "gx", -1)
    moved = moved.at[rising].set(jnp.concatenate([edge_up, upper[:, :-1]], axis=1))
    moved = moved.at[falling].set(jnp.concatenate([lower[:, 1:], edge_down], axis=1))
    rising, falling = leaving(1)
    upper = moved[rising]
    lower = moved[falling]
    edge_up = passed_along(upper[:, :, -1:], "gy", 1)
    edge_down = passed_along(lower[:, :, :1], "gy", -1)
    moved = moved.at[rising].set(jnp.concatenate([edge_up, upper[:, :, :-1]], axis=2))
    moved = moved.at[falling].set(jnp.concatenate([lower[:, :, 1:], edge_down], axis=2))
    rising, falling = leaving(2)
    upper = moved[rising]
    lower = moved[falling]
    edge_up = passed_along_2(upper[:, :, :, -1:], "gz", 1)
    edge_down = passed_along_2(lower[:, :, :, :1], "gz", -1)
    moved = moved.at[rising].set(jnp.concatenate([edge_up, upper[:, :, :, :-1]], axis=3))
    moved = moved.at[falling].set(jnp.concatenate([lower[:, :, :, 1:], edge_down], axis=3))
    return walls(moved, post)


def carry_flow(outgoing):
    result = lax.all_to_all(outgoing, ("gx", "gy"), split_axis=1, concat_axis=1, tiled=True)
    return result


def carry_force(outgoing):
    result = lax.all_to_all(outgoing, ("gx", "gy"), split_axis=1, concat_axis=1, tiled=True)
    return result


def rank_within(source):
    count = source.shape[-1]
    before = jnp.arange(count)[None, :] < jnp.arange(count)[:, None]
    same = source[..., :, None] == source[..., None, :]
    return jnp.sum((same & before).astype(jnp.int32), axis=-1)


def columns_body(populations, grain_velocity, grain_volume, slots, contacts, bin_cell):
    n_gx = lax.axis_size("gx")
    n_gy = lax.axis_size("gy")
    n_gz = lax.axis_size("gz")
    sources = n_gx * n_gy
    bins = contacts.shape[1]
    grains = grain_velocity.shape[2]
    depth_x, depth_y, depth_z = (populations.shape[1], populations.shape[2], populations.shape[3])
    zblocks = depth_z // grains
    capacity = max(2, 4 * bins // sources)
    width_y = depth_y * n_gy
    column_blocks = depth_z * n_gz // grains

    def locate(cells):
        xcell = cells // (width_y * column_blocks)
        ycell = cells // column_blocks % width_y
        zblock = cells % column_blocks
        source = xcell // depth_x * n_gy + ycell // depth_y
        local = (xcell % depth_x * depth_y + ycell % depth_y) * zblocks + zblock % zblocks
        return (source, local)

    own_source, own_local = locate(bin_cell)
    own_row = own_source * capacity + rank_within(own_source)
    every = lax.all_gather(bin_cell, ("gx", "gy"), axis=0, tiled=True).reshape(sources, bins)
    all_source, all_local = locate(every)
    all_rank = rank_within(all_source)
    here = lax.axis_index("gx") * n_gy + lax.axis_index("gy")
    slot_ids = jnp.arange(capacity, dtype=jnp.int32)
    picked = (all_source == here)[:, None, :] & (all_rank[:, None, :] == slot_ids[None, :, None])
    send_column = jnp.sum(jnp.where(picked, all_local[:, None, :], 0), axis=2).reshape(-1)
    send_mask = jnp.any(picked, axis=2).reshape(-1).astype(jnp.float32)
    live = slots.astype(jnp.float32)
    links = contacts.astype(jnp.float32)
    fluid = populations
    velocity = grain_velocity
    for step in range(SUBSTEPS):
        density, speed = moments(fluid)
        flow = jnp.stack(speed + [density]).reshape(4, -1, grains)
        outgoing = jnp.take(flow, send_column, axis=1) * send_mask[None, :, None]
        incoming = carry_flow(outgoing)
        block = jnp.take(incoming, own_row, axis=1)
        velocity, forces = grain_step(block, velocity, live, grain_volume, links)
        back = jnp.zeros((4, sources * capacity, grains), jnp.float32).at[:, own_row].set(forces)
        returned = carry_force(back)
        field = jnp.zeros_like(flow).at[:, send_column].add(returned * send_mask[None, :, None])
        field = field.reshape(4, depth_x, depth_y, depth_z)
        post = collide(fluid, density, speed, field)
        fluid = stream(post)
    return (fluid, velocity)


LANES = 128
SUBLANES = 8
VMEM_LIMIT = 24 * 1024 * 1024
VMEM = pl.BlockSpec(memory_space=pltpu.VMEM)
FIELD_V = (19, 21, 22)
FIELD_CELL = 20
FIELD_RATE = 23


class Plan:
    def __init__(self, n_gx, n_gy, n_gz, populations, contacts, grains):
        self.n_gx, self.n_gy, self.n_gz = n_gx, n_gy, n_gz
        self.dx, self.dy, self.depth = populations.shape[1:]
        self.grains = grains
        self.bins = contacts.shape[1]
        self.sources = n_gx * n_gy
        self.group = self.dx * self.dy
        self.halo = SUBSTEPS
        self.own = self.depth // self.sources
        self.rows = self.own + 2 * self.halo
        self.columns = self.sources * self.group
        self.per_tile = max(1, LANES // self.group)
        self.fields = 24
        self.tiles = self.fields // self.per_tile
        self.width = self.fields * self.group
        self.wide = self.width + LANES

    def fits(self):
        group = self.group
        return (
            self.sources % 2 == 0
            and self.depth == LANES
            and self.grains == LANES
            and self.own * self.sources == LANES
            and self.own == SUBLANES
            and self.rows == 2 * SUBLANES
            and group == self.bins
            and group * group == SUBLANES * LANES
            and self.per_tile == self.n_gy
        )

    def device(self, window):
        layer, place = divmod(window, self.sources)
        if layer % 2:
            place = self.sources - 1 - place
        return place * self.n_gz + layer

    def swaps(self, start):
        count = self.n_gz * self.sources
        paired = []
        for a in range(start, count - 1, 2):
            paired += [(a, a + 1), (a + 1, a)]
        if start:
            paired += [(0, 0), (count - 1, count - 1)]
        return [(self.device(a), self.device(b)) for a, b in paired]

    def place(self):
        layer = lax.axis_index("gz")
        here = lax.axis_index("gx") * self.n_gy + lax.axis_index("gy")
        return jnp.where(lax.rem(layer, 2) == 1, self.sources - 1 - here, here), layer

    def holder(self, window):
        layer = lax.axis_index("gz")
        return jnp.where(lax.rem(layer, 2) == 1, self.sources - 1 - window, window)


def swap_groups(parts, group):
    parts = list(parts)
    lane = lax.broadcasted_iota(jnp.int32, parts[0].shape, 1)
    step = len(parts) // 2
    while step:
        low = lane // (group * step) % 2 == 0
        for a in range(len(parts)):
            if a // step % 2 == 0:
                first, second = parts[a], parts[a + step]
                shift = group * step
                parts[a] = jnp.where(low, first, pltpu.roll(second, shift, 1))
                parts[a + step] = jnp.where(low, pltpu.roll(first, LANES - shift, 1), second)
        step //= 2
    return parts


def prepare_kernel(plan, pop_ref, vel_ref, vol_ref, slot_ref, link_ref, cell_ref, out_ref):
    group, bins, own = plan.group, plan.bins, plan.own
    whole = 19 * group // LANES
    cell = cell_ref[...]
    width_y = plan.dy * plan.n_gy
    xcell = lax.div(cell, width_y * plan.n_gz)
    ycell = lax.rem(lax.div(cell, plan.n_gz), width_y)
    source = lax.div(xcell, plan.dx) * plan.n_gy + lax.div(ycell, plan.dy)
    cell = source * group + lax.rem(xcell, plan.dx) * plan.dy + lax.rem(ycell, plan.dy)
    cell = jnp.concatenate([cell.astype(jnp.float32), jnp.zeros((1, LANES - bins), jnp.float32)], axis=1)
    packed = jnp.concatenate(
        [link_ref[g * SUBLANES : (g + 1) * SUBLANES, :].astype(jnp.float32) for g in range(bins // SUBLANES)],
        axis=1,
    )
    holders = [plan.holder(q) for q in range(plan.sources)]
    for t in range(plan.tiles):
        if t < whole:
            block = pop_ref[t * LANES : (t + 1) * LANES, :]
        elif t == whole:
            block = jnp.concatenate([pop_ref[whole * LANES :, :], vel_ref[:bins, :]], axis=0)
        else:
            rate = vol_ref[...] * slot_ref[...].astype(jnp.float32)
            block = jnp.concatenate([rate, vel_ref[bins:, :], rate], axis=0)
        block = block.T
        if t == plan.tiles - 1:
            lane = lax.broadcasted_iota(jnp.int32, block.shape, 1)
            block = jnp.where(lane < bins, cell, block)
        for q in range(plan.sources):
            out_ref[holders[q], :, t * LANES : (t + 1) * LANES] = block[q * own : (q + 1) * own, :]
    for q in range(plan.sources):
        out_ref[q, :, plan.width :] = packed


def edges_kernel(plan, in_ref, inner_ref, outer_ref):
    window, _ = plan.place()
    even = lax.rem(window, 2) == 0
    halo = plan.halo
    low_rows = lax.broadcasted_iota(jnp.int32, (SUBLANES, LANES), 0) < halo
    for h in range(plan.sources // 2):
        for t in range(plan.tiles):
            lanes = slice(t * LANES, (t + 1) * LANES)
            a, b = in_ref[2 * h, :, lanes], in_ref[2 * h + 1, :, lanes]
            low = jnp.where(low_rows, a, pltpu.roll(b, halo, 0))
            high = jnp.where(low_rows, pltpu.roll(a, halo, 0), b)
            inner_ref[h, :, lanes] = jnp.where(even, high, low)
            outer_ref[h, :, lanes] = jnp.where(even, low, high)
        for k in range(2):
            start = plan.width + k * LANES
            outer_ref[h, :, start : start + LANES] = in_ref[2 * h + k, :, plan.width :]


def two_part_dot(parts, matrix, contract):
    whole = jnp.concatenate(parts, axis=0)
    rest = whole - whole.astype(jnp.bfloat16).astype(jnp.float32)
    stacked = jnp.concatenate([whole, rest], axis=0).astype(jnp.bfloat16)
    out = lax.dot_general(
        stacked, matrix, (((1,), (contract,)), ((), ())), preferred_element_type=jnp.float32
    )
    rows = parts[0].shape[0]
    half = rows * len(parts)
    return [
        out[i * rows : (i + 1) * rows] + out[half + i * rows : half + (i + 1) * rows]
        for i in range(len(parts))
    ]


def substeps_kernel(plan, in_ref, inner_ref, outer_ref, out_ref, f_ref, post_ref, u_ref, force_ref, v_ref,
                    aux_ref, column_ref, link_ref):
    rows, columns, group, per = plan.rows, plan.columns, plan.group, plan.per_tile
    halo, own, dx, dy = plan.halo, plan.own, plan.dx, plan.dy
    quads = plan.sources // per
    window, layer = plan.place()
    even = lax.rem(window, 2) == 0
    first, last = window == 0, window == plan.sources - 1
    ground, ceiling = first & (layer == 0), last & (layer == plan.n_gz - 1)
    tile_row = lax.broadcasted_iota(jnp.int32, (SUBLANES, LANES), 0)

    def store(field, lanes, part):
        if field < 19:
            f_ref[field, :, lanes] = part
        elif field in FIELD_V:
            v_ref[FIELD_V.index(field), :, lanes] = part
        else:
            aux_ref[0 if field == FIELD_RATE else 1, :, lanes] = part

    for t in range(plan.tiles):
        at = slice(t * LANES, (t + 1) * LANES)
        for q in range(quads):
            parts = []
            for s in range(q * per, (q + 1) * per):
                inner, outer = inner_ref[s // 2, :, at], outer_ref[s // 2, :, at]
                below = jnp.where(even, outer, inner)
                above = jnp.where(even, inner, outer)
                if s % 2:
                    below = pltpu.roll(below, halo, 0)
                else:
                    above = pltpu.roll(above, halo, 0)
                turned = pltpu.roll(in_ref[s, :, at], halo, 0)
                parts.append(
                    jnp.concatenate(
                        [jnp.where(tile_row < halo, below, turned), jnp.where(tile_row < halo, turned, above)],
                        axis=0,
                    )
                )
            lanes = slice(q * LANES, (q + 1) * LANES)
            for j, part in enumerate(swap_groups(parts, group)):
                store(t * per + j, lanes, part)

    rate = aux_ref[0]
    live = (rate > 0.0).astype(jnp.float32)
    cells = aux_ref[1]
    other_cells = jnp.where(first, cells[0:1, :], cells[rows - 1 : rows, :])
    which = lax.broadcasted_iota(jnp.int32, (columns, columns), 0).astype(jnp.float32)
    for k, chosen in enumerate((cells[halo : halo + 1, :], other_cells)):
        column_ref[k] = (which == chosen).astype(jnp.float32).astype(jnp.bfloat16)
    lane = lax.broadcasted_iota(jnp.int32, (SUBLANES, LANES), 1)
    for k in range(2):
        for s in range(plan.sources):
            if k == 0:
                packed = in_ref[s, :, plan.width :]
            else:
                start = plan.width + s % 2 * LANES
                packed = outer_ref[s // 2, :, start : start + LANES]
            place = s % per
            pieces = []
            for g in range(per):
                moved = packed if g == place else pltpu.roll(packed, (place - g) * group % LANES, 1)
                pieces.append(jnp.where(lane // group == place, moved, 0.0))
            link_ref[k, s * group : (s + 1) * group, :] = jnp.concatenate(pieces, axis=0).astype(jnp.bfloat16)

    row = lax.broadcasted_iota(jnp.int32, (rows, columns), 0)
    tile_rows = lax.broadcasted_iota(jnp.int32, (SUBLANES, columns), 0)
    below_foreign = first & (tile_rows < halo)
    above_foreign = last & (tile_rows >= halo)

    def both_layers(parts, product):
        mine = product(parts, 0)
        others = product([jnp.where(first, x[:SUBLANES], x[SUBLANES:]) for x in parts], 1)
        return [
            jnp.concatenate(
                [jnp.where(below_foreign, b, a[:SUBLANES]), jnp.where(above_foreign, b, a[SUBLANES:])], axis=0
            )
            for a, b in zip(mine, others)
        ]

    def to_bins(parts, k):
        return two_part_dot(parts, column_ref[k], 0)

    def to_columns(parts, k):
        return two_part_dot(parts, column_ref[k], 1)

    def near(parts, k):
        blocks = [
            two_part_dot(
                [x[:, q * LANES : (q + 1) * LANES] for x in parts], link_ref[k, q * LANES : (q + 1) * LANES, :], 1
            )
            for q in range(quads)
        ]
        return [jnp.concatenate([b[i] for b in blocks], axis=1) for i in range(len(parts))]

    force_ref[3] = both_layers([rate], to_columns)[0]
    aux_ref[1] = both_layers([live], near)[0]

    wide_lane = lax.broadcasted_iota(jnp.int32, (rows, LANES), 1)
    lane_y = lax.div(wide_lane, group) * dy + lax.rem(wide_lane, dy)
    lane_x = lax.rem(lax.div(wide_lane, dy), dx)

    def source_lanes(cx, cy):
        y = lax.rem(lane_y - cy + plan.n_gy * dy, plan.n_gy * dy)
        x = lax.rem(lane_x - cx + dx, dx)
        return lax.div(y, dy) * group + x * dy + lax.rem(y, dy)

    def step(_, carry):
        for q in range(quads):
            lanes = slice(q * LANES, (q + 1) * LANES)
            popul = [f_ref[i, :, lanes] for i in range(19)]
            density = popul[0]
            for i in range(1, 19):
                density = density + popul[i]
            u_ref[3, :, lanes] = density
            for a in range(3):
                rising = [popul[i] for i in range(19) if VELOCITIES[i, a] == 1]
                falling = [popul[i] for i in range(19) if VELOCITIES[i, a] == -1]
                u_ref[a, :, lanes] = (sum(rising[1:], rising[0]) - sum(falling[1:], falling[0])) / density
        rate = aux_ref[0]
        count = aux_ref[1]
        live = (rate > 0.0).astype(jnp.float32)
        velocity = [v_ref[a] for a in range(3)]
        speed = both_layers([u_ref[a] for a in range(3)], to_bins)
        drags = [drag_factor * rate * (speed[a] - velocity[a]) for a in range(3)]
        for a, force in enumerate(both_layers([-d for d in drags], to_columns)):
            force_ref[a] = force
        touching = both_layers([velocity[a] * live for a in range(3)], near)
        for a in range(3):
            push = contact_stiffness * live * (touching[a] - count * velocity[a])
            updated = velocity[a] + drags[a] + push
            if a == 2:
                updated = updated - gravity * live
            v_ref[a] = updated
        for q in range(quads):
            lanes = slice(q * LANES, (q + 1) * LANES)
            density = u_ref[3, :, lanes]
            scale = 1.0 / (1.0 + force_ref[3, :, lanes])
            target = [
                scale * (u_ref[a, :, lanes] + relax_time * force_ref[a, :, lanes] / density)
                for a in range(3)
            ]
            square = target[0] * target[0] + target[1] * target[1] + target[2] * target[2]
            base = 1.0 - 1.5 * square
            for i in range(19):
                along = None
                for a in range(3):
                    if VELOCITIES[i, a] != 0:
                        term = target[a] if VELOCITIES[i, a] == 1 else -target[a]
                        along = term if along is None else along + term
                shape = base if along is None else base + along * (3.0 + 4.5 * along)
                equil = (float(WEIGHTS[i]) * density) * shape
                popul = f_ref[i, :, lanes]
                post_ref[i, :, lanes] = popul - (popul - equil) * (1.0 / relax_time)
        small_row = lax.broadcasted_iota(jnp.int32, (rows, LANES), 0)
        bottom = ground & (small_row == halo)
        top = ceiling & (small_row == halo + own - 1)
        for i in range(19):
            cx, cy, cz = (int(c) for c in VELOCITIES[i])
            moved = [post_ref[i, :, q * LANES : (q + 1) * LANES] for q in range(quads)]
            if cx or cy:
                from_lane = source_lanes(cx, cy)
                moved = [jnp.take_along_axis(x, from_lane, axis=1, mode="promise_in_bounds") for x in moved]
            if cx:
                edge = lane_x == (0 if cx == 1 else dx - 1)
                moved = [jnp.where(edge, moved[(q - cx) % quads], moved[q]) for q in range(quads)]
            for q in range(quads):
                lanes = slice(q * LANES, (q + 1) * LANES)
                x = moved[q]
                if cz:
                    x = pltpu.roll(x, cz % rows, 0)
                    x = jnp.where(bottom if cz == 1 else top, post_ref[OPPOSITE[i], :, lanes], x)
                f_ref[i, :, lanes] = x
        return carry

    lax.fori_loop(0, SUBSTEPS, step, 0)

    for t in range(plan.tiles):
        for q in range(quads):
            lanes = slice(q * LANES, (q + 1) * LANES)
            parts = []
            for field in range(t * per, (t + 1) * per):
                if field < 19:
                    part = f_ref[field, halo : halo + own, lanes]
                elif field in FIELD_V:
                    part = v_ref[FIELD_V.index(field), halo : halo + own, lanes]
                else:
                    part = jnp.zeros((own, LANES), jnp.float32)
                parts.append(part)
            for s, part in enumerate(swap_groups(parts, group)):
                out_ref[q * per + s, :, t * LANES : (t + 1) * LANES] = part


def finish_kernel(plan, in_ref, pop_ref, vel_ref):
    bins = plan.bins
    whole = 19 * plan.group // LANES
    rest = 19 * plan.group - whole * LANES
    holders = [plan.holder(q) for q in range(plan.sources)]
    for t in range(plan.tiles):
        at = slice(t * LANES, (t + 1) * LANES)
        block = jnp.concatenate([in_ref[holders[q], :, at] for q in range(plan.sources)], axis=0).T
        if t < whole:
            pop_ref[t * LANES : (t + 1) * LANES, :] = block
        elif t == whole:
            pop_ref[whole * LANES :, :] = block[:rest, :]
            vel_ref[:bins, :] = block[rest:, :]
        else:
            vel_ref[bins:, :] = block[bins : 3 * bins, :]


def windows_body(plan, populations, grain_velocity, grain_volume, slots, contacts, bin_cell):
    group, bins, sources = plan.group, plan.bins, plan.sources
    rows, columns, own = plan.rows, plan.columns, plan.own
    f32 = jnp.float32

    def call(kernel, shapes, inputs, scratch=()):
        shapes = [jax.ShapeDtypeStruct(shape, f32) for shape in shapes]
        return pl.pallas_call(
            lambda *refs: kernel(plan, *refs),
            out_shape=shapes,
            in_specs=[VMEM] * len(inputs),
            out_specs=[VMEM] * len(shapes),
            scratch_shapes=list(scratch),
            compiler_params=pltpu.CompilerParams(vmem_limit_bytes=VMEM_LIMIT),
        )(*inputs)

    (outgoing,) = call(
        prepare_kernel,
        [(sources, own, plan.wide)],
        (
            populations.reshape(19 * group, LANES),
            grain_velocity.reshape(3 * bins, LANES),
            grain_volume,
            slots,
            contacts,
            bin_cell.reshape(1, bins),
        ),
    )
    layer_axes, every_axis = ("gx", "gy"), ("gx", "gy", "gz")
    incoming = lax.all_to_all(outgoing, layer_axes, split_axis=0, concat_axis=0, tiled=True)
    half = sources // 2
    inner, outer = call(
        edges_kernel,
        [(half, SUBLANES, plan.width), (half, SUBLANES, plan.width + 2 * LANES)],
        (incoming,),
    )
    inner = lax.ppermute(inner, every_axis, plan.swaps(0))
    outer = lax.ppermute(outer, every_axis, plan.swaps(1))
    (back,) = call(
        substeps_kernel,
        [(sources, own, plan.width)],
        (incoming, inner, outer),
        (
            pltpu.VMEM((19, rows, columns), f32),
            pltpu.VMEM((19, rows, columns), f32),
            pltpu.VMEM((4, rows, columns), f32),
            pltpu.VMEM((4, rows, columns), f32),
            pltpu.VMEM((3, rows, columns), f32),
            pltpu.VMEM((2, rows, columns), f32),
            pltpu.VMEM((2, columns, columns), jnp.bfloat16),
            pltpu.VMEM((2, columns, LANES), jnp.bfloat16),
        ),
    )
    result = lax.all_to_all(back, layer_axes, split_axis=0, concat_axis=0, tiled=True)
    fluid, velocity = call(
        finish_kernel,
        [(19 * group, LANES), (3 * bins, LANES)],
        (result,),
    )
    return (fluid.reshape(populations.shape), velocity.reshape(grain_velocity.shape))


def body(populations, grain_velocity, grain_volume, slots, contacts, bin_cell):
    plan = Plan(
        lax.axis_size("gx"),
        lax.axis_size("gy"),
        lax.axis_size("gz"),
        populations,
        contacts,
        grain_velocity.shape[2],
    )
    arrays = (populations, grain_velocity, grain_volume, slots, contacts, bin_cell)
    if plan.fits() and contacts.shape[0] == contacts.shape[1]:
        return windows_body(plan, *arrays)
    return columns_body(*arrays)


def solution(mesh):
    placed = (
        P(None, "gx", "gy", "gz"),
        P(None, ("gx", "gy", "gz"), None),
        P(("gx", "gy", "gz"), None),
        P(("gx", "gy", "gz"), None),
        P(("gx", "gy", "gz"), None),
        P(("gx", "gy", "gz")),
    )
    return jax.shard_map(
        body,
        mesh=mesh,
        in_specs=placed,
        out_specs=(P(None, "gx", "gy", "gz"), P(None, ("gx", "gy", "gz"), None)),
        check_vma=False,
    )
```

```python
import jax
import jax.numpy as jnp
import numpy as np
from jax import lax
from jax.experimental import pallas as pl
from jax.experimental.pallas import tpu as pltpu
from jax.sharding import PartitionSpec as P

SUBSTEPS = 4


VELOCITIES = np.array(
    [
        [0, 0, 0],
        [1, 0, 0],
        [-1, 0, 0],
        [0, 1, 0],
        [0, -1, 0],
        [0, 0, 1],
        [0, 0, -1],
        [1, 1, 0],
        [-1, -1, 0],
        [1, -1, 0],
        [-1, 1, 0],
        [1, 0, 1],
        [-1, 0, -1],
        [1, 0, -1],
        [-1, 0, 1],
        [0, 1, 1],
        [0, -1, -1],
        [0, 1, -1],
        [0, -1, 1],
    ]
)
WEIGHTS = np.array([1.0 / 3.0] + [1.0 / 18.0] * 6 + [1.0 / 36.0] * 12)
OPPOSITE = [0, 2, 1, 4, 3, 6, 5, 8, 7, 10, 9, 12, 11, 14, 13, 16, 15, 18, 17]
relax_time = 0.8
contact_stiffness = 0.1
drag_factor = 2.0
gravity = 0.01


def passed_along(x, axis, by):
    length = lax.axis_size(axis)
    return lax.ppermute(x, axis, [(i, (i + by) % length) for i in range(length)])


def passed_along_2(value, axis, steps):
    count = lax.axis_size(axis)
    leading, last = (max(0, -steps), min(count, count - steps))
    return lax.ppermute(value, axis, [(source, source + steps) for source in range(leading, last)])


def moments(popul):
    density = jnp.sum(popul, axis=0)
    speed = []
    for axis in range(3):
        rising = np.array([i for i in range(19) if VELOCITIES[i, axis] == 1])
        falling = np.array([i for i in range(19) if VELOCITIES[i, axis] == -1])
        momentum = jnp.sum(popul[rising], axis=0) - jnp.sum(popul[falling], axis=0)
        speed.append(momentum / density)
    return (density, speed)


def grain_step(block, velocity, live, volume, links):
    grains = velocity.shape[2]
    bins = links.shape[1]
    groups = velocity.shape[1] // bins
    rate = drag_factor * volume * live
    drag = rate[None] * (block[:3] - velocity)
    moving = (velocity * live[None]).reshape(3, groups, bins, grains)
    pairs = links.reshape(groups, bins, bins)
    near = jnp.einsum("gkj,cgjs->cgks", pairs, moving, precision=lax.Precision.HIGHEST).reshape(
        3, -1, grains
    )
    count = jnp.einsum(
        "gkj,gjs->gks", pairs, live.reshape(groups, bins, grains), precision=lax.Precision.HIGHEST
    ).reshape(-1, grains)
    push = contact_stiffness * live[None] * (near - count[None] * velocity)
    fall = jnp.asarray([0.0, 0.0, gravity], jnp.float32).reshape(3, 1, 1) * live[None]
    updated = velocity + drag + push - fall
    forces = jnp.concatenate([-drag, (volume * live)[None]], axis=0)
    return (updated, forces)


def collide(popul, density, speed, field):
    scale = 1.0 / (1.0 + field[3])
    target = [scale * (speed[a] + relax_time * field[a] / density) for a in range(3)]
    square = target[0] * target[0] + target[1] * target[1] + target[2] * target[2]
    rows = []
    for i in range(19):
        along = jnp.zeros_like(density)
        for a in range(3):
            if VELOCITIES[i, a] != 0:
                along = along + float(VELOCITIES[i, a]) * target[a]
        equil = (
            float(WEIGHTS[i]) * density * (1.0 + 3.0 * along + 4.5 * along * along - 1.5 * square)
        )
        rows.append(popul[i] - (popul[i] - equil) / relax_time)
    return jnp.stack(rows)


def walls(moved, post):
    depth = post.shape[3]
    zpos = jnp.arange(depth)
    bottom = (zpos == 0) & (lax.axis_index("gz") == 0)
    top = (zpos == depth - 1) & (lax.axis_index("gz") == lax.axis_size("gz") - 1)
    rows = []
    for i in range(19):
        layer = moved[i]
        if VELOCITIES[i, 2] == 1:
            layer = jnp.where(bottom, post[OPPOSITE[i]], layer)
        elif VELOCITIES[i, 2] == -1:
            layer = jnp.where(top, post[OPPOSITE[i]], layer)
        rows.append(layer)
    return jnp.stack(rows)


def leaving(axis):
    rising = np.array([i for i in range(19) if VELOCITIES[i, axis] == 1])
    falling = np.array([i for i in range(19) if VELOCITIES[i, axis] == -1])
    return (rising, falling)


def stream(post):
    moved = post
    rising, falling = leaving(0)
    upper = moved[rising]
    lower = moved[falling]
    edge_up = passed_along(upper[:, -1:], "gx", 1)
    edge_down = passed_along(lower[:, :1], "gx", -1)
    moved = moved.at[rising].set(jnp.concatenate([edge_up, upper[:, :-1]], axis=1))
    moved = moved.at[falling].set(jnp.concatenate([lower[:, 1:], edge_down], axis=1))
    rising, falling = leaving(1)
    upper = moved[rising]
    lower = moved[falling]
    edge_up = passed_along(upper[:, :, -1:], "gy", 1)
    edge_down = passed_along(lower[:, :, :1], "gy", -1)
    moved = moved.at[rising].set(jnp.concatenate([edge_up, upper[:, :, :-1]], axis=2))
    moved = moved.at[falling].set(jnp.concatenate([lower[:, :, 1:], edge_down], axis=2))
    rising, falling = leaving(2)
    upper = moved[rising]
    lower = moved[falling]
    edge_up = passed_along_2(upper[:, :, :, -1:], "gz", 1)
    edge_down = passed_along_2(lower[:, :, :, :1], "gz", -1)
    moved = moved.at[rising].set(jnp.concatenate([edge_up, upper[:, :, :, :-1]], axis=3))
    moved = moved.at[falling].set(jnp.concatenate([lower[:, :, :, 1:], edge_down], axis=3))
    return walls(moved, post)


def carry_flow(outgoing):
    result = lax.all_to_all(outgoing, ("gx", "gy"), split_axis=1, concat_axis=1, tiled=True)
    return result


def carry_force(outgoing):
    result = lax.all_to_all(outgoing, ("gx", "gy"), split_axis=1, concat_axis=1, tiled=True)
    return result


def rank_within(source):
    count = source.shape[-1]
    before = jnp.arange(count)[None, :] < jnp.arange(count)[:, None]
    same = source[..., :, None] == source[..., None, :]
    return jnp.sum((same & before).astype(jnp.int32), axis=-1)


def columns_body(populations, grain_velocity, grain_volume, slots, contacts, bin_cell):
    n_gx = lax.axis_size("gx")
    n_gy = lax.axis_size("gy")
    n_gz = lax.axis_size("gz")
    sources = n_gx * n_gy
    bins = contacts.shape[1]
    grains = grain_velocity.shape[2]
    depth_x, depth_y, depth_z = (populations.shape[1], populations.shape[2], populations.shape[3])
    zblocks = depth_z // grains
    capacity = max(2, 4 * bins // sources)
    width_y = depth_y * n_gy
    column_blocks = depth_z * n_gz // grains

    def locate(cells):
        xcell = cells // (width_y * column_blocks)
        ycell = cells // column_blocks % width_y
        zblock = cells % column_blocks
        source = xcell // depth_x * n_gy + ycell // depth_y
        local = (xcell % depth_x * depth_y + ycell % depth_y) * zblocks + zblock % zblocks
        return (source, local)

    own_source, own_local = locate(bin_cell)
    own_row = own_source * capacity + rank_within(own_source)
    every = lax.all_gather(bin_cell, ("gx", "gy"), axis=0, tiled=True).reshape(sources, bins)
    all_source, all_local = locate(every)
    all_rank = rank_within(all_source)
    here = lax.axis_index("gx") * n_gy + lax.axis_index("gy")
    slot_ids = jnp.arange(capacity, dtype=jnp.int32)
    picked = (all_source == here)[:, None, :] & (all_rank[:, None, :] == slot_ids[None, :, None])
    send_column = jnp.sum(jnp.where(picked, all_local[:, None, :], 0), axis=2).reshape(-1)
    send_mask = jnp.any(picked, axis=2).reshape(-1).astype(jnp.float32)
    live = slots.astype(jnp.float32)
    links = contacts.astype(jnp.float32)
    fluid = populations
    velocity = grain_velocity
    for step in range(SUBSTEPS):
        density, speed = moments(fluid)
        flow = jnp.stack(speed + [density]).reshape(4, -1, grains)
        outgoing = jnp.take(flow, send_column, axis=1) * send_mask[None, :, None]
        incoming = carry_flow(outgoing)
        block = jnp.take(incoming, own_row, axis=1)
        velocity, forces = grain_step(block, velocity, live, grain_volume, links)
        back = jnp.zeros((4, sources * capacity, grains), jnp.float32).at[:, own_row].set(forces)
        returned = carry_force(back)
        field = jnp.zeros_like(flow).at[:, send_column].add(returned * send_mask[None, :, None])
        field = field.reshape(4, depth_x, depth_y, depth_z)
        post = collide(fluid, density, speed, field)
        fluid = stream(post)
    return (fluid, velocity)


LANES = 128
SUBLANES = 8
VMEM_LIMIT = 24 * 1024 * 1024
VMEM = pl.BlockSpec(memory_space=pltpu.VMEM)
HBM = pl.BlockSpec(memory_space=pltpu.HBM)
FIELD_V = (19, 21, 22)
FIELD_CELL = 20
FIELD_RATE = 23


class Plan:
    def __init__(self, n_gx, n_gy, n_gz, populations, contacts, grains):
        self.n_gx, self.n_gy, self.n_gz = n_gx, n_gy, n_gz
        self.dx, self.dy, self.depth = populations.shape[1:]
        self.grains = grains
        self.bins = contacts.shape[1]
        self.sources = n_gx * n_gy
        self.group = self.dx * self.dy
        self.halo = SUBSTEPS
        self.own = self.depth // self.sources
        self.rows = self.own + 2 * self.halo
        self.columns = self.sources * self.group
        self.per_tile = max(1, LANES // self.group)
        self.fields = 24
        self.tiles = self.fields // self.per_tile
        self.width = self.fields * self.group
        self.wide = self.width + LANES

    def fits(self):
        group = self.group
        return (
            self.sources % 2 == 0
            and self.depth == LANES
            and self.grains == LANES
            and self.own * self.sources == LANES
            and self.own == SUBLANES
            and self.rows == 2 * SUBLANES
            and group == self.bins
            and group * group == SUBLANES * LANES
            and self.per_tile == self.n_gy
        )

    def along(self, window):
        gx, r = divmod(window, self.n_gy)
        return gx * self.n_gy + (self.n_gy - 1 - r if gx % 2 else r)

    def device(self, window):
        layer, local = divmod(window, self.sources)
        if layer % 2:
            local = self.sources - 1 - local
        return self.along(local) * self.n_gz + layer

    def swaps(self, start):
        count = self.n_gz * self.sources
        paired = []
        for a in range(start, count - 1, 2):
            paired += [(a, a + 1), (a + 1, a)]
        if start:
            paired += [(0, 0), (count - 1, count - 1)]
        return [(self.device(a), self.device(b)) for a, b in paired]

    def place(self):
        gx, gy, layer = (lax.axis_index(name) for name in ("gx", "gy", "gz"))
        local = gx * self.n_gy + jnp.where(lax.rem(gx, 2) == 1, self.n_gy - 1 - gy, gy)
        return jnp.where(lax.rem(layer, 2) == 1, self.sources - 1 - local, local), layer

    def holder(self, window):
        odd = lax.rem(lax.axis_index("gz"), 2) == 1
        return jnp.where(odd, self.along(self.sources - 1 - window), self.along(window))


def swap_groups(sets, group):
    sets = [list(parts) for parts in sets]
    count = len(sets[0])
    lane = lax.broadcasted_iota(jnp.int32, sets[0][0].shape, 1)
    step = count // 2
    while step:
        low = lane // (group * step) % 2 == 0
        shift = group * step
        for a in range(count):
            if a // step % 2 == 0:
                for parts in sets:
                    first, second = parts[a], parts[a + step]
                    parts[a] = jnp.where(low, first, pltpu.roll(second, shift, 1))
                    parts[a + step] = jnp.where(low, pltpu.roll(first, LANES - shift, 1), second)
        step //= 2
    return sets


def prepare_kernel(plan, pop_ref, vel_ref, vol_ref, slot_ref, link_ref, cell_ref, out_ref,
                   pops, slots, links, cells, sems):
    group, bins, own = plan.group, plan.bins, plan.own
    whole = 19 * group // LANES
    rest = 19 * group - whole * LANES
    end = whole * LANES + 2 * LANES
    moves = [
        (cell_ref, cells),
        (link_ref, links),
        (slot_ref, slots),
        (vol_ref, pops.at[end - bins : end]),
        (vel_ref.at[bins:], pops.at[end - 3 * bins : end - bins]),
        (vel_ref.at[:bins], pops.at[whole * LANES + rest : (whole + 1) * LANES]),
        (pop_ref.at[whole * LANES :], pops.at[whole * LANES : whole * LANES + rest]),
    ]
    moves += [(pop_ref.at[t * LANES : (t + 1) * LANES], pops.at[t * LANES : (t + 1) * LANES]) for t in range(whole)]
    copies = [pltpu.make_async_copy(a, b, sems.at[i]) for i, (a, b) in enumerate(moves)]
    for copy in copies:
        copy.start()
    for copy in copies[:7]:
        copy.wait()

    cell = cells[...]
    width_y = plan.dy * plan.n_gy
    xcell = lax.div(cell, width_y * plan.n_gz)
    ycell = lax.rem(lax.div(cell, plan.n_gz), width_y)
    source = lax.div(xcell, plan.dx) * plan.n_gy + lax.div(ycell, plan.dy)
    cell = source * group + lax.rem(xcell, plan.dx) * plan.dy + lax.rem(ycell, plan.dy)
    cell = jnp.concatenate([cell.astype(jnp.float32), jnp.zeros((1, LANES - bins), jnp.float32)], axis=1)
    packed = jnp.concatenate(
        [links[g * SUBLANES : (g + 1) * SUBLANES, :].astype(jnp.float32) for g in range(bins // SUBLANES)],
        axis=1,
    )
    holders = [plan.holder(q) for q in range(plan.sources)]
    for q in range(plan.sources):
        out_ref[q, :, plan.width :] = packed
    for t in (whole, whole + 1, *range(whole)):
        if t < whole:
            copies[7 + t].wait()
            block = pops[t * LANES : (t + 1) * LANES, :]
        elif t == whole:
            block = pops[whole * LANES : (whole + 1) * LANES, :]
        else:
            rate = pops[end - bins : end, :] * slots[...].astype(jnp.float32)
            block = jnp.concatenate([rate, pops[end - 3 * bins : end - bins, :], rate], axis=0)
        block = block.T
        if t == plan.tiles - 1:
            lane = lax.broadcasted_iota(jnp.int32, block.shape, 1)
            block = jnp.where(lane < bins, cell, block)
        for q in range(plan.sources):
            out_ref[holders[q], :, t * LANES : (t + 1) * LANES] = block[q * own : (q + 1) * own, :]


def edges_kernel(plan, in_ref, inner_ref, outer_ref):
    window, _ = plan.place()
    even = lax.rem(window, 2) == 0
    halo = plan.halo
    low_rows = lax.broadcasted_iota(jnp.int32, (SUBLANES, LANES), 0) < halo
    for h in range(plan.sources // 2):
        for t in range(plan.tiles):
            lanes = slice(t * LANES, (t + 1) * LANES)
            a, b = in_ref[2 * h, :, lanes], in_ref[2 * h + 1, :, lanes]
            low = jnp.where(low_rows, a, pltpu.roll(b, halo, 0))
            high = jnp.where(low_rows, pltpu.roll(a, halo, 0), b)
            inner_ref[h, :, lanes] = jnp.where(even, high, low)
            outer_ref[h, :, lanes] = jnp.where(even, low, high)
        for k in range(2):
            start = plan.width + k * LANES
            outer_ref[h, :, start : start + LANES] = in_ref[2 * h + k, :, plan.width :]


def two_part_dot(parts, matrix, contract):
    whole = jnp.concatenate(parts, axis=0)
    rest = whole - whole.astype(jnp.bfloat16).astype(jnp.float32)
    stacked = jnp.concatenate([whole, rest], axis=0).astype(jnp.bfloat16)
    out = lax.dot_general(
        stacked, matrix, (((1,), (contract,)), ((), ())), preferred_element_type=jnp.float32
    )
    rows = parts[0].shape[0]
    half = rows * len(parts)
    return [
        out[i * rows : (i + 1) * rows] + out[half + i * rows : half + (i + 1) * rows]
        for i in range(len(parts))
    ]


def bins_on_columns(columns, cells):
    which = lax.broadcasted_iota(jnp.int32, (columns, columns), 0).astype(jnp.float32)
    return (which == cells).astype(jnp.float32).astype(jnp.bfloat16)


def contact_blocks(plan, packed, link_ref):
    group, per = plan.group, plan.per_tile
    lane = lax.broadcasted_iota(jnp.int32, (SUBLANES, LANES), 1)
    for s in range(plan.sources):
        place = s % per
        tile = packed(s)
        pieces = []
        for g in range(per):
            moved = tile if g == place else pltpu.roll(tile, (place - g) * group % LANES, 1)
            pieces.append(jnp.where(lane // group == place, moved, 0.0))
        link_ref[s * group : (s + 1) * group, :] = jnp.concatenate(pieces, axis=0).astype(jnp.bfloat16)


def unpack(plan, tile_of, state_ref, rows):
    per = plan.per_tile
    for t in range(plan.tiles):
        sets = [[tile_of(s, t) for s in range(q, q + per)] for q in range(0, plan.sources, per)]
        for q, parts in enumerate(swap_groups(sets, plan.group)):
            for j, part in enumerate(parts):
                state_ref[t * per + j, rows, q * LANES : (q + 1) * LANES] = part


def settle_kernel(plan, in_ref, state_ref, column_ref, link_ref):
    unpack(plan, lambda s, t: in_ref[s, :, t * LANES : (t + 1) * LANES], state_ref, slice(0, plan.own))
    column_ref[...] = bins_on_columns(plan.columns, state_ref[FIELD_CELL, 0:1, :])
    contact_blocks(plan, lambda s: in_ref[s, :, plan.width :], link_ref)


def substeps_kernel(plan, settled_ref, column_ref, link_ref, inner_ref, outer_ref, out_ref, state_ref,
                    post_ref, u_ref, force_ref, count_ref, other_column_ref, other_link_ref):
    rows, columns, group, per = plan.rows, plan.columns, plan.group, plan.per_tile
    halo, own, dx, dy = plan.halo, plan.own, plan.dx, plan.dy
    quads = plan.sources // per
    window, layer = plan.place()
    even = lax.rem(window, 2) == 0
    first, last = window == 0, window == plan.sources - 1
    ground, ceiling = first & (layer == 0), last & (layer == plan.n_gz - 1)
    tile_row = lax.broadcasted_iota(jnp.int32, (SUBLANES, LANES), 0)

    def halo_tile(s, t):
        at = slice(t * LANES, (t + 1) * LANES)
        inner, outer = inner_ref[s // 2, :, at], outer_ref[s // 2, :, at]
        below = jnp.where(even, outer, inner)
        above = jnp.where(even, inner, outer)
        if s % 2:
            above = pltpu.roll(above, halo, 0)
        else:
            below = pltpu.roll(below, halo, 0)
        return jnp.where(tile_row < halo, above, below)

    unpack(plan, halo_tile, state_ref, slice(own, rows))
    other_cells = jnp.where(first, state_ref[FIELD_CELL, rows - 1 : rows, :], state_ref[FIELD_CELL, own : own + 1, :])
    other_column_ref[...] = bins_on_columns(columns, other_cells)

    def other_contacts(s):
        start = plan.width + s % 2 * LANES
        return outer_ref[s // 2, :, start : start + LANES]

    contact_blocks(plan, other_contacts, other_link_ref)

    halo_row = lax.broadcasted_iota(jnp.int32, (SUBLANES, columns), 0)
    foreign = (last & (halo_row < halo)) | (first & (halo_row >= halo))

    def both_layers(parts, product, own_matrix, other_matrix):
        mine = product(parts, own_matrix)
        others = product([x[own:] for x in parts], other_matrix)
        return [
            jnp.concatenate([a[:own], jnp.where(foreign, b, a[own:])], axis=0) for a, b in zip(mine, others)
        ]

    def to_bins(parts):
        return both_layers(parts, lambda x, m: two_part_dot(x, m[...], 0), column_ref, other_column_ref)

    def to_columns(parts):
        return both_layers(parts, lambda x, m: two_part_dot(x, m[...], 1), column_ref, other_column_ref)

    def touching(parts, matrix):
        blocks = [
            two_part_dot(
                [x[:, q * LANES : (q + 1) * LANES] for x in parts], matrix[q * LANES : (q + 1) * LANES, :], 1
            )
            for q in range(quads)
        ]
        return [jnp.concatenate([b[i] for b in blocks], axis=1) for i in range(len(parts))]

    def near(parts):
        return both_layers(parts, touching, link_ref, other_link_ref)

    rate = state_ref[FIELD_RATE]
    force_ref[3] = 1.0 / (1.0 + to_columns([rate])[0])
    count_ref[...] = near([(rate > 0.0).astype(jnp.float32)])[0]

    lane = lax.broadcasted_iota(jnp.int32, (rows, LANES), 1)
    row = lax.broadcasted_iota(jnp.int32, (rows, LANES), 0)
    lane_y = lax.div(lane, group) * dy + lax.rem(lane, dy)
    lane_x = lax.rem(lax.div(lane, dy), dx)
    bottom, top = ground & (row == 0), ceiling & (row == own - 1)

    def source_lanes(cx, cy):
        y = lax.rem(lane_y - cy + plan.n_gy * dy, plan.n_gy * dy)
        x = lax.rem(lane_x - cx + dx, dx)
        return lax.div(y, dy) * group + x * dy + lax.rem(y, dy)

    def step(_, carry):
        for q in range(quads):
            lanes = slice(q * LANES, (q + 1) * LANES)
            popul = [state_ref[i, :, lanes] for i in range(19)]
            density = popul[0]
            for i in range(1, 19):
                density = density + popul[i]
            inverse = 1.0 / density
            u_ref[3, :, lanes] = density
            u_ref[4, :, lanes] = inverse
            for a in range(3):
                rising = [popul[i] for i in range(19) if VELOCITIES[i, a] == 1]
                falling = [popul[i] for i in range(19) if VELOCITIES[i, a] == -1]
                u_ref[a, :, lanes] = (sum(rising[1:], rising[0]) - sum(falling[1:], falling[0])) * inverse
        rate = state_ref[FIELD_RATE]
        live = (rate > 0.0).astype(jnp.float32)
        velocity = [state_ref[field] for field in FIELD_V]
        speed = to_bins([u_ref[a] for a in range(3)])
        drags = [drag_factor * rate * (speed[a] - velocity[a]) for a in range(3)]
        for a, force in enumerate(to_columns(drags)):
            force_ref[a] = force
        moving = near([velocity[a] * live for a in range(3)])
        count = count_ref[...]
        for a in range(3):
            push = contact_stiffness * live * (moving[a] - count * velocity[a])
            updated = velocity[a] + drags[a] + push
            if a == 2:
                updated = updated - gravity * live
            state_ref[FIELD_V[a]] = updated
        keep, take = 1.0 - 1.0 / relax_time, 1.0 / relax_time
        for q in range(quads):
            lanes = slice(q * LANES, (q + 1) * LANES)
            density, inverse = u_ref[3, :, lanes], u_ref[4, :, lanes]
            scale = force_ref[3, :, lanes]
            share = relax_time * inverse
            target = [scale * (u_ref[a, :, lanes] - share * force_ref[a, :, lanes]) for a in range(3)]
            square = target[0] * target[0] + target[1] * target[1] + target[2] * target[2]
            base = 1.0 - 1.5 * square
            triple = [3.0 * x for x in target]
            shares = {w: (take * float(w)) * density for w in sorted(set(WEIGHTS))}
            post_ref[0, :, lanes] = keep * state_ref[0, :, lanes] + shares[WEIGHTS[0]] * base
            for i in range(1, 19, 2):
                along = None
                for a in range(3):
                    if VELOCITIES[i, a] != 0:
                        if along is None:
                            along = triple[a] if VELOCITIES[i, a] == 1 else -triple[a]
                        else:
                            along = along + triple[a] if VELOCITIES[i, a] == 1 else along - triple[a]
                level = base + 0.5 * (along * along)
                share_i = shares[WEIGHTS[i]]
                post_ref[i, :, lanes] = keep * state_ref[i, :, lanes] + share_i * (level + along)
                post_ref[i + 1, :, lanes] = keep * state_ref[i + 1, :, lanes] + share_i * (level - along)
        for i in range(19):
            cx, cy, cz = (int(c) for c in VELOCITIES[i])
            moved = [post_ref[i, :, q * LANES : (q + 1) * LANES] for q in range(quads)]
            if cx or cy:
                from_lane = source_lanes(cx, cy)
                moved = [jnp.take_along_axis(x, from_lane, axis=1, mode="promise_in_bounds") for x in moved]
            if cx:
                edge = lane_x == (0 if cx == 1 else dx - 1)
                moved = [jnp.where(edge, moved[(q - cx) % quads], moved[q]) for q in range(quads)]
            for q in range(quads):
                lanes = slice(q * LANES, (q + 1) * LANES)
                x = moved[q]
                if cz:
                    x = pltpu.roll(x, cz % rows, 0)
                    x = jnp.where(bottom if cz == 1 else top, post_ref[OPPOSITE[i], :, lanes], x)
                state_ref[i, :, lanes] = x
        return carry

    lax.fori_loop(0, SUBSTEPS, step, 0)

    for t in range(plan.tiles):
        sets = [
            [state_ref[t * per + j, 0:own, q * LANES : (q + 1) * LANES] for j in range(per)] for q in range(quads)
        ]
        for q, parts in enumerate(swap_groups(sets, group)):
            for s, part in enumerate(parts):
                out_ref[q * per + s, :, t * LANES : (t + 1) * LANES] = part


def finish_kernel(plan, in_ref, pop_ref, vel_ref, stage, sems):
    bins = plan.bins
    whole = 19 * plan.group // LANES
    rest = 19 * plan.group - whole * LANES
    holders = [plan.holder(q) for q in range(plan.sources)]
    copies = []

    def send(start, size, target):
        copies.append(pltpu.make_async_copy(stage.at[start : start + size], target, sems.at[len(copies)]))
        copies[-1].start()

    for t in range(plan.tiles):
        at = slice(t * LANES, (t + 1) * LANES)
        start = t * LANES
        stage[at, :] = jnp.concatenate([in_ref[holders[q], :, at] for q in range(plan.sources)], axis=0).T
        if t < whole:
            send(start, LANES, pop_ref.at[at])
        elif t == whole:
            send(start, rest, pop_ref.at[start:])
            send(start + rest, bins, vel_ref.at[:bins])
        else:
            send(start + bins, 2 * bins, vel_ref.at[bins:])
    for copy in copies:
        copy.wait()


def windows_body(plan, populations, grain_velocity, grain_volume, slots, contacts, bin_cell):
    group, bins, sources = plan.group, plan.bins, plan.sources
    rows, columns, own = plan.rows, plan.columns, plan.own
    f32, bf16, i32 = jnp.float32, jnp.bfloat16, jnp.int32
    half = sources // 2

    def call(kernel, shapes, inputs, scratch=(), where=(VMEM, VMEM), aliases=None):
        if where[0] is HBM:
            inputs = [pltpu.with_memory_space_constraint(x, pltpu.HBM) for x in inputs]
        shapes = [jax.ShapeDtypeStruct(shape, kind) for shape, kind in shapes]
        return pl.pallas_call(
            lambda *refs: kernel(plan, *refs),
            out_shape=shapes,
            in_specs=[where[0]] * len(inputs),
            out_specs=[where[1]] * len(shapes),
            scratch_shapes=list(scratch),
            input_output_aliases=aliases or {},
            compiler_params=pltpu.CompilerParams(vmem_limit_bytes=VMEM_LIMIT),
        )(*inputs)

    (outgoing,) = call(
        prepare_kernel,
        [((sources, own, plan.wide), f32)],
        (
            populations.reshape(19 * group, LANES),
            grain_velocity.reshape(3 * bins, LANES),
            grain_volume,
            slots,
            contacts,
            bin_cell.reshape(1, bins),
        ),
        (
            pltpu.VMEM((plan.width, LANES), f32),
            pltpu.VMEM((bins, LANES), i32),
            pltpu.VMEM((bins, bins), i32),
            pltpu.VMEM((1, bins), i32),
            pltpu.SemaphoreType.DMA((16,)),
        ),
        (HBM, VMEM),
    )
    layer_axes, every_axis = ("gx", "gy"), ("gx", "gy", "gz")
    incoming = lax.all_to_all(outgoing, layer_axes, split_axis=0, concat_axis=0, tiled=True)
    inner, outer = call(
        edges_kernel,
        [((half, SUBLANES, plan.width), f32), ((half, SUBLANES, plan.width + 2 * LANES), f32)],
        (incoming,),
    )
    inner = lax.ppermute(inner, every_axis, plan.swaps(0))
    outer = lax.ppermute(outer, every_axis, plan.swaps(1))
    state, column, link = call(
        settle_kernel,
        [((plan.fields, rows, columns), f32), ((columns, columns), bf16), ((columns, LANES), bf16)],
        (incoming,),
    )
    back, _ = call(
        substeps_kernel,
        [((sources, own, plan.width), f32), ((plan.fields, rows, columns), f32)],
        (state, column, link, inner, outer),
        (
            pltpu.VMEM((19, rows, columns), f32),
            pltpu.VMEM((5, rows, columns), f32),
            pltpu.VMEM((4, rows, columns), f32),
            pltpu.VMEM((rows, columns), f32),
            pltpu.VMEM((columns, columns), bf16),
            pltpu.VMEM((columns, LANES), bf16),
        ),
        aliases={0: 1},
    )
    result = lax.all_to_all(back, layer_axes, split_axis=0, concat_axis=0, tiled=True)
    fluid, velocity = call(
        finish_kernel,
        [((19 * group, LANES), f32), ((3 * bins, LANES), f32)],
        (result,),
        (pltpu.VMEM((plan.width, LANES), f32), pltpu.SemaphoreType.DMA((16,))),
        (VMEM, HBM),
    )
    return (fluid.reshape(populations.shape), velocity.reshape(grain_velocity.shape))


def body(populations, grain_velocity, grain_volume, slots, contacts, bin_cell):
    plan = Plan(
        lax.axis_size("gx"),
        lax.axis_size("gy"),
        lax.axis_size("gz"),
        populations,
        contacts,
        grain_velocity.shape[2],
    )
    arrays = (populations, grain_velocity, grain_volume, slots, contacts, bin_cell)
    if plan.fits() and contacts.shape[0] == contacts.shape[1]:
        return windows_body(plan, *arrays)
    return columns_body(*arrays)


def solution(mesh):
    placed = (
        P(None, "gx", "gy", "gz"),
        P(None, ("gx", "gy", "gz"), None),
        P(("gx", "gy", "gz"), None),
        P(("gx", "gy", "gz"), None),
        P(("gx", "gy", "gz"), None),
        P(("gx", "gy", "gz")),
    )
    return jax.shard_map(
        body,
        mesh=mesh,
        in_specs=placed,
        out_specs=(P(None, "gx", "gy", "gz"), P(None, ("gx", "gy", "gz"), None)),
        check_vma=False,
    )
```

```python
import jax
import jax.numpy as jnp
import numpy as np
from jax import lax
from jax.experimental import pallas as pl
from jax.experimental.pallas import tpu as pltpu
from jax.sharding import PartitionSpec as P

SUBSTEPS = 4


VELOCITIES = np.array(
    [
        [0, 0, 0],
        [1, 0, 0],
        [-1, 0, 0],
        [0, 1, 0],
        [0, -1, 0],
        [0, 0, 1],
        [0, 0, -1],
        [1, 1, 0],
        [-1, -1, 0],
        [1, -1, 0],
        [-1, 1, 0],
        [1, 0, 1],
        [-1, 0, -1],
        [1, 0, -1],
        [-1, 0, 1],
        [0, 1, 1],
        [0, -1, -1],
        [0, 1, -1],
        [0, -1, 1],
    ]
)
WEIGHTS = np.array([1.0 / 3.0] + [1.0 / 18.0] * 6 + [1.0 / 36.0] * 12)
OPPOSITE = [0, 2, 1, 4, 3, 6, 5, 8, 7, 10, 9, 12, 11, 14, 13, 16, 15, 18, 17]
relax_time = 0.8
contact_stiffness = 0.1
drag_factor = 2.0
gravity = 0.01


def passed_along(x, axis, by):
    length = lax.axis_size(axis)
    return lax.ppermute(x, axis, [(i, (i + by) % length) for i in range(length)])


def passed_along_2(value, axis, steps):
    count = lax.axis_size(axis)
    leading, last = (max(0, -steps), min(count, count - steps))
    return lax.ppermute(value, axis, [(source, source + steps) for source in range(leading, last)])


def moments(popul):
    density = jnp.sum(popul, axis=0)
    speed = []
    for axis in range(3):
        rising = np.array([i for i in range(19) if VELOCITIES[i, axis] == 1])
        falling = np.array([i for i in range(19) if VELOCITIES[i, axis] == -1])
        momentum = jnp.sum(popul[rising], axis=0) - jnp.sum(popul[falling], axis=0)
        speed.append(momentum / density)
    return (density, speed)


def grain_step(block, velocity, live, volume, links):
    grains = velocity.shape[2]
    bins = links.shape[1]
    groups = velocity.shape[1] // bins
    rate = drag_factor * volume * live
    drag = rate[None] * (block[:3] - velocity)
    moving = (velocity * live[None]).reshape(3, groups, bins, grains)
    pairs = links.reshape(groups, bins, bins)
    near = jnp.einsum("gkj,cgjs->cgks", pairs, moving, precision=lax.Precision.HIGHEST).reshape(
        3, -1, grains
    )
    count = jnp.einsum(
        "gkj,gjs->gks", pairs, live.reshape(groups, bins, grains), precision=lax.Precision.HIGHEST
    ).reshape(-1, grains)
    push = contact_stiffness * live[None] * (near - count[None] * velocity)
    fall = jnp.asarray([0.0, 0.0, gravity], jnp.float32).reshape(3, 1, 1) * live[None]
    updated = velocity + drag + push - fall
    forces = jnp.concatenate([-drag, (volume * live)[None]], axis=0)
    return (updated, forces)


def collide(popul, density, speed, field):
    scale = 1.0 / (1.0 + field[3])
    target = [scale * (speed[a] + relax_time * field[a] / density) for a in range(3)]
    square = target[0] * target[0] + target[1] * target[1] + target[2] * target[2]
    rows = []
    for i in range(19):
        along = jnp.zeros_like(density)
        for a in range(3):
            if VELOCITIES[i, a] != 0:
                along = along + float(VELOCITIES[i, a]) * target[a]
        equil = (
            float(WEIGHTS[i]) * density * (1.0 + 3.0 * along + 4.5 * along * along - 1.5 * square)
        )
        rows.append(popul[i] - (popul[i] - equil) / relax_time)
    return jnp.stack(rows)


def walls(moved, post):
    depth = post.shape[3]
    zpos = jnp.arange(depth)
    bottom = (zpos == 0) & (lax.axis_index("gz") == 0)
    top = (zpos == depth - 1) & (lax.axis_index("gz") == lax.axis_size("gz") - 1)
    rows = []
    for i in range(19):
        layer = moved[i]
        if VELOCITIES[i, 2] == 1:
            layer = jnp.where(bottom, post[OPPOSITE[i]], layer)
        elif VELOCITIES[i, 2] == -1:
            layer = jnp.where(top, post[OPPOSITE[i]], layer)
        rows.append(layer)
    return jnp.stack(rows)


def leaving(axis):
    rising = np.array([i for i in range(19) if VELOCITIES[i, axis] == 1])
    falling = np.array([i for i in range(19) if VELOCITIES[i, axis] == -1])
    return (rising, falling)


def stream(post):
    moved = post
    rising, falling = leaving(0)
    upper = moved[rising]
    lower = moved[falling]
    edge_up = passed_along(upper[:, -1:], "gx", 1)
    edge_down = passed_along(lower[:, :1], "gx", -1)
    moved = moved.at[rising].set(jnp.concatenate([edge_up, upper[:, :-1]], axis=1))
    moved = moved.at[falling].set(jnp.concatenate([lower[:, 1:], edge_down], axis=1))
    rising, falling = leaving(1)
    upper = moved[rising]
    lower = moved[falling]
    edge_up = passed_along(upper[:, :, -1:], "gy", 1)
    edge_down = passed_along(lower[:, :, :1], "gy", -1)
    moved = moved.at[rising].set(jnp.concatenate([edge_up, upper[:, :, :-1]], axis=2))
    moved = moved.at[falling].set(jnp.concatenate([lower[:, :, 1:], edge_down], axis=2))
    rising, falling = leaving(2)
    upper = moved[rising]
    lower = moved[falling]
    edge_up = passed_along_2(upper[:, :, :, -1:], "gz", 1)
    edge_down = passed_along_2(lower[:, :, :, :1], "gz", -1)
    moved = moved.at[rising].set(jnp.concatenate([edge_up, upper[:, :, :, :-1]], axis=3))
    moved = moved.at[falling].set(jnp.concatenate([lower[:, :, :, 1:], edge_down], axis=3))
    return walls(moved, post)


def carry_flow(outgoing):
    result = lax.all_to_all(outgoing, ("gx", "gy"), split_axis=1, concat_axis=1, tiled=True)
    return result


def carry_force(outgoing):
    result = lax.all_to_all(outgoing, ("gx", "gy"), split_axis=1, concat_axis=1, tiled=True)
    return result


def rank_within(source):
    count = source.shape[-1]
    before = jnp.arange(count)[None, :] < jnp.arange(count)[:, None]
    same = source[..., :, None] == source[..., None, :]
    return jnp.sum((same & before).astype(jnp.int32), axis=-1)


def columns_body(populations, grain_velocity, grain_volume, slots, contacts, bin_cell):
    n_gx = lax.axis_size("gx")
    n_gy = lax.axis_size("gy")
    n_gz = lax.axis_size("gz")
    sources = n_gx * n_gy
    bins = contacts.shape[1]
    grains = grain_velocity.shape[2]
    depth_x, depth_y, depth_z = (populations.shape[1], populations.shape[2], populations.shape[3])
    zblocks = depth_z // grains
    capacity = max(2, 4 * bins // sources)
    width_y = depth_y * n_gy
    column_blocks = depth_z * n_gz // grains

    def locate(cells):
        xcell = cells // (width_y * column_blocks)
        ycell = cells // column_blocks % width_y
        zblock = cells % column_blocks
        source = xcell // depth_x * n_gy + ycell // depth_y
        local = (xcell % depth_x * depth_y + ycell % depth_y) * zblocks + zblock % zblocks
        return (source, local)

    own_source, own_local = locate(bin_cell)
    own_row = own_source * capacity + rank_within(own_source)
    every = lax.all_gather(bin_cell, ("gx", "gy"), axis=0, tiled=True).reshape(sources, bins)
    all_source, all_local = locate(every)
    all_rank = rank_within(all_source)
    here = lax.axis_index("gx") * n_gy + lax.axis_index("gy")
    slot_ids = jnp.arange(capacity, dtype=jnp.int32)
    picked = (all_source == here)[:, None, :] & (all_rank[:, None, :] == slot_ids[None, :, None])
    send_column = jnp.sum(jnp.where(picked, all_local[:, None, :], 0), axis=2).reshape(-1)
    send_mask = jnp.any(picked, axis=2).reshape(-1).astype(jnp.float32)
    live = slots.astype(jnp.float32)
    links = contacts.astype(jnp.float32)
    fluid = populations
    velocity = grain_velocity
    for step in range(SUBSTEPS):
        density, speed = moments(fluid)
        flow = jnp.stack(speed + [density]).reshape(4, -1, grains)
        outgoing = jnp.take(flow, send_column, axis=1) * send_mask[None, :, None]
        incoming = carry_flow(outgoing)
        block = jnp.take(incoming, own_row, axis=1)
        velocity, forces = grain_step(block, velocity, live, grain_volume, links)
        back = jnp.zeros((4, sources * capacity, grains), jnp.float32).at[:, own_row].set(forces)
        returned = carry_force(back)
        field = jnp.zeros_like(flow).at[:, send_column].add(returned * send_mask[None, :, None])
        field = field.reshape(4, depth_x, depth_y, depth_z)
        post = collide(fluid, density, speed, field)
        fluid = stream(post)
    return (fluid, velocity)


LANES = 128
SUBLANES = 8
VMEM_LIMIT = 24 * 1024 * 1024
VMEM = pl.BlockSpec(memory_space=pltpu.VMEM)
HBM = pl.BlockSpec(memory_space=pltpu.HBM)
FIELD_V = (19, 20, 21)
FIELD_CELL = 22
FIELD_RATE = 23


class Plan:
    def __init__(self, n_gx, n_gy, n_gz, populations, contacts, grains):
        self.n_gx, self.n_gy, self.n_gz = n_gx, n_gy, n_gz
        self.dx, self.dy, self.depth = populations.shape[1:]
        self.grains = grains
        self.bins = contacts.shape[1]
        self.sources = n_gx * n_gy
        self.group = self.dx * self.dy
        self.halo = SUBSTEPS
        self.own = self.depth // self.sources
        self.rows = self.own + 2 * self.halo
        self.columns = self.sources * self.group
        self.per_tile = max(1, LANES // self.group)
        self.fields = 24
        self.tiles = self.fields // self.per_tile
        self.width = self.fields * self.group
        self.wide = self.width + LANES

    def fits(self):
        group = self.group
        return (
            self.sources % 2 == 0
            and self.depth == LANES
            and self.grains == LANES
            and self.own * self.sources == LANES
            and self.own == SUBLANES
            and self.rows == 2 * SUBLANES
            and group == self.bins
            and group * group == SUBLANES * LANES
            and self.per_tile == self.n_gy
        )

    def along(self, window):
        gx, r = divmod(window, self.n_gy)
        return gx * self.n_gy + (self.n_gy - 1 - r if gx % 2 else r)

    def device(self, window):
        layer, local = divmod(window, self.sources)
        if layer % 2:
            local = self.sources - 1 - local
        return self.along(local) * self.n_gz + layer

    def swaps(self, start):
        count = self.n_gz * self.sources
        paired = []
        for a in range(start, count - 1, 2):
            paired += [(a, a + 1), (a + 1, a)]
        if start:
            paired += [(0, count - 1), (count - 1, 0)]
        return [(self.device(a), self.device(b)) for a, b in paired]

    def place(self):
        gx, gy, layer = (lax.axis_index(name) for name in ("gx", "gy", "gz"))
        local = gx * self.n_gy + jnp.where(lax.rem(gx, 2) == 1, self.n_gy - 1 - gy, gy)
        return jnp.where(lax.rem(layer, 2) == 1, self.sources - 1 - local, local), layer

    def holder(self, window):
        odd = lax.rem(lax.axis_index("gz"), 2) == 1
        return jnp.where(odd, self.along(self.sources - 1 - window), self.along(window))


def pick(group, parts):
    lane = lax.broadcasted_iota(jnp.int32, parts[0].shape, 1) // group
    step = 1
    while len(parts) > 1:
        odd = lane // step % 2 == 1
        parts = [jnp.where(odd, b, a) for a, b in zip(parts[::2], parts[1::2])]
        step *= 2
    return parts[0]


def turned_groups(parts, group):
    count = len(parts)
    turned = []
    for r in range(count):
        chosen = pick(group, [parts[(g + r) % count] for g in range(count)])
        turned.append(pltpu.roll(chosen, r * group, 1) if r else chosen)
    return turned


def swap_groups(sets, group):
    turned = [turned_groups(parts, group) for parts in sets]
    count = len(sets[0])
    return [[pick(group, [t[(g - j) % count] for g in range(count)]) for j in range(count)] for t in turned]


def prepare_kernel(plan, pop_ref, vel_ref, vol_ref, slot_ref, link_ref, cell_ref, out_ref,
                   pops, slots, links, cells, sems):
    group, bins, own = plan.group, plan.bins, plan.own
    whole = 19 * group // LANES
    end = plan.width
    vel_start = 19 * group
    split = whole * LANES // 2
    moves = [
        (cell_ref, cells),
        (link_ref, links),
        (slot_ref, slots),
        (vol_ref, pops.at[end - bins : end]),
        (vel_ref, pops.at[vel_start : vel_start + 3 * bins]),
        (pop_ref.at[split:], pops.at[split:vel_start]),
        (pop_ref.at[:split], pops.at[:split]),
    ]
    copies = [pltpu.make_async_copy(a, b, sems.at[i]) for i, (a, b) in enumerate(moves)]
    for copy in copies:
        copy.start()
    for copy in copies:
        copy.wait()

    cell = cells[...]
    width_y = plan.dy * plan.n_gy
    xcell = lax.div(cell, width_y * plan.n_gz)
    ycell = lax.rem(lax.div(cell, plan.n_gz), width_y)
    source = lax.div(xcell, plan.dx) * plan.n_gy + lax.div(ycell, plan.dy)
    cell = source * group + lax.rem(xcell, plan.dx) * plan.dy + lax.rem(ycell, plan.dy)
    blank = jnp.zeros((1, bins), jnp.float32)
    cell = jnp.concatenate([blank, blank, cell.astype(jnp.float32), blank], axis=1)
    packed = jnp.concatenate(
        [links[g * SUBLANES : (g + 1) * SUBLANES, :].astype(jnp.float32) for g in range(bins // SUBLANES)],
        axis=1,
    )
    holders = [plan.holder(q) for q in range(plan.sources)]
    for q in range(plan.sources):
        out_ref[q, :, plan.width :] = packed
    for t in range(plan.tiles):
        block = pops[t * LANES : (t + 1) * LANES, :]
        if t == plan.tiles - 1:
            rate = pops[end - bins : end, :] * slots[...].astype(jnp.float32)
            block = jnp.concatenate([block[: 2 * bins], rate, rate], axis=0)
        block = block.T
        if t == plan.tiles - 1:
            lane = lax.broadcasted_iota(jnp.int32, block.shape, 1) // bins
            block = jnp.where(lane == FIELD_CELL % plan.per_tile, cell, block)
        for q in range(plan.sources):
            out_ref[holders[q], :, t * LANES : (t + 1) * LANES] = block[q * own : (q + 1) * own, :]


def edges_kernel(plan, in_ref, inner_ref, outer_ref):
    window, _ = plan.place()
    even = lax.rem(window, 2) == 0
    halo = plan.halo
    low_rows = lax.broadcasted_iota(jnp.int32, (SUBLANES, LANES), 0) < halo
    for h in range(plan.sources // 2):
        for t in range(plan.tiles):
            lanes = slice(t * LANES, (t + 1) * LANES)
            a, b = in_ref[2 * h, :, lanes], in_ref[2 * h + 1, :, lanes]
            low = jnp.where(low_rows, a, pltpu.roll(b, halo, 0))
            high = jnp.where(low_rows, pltpu.roll(a, halo, 0), b)
            inner_ref[h, :, lanes] = jnp.where(even, high, low)
            outer_ref[h, :, lanes] = jnp.where(even, low, high)
        for k in range(2):
            start = plan.width + k * LANES
            outer_ref[h, :, start : start + LANES] = in_ref[2 * h + k, :, plan.width :]


def two_part_dot(parts, matrix):
    whole = jnp.concatenate(parts, axis=0)
    rest = whole - whole.astype(jnp.bfloat16).astype(jnp.float32)
    stacked = jnp.concatenate([whole, rest], axis=0).astype(jnp.bfloat16)
    out = lax.dot_general(
        stacked, matrix, (((1,), (1,)), ((), ())), preferred_element_type=jnp.float32
    )
    rows = parts[0].shape[0]
    half = rows * len(parts)
    return [
        out[i * rows : (i + 1) * rows] + out[half + i * rows : half + (i + 1) * rows]
        for i in range(len(parts))
    ]


def bins_on_columns(columns, cells):
    which = lax.broadcasted_iota(jnp.int32, (columns, columns), 0).astype(jnp.float32)
    return (which == cells).astype(jnp.float32).astype(jnp.bfloat16)


def contact_blocks(plan, packed, link_ref):
    group, per = plan.group, plan.per_tile
    lane = lax.broadcasted_iota(jnp.int32, (SUBLANES, LANES), 1) // group
    for q in range(0, plan.sources, per):
        turned = turned_groups([packed(s) for s in range(q, q + per)], group)
        for s in range(per):
            pieces = [jnp.where(lane == s, turned[(s - g) % per], 0.0) for g in range(per)]
            start = (q + s) * group
            link_ref[start : start + group, :] = jnp.concatenate(pieces, axis=0).astype(jnp.bfloat16)


def unpack(plan, tile_of, state_ref, rows):
    per = plan.per_tile
    for t in range(plan.tiles):
        sets = [[tile_of(s, t) for s in range(q, q + per)] for q in range(0, plan.sources, per)]
        for q, parts in enumerate(swap_groups(sets, plan.group)):
            for j, part in enumerate(parts):
                state_ref[t * per + j, rows, q * LANES : (q + 1) * LANES] = part


def touching(plan, parts, matrix):
    quads = plan.sources // plan.per_tile
    blocks = []
    for q in range(quads):
        at = slice(q * LANES, (q + 1) * LANES)
        blocks.append(two_part_dot([x[:, at] for x in parts], matrix[at, :]))
    return [jnp.concatenate([b[i] for b in blocks], axis=1) for i in range(len(parts))]


def tile_lanes(plan):
    return [slice(q * LANES, (q + 1) * LANES) for q in range(plan.sources // plan.per_tile)]


def on_bins(plan, fields, cells):
    tiles = tile_lanes(plan)
    cells = cells.astype(jnp.int32)
    lane, tile = lax.rem(cells, LANES), lax.div(cells, LANES)
    out = []
    for x in fields:
        pieces = []
        for to in tiles:
            found = None
            for q, at in enumerate(tiles):
                moved = jnp.take_along_axis(x[:, at], lane[:, to], axis=1, mode="promise_in_bounds")
                found = moved if found is None else jnp.where(tile[:, to] == q, moved, found)
            pieces.append(found)
        out.append(jnp.concatenate(pieces, axis=1))
    return out


def fixed_fields(products, state_ref, aux_ref, rows):
    to_columns, near = products
    rate = state_ref[FIELD_RATE, rows]
    aux_ref[0, rows] = 1.0 / (1.0 + to_columns([rate])[0])
    aux_ref[1, rows] = near([(rate > 0.0).astype(jnp.float32)])[0]


def collide_rows(plan, products, state_ref, post_ref, aux_ref, u_ref, force_ref, rows):
    to_columns, near = products
    for lanes in tile_lanes(plan):
        popul = [state_ref[i, rows, lanes] for i in range(19)]
        density = popul[0]
        for i in range(1, 19):
            density = density + popul[i]
        inverse = 1.0 / density
        u_ref[3, rows, lanes] = density
        u_ref[4, rows, lanes] = inverse
        for a in range(3):
            rising = [popul[i] for i in range(19) if VELOCITIES[i, a] == 1]
            falling = [popul[i] for i in range(19) if VELOCITIES[i, a] == -1]
            u_ref[a, rows, lanes] = (sum(rising[1:], rising[0]) - sum(falling[1:], falling[0])) * inverse
    rate = state_ref[FIELD_RATE, rows]
    live = (rate > 0.0).astype(jnp.float32)
    velocity = [state_ref[field, rows] for field in FIELD_V]
    speed = on_bins(plan, [u_ref[a, rows] for a in range(3)], state_ref[FIELD_CELL, rows])
    drags = [drag_factor * rate * (speed[a] - velocity[a]) for a in range(3)]
    for a, force in enumerate(to_columns(drags)):
        force_ref[a, rows] = force
    moving = near([velocity[a] * live for a in range(3)])
    count = aux_ref[1, rows]
    for a in range(3):
        push = contact_stiffness * live * (moving[a] - count * velocity[a])
        updated = velocity[a] + drags[a] + push
        if a == 2:
            updated = updated - gravity * live
        state_ref[FIELD_V[a], rows] = updated
    keep, take = 1.0 - 1.0 / relax_time, 1.0 / relax_time
    for lanes in tile_lanes(plan):
        density, inverse = u_ref[3, rows, lanes], u_ref[4, rows, lanes]
        scale = aux_ref[0, rows, lanes]
        share = relax_time * inverse
        target = [scale * (u_ref[a, rows, lanes] - share * force_ref[a, rows, lanes]) for a in range(3)]
        square = target[0] * target[0] + target[1] * target[1] + target[2] * target[2]
        base = 1.0 - 1.5 * square
        triple = [3.0 * x for x in target]
        shares = {w: (take * float(w)) * density for w in sorted(set(WEIGHTS))}
        post_ref[0, rows, lanes] = keep * state_ref[0, rows, lanes] + shares[WEIGHTS[0]] * base
        for i in range(1, 19, 2):
            along = None
            for a in range(3):
                if VELOCITIES[i, a] != 0:
                    if along is None:
                        along = triple[a] if VELOCITIES[i, a] == 1 else -triple[a]
                    else:
                        along = along + triple[a] if VELOCITIES[i, a] == 1 else along - triple[a]
            level = base + 0.5 * (along * along)
            share_i = shares[WEIGHTS[i]]
            post_ref[i, rows, lanes] = keep * state_ref[i, rows, lanes] + share_i * (level + along)
            post_ref[i + 1, rows, lanes] = keep * state_ref[i + 1, rows, lanes] + share_i * (level - along)


def stream_rows(plan, state_ref, post_ref, ground, ceiling):
    rows, group, dx, dy = plan.rows, plan.group, plan.dx, plan.dy
    lane = lax.broadcasted_iota(jnp.int32, (rows, LANES), 1)
    row = lax.broadcasted_iota(jnp.int32, (rows, LANES), 0)
    lane_y = lax.div(lane, group) * dy + lax.rem(lane, dy)
    lane_x = lax.rem(lax.div(lane, dy), dx)
    bottom, top = ground & (row == 0), ceiling & (row == plan.own - 1)
    tiles = tile_lanes(plan)
    for i in range(19):
        cx, cy, cz = (int(c) for c in VELOCITIES[i])
        moved = [post_ref[i, :, lanes] for lanes in tiles]
        if cx or cy:
            y = lax.rem(lane_y - cy + plan.n_gy * dy, plan.n_gy * dy)
            x = lax.rem(lane_x - cx + dx, dx)
            from_lane = lax.div(y, dy) * group + x * dy + lax.rem(y, dy)
            moved = [jnp.take_along_axis(x, from_lane, axis=1, mode="promise_in_bounds") for x in moved]
        if cx:
            edge = lane_x == (0 if cx == 1 else dx - 1)
            moved = [jnp.where(edge, moved[(q - cx) % len(tiles)], moved[q]) for q in range(len(tiles))]
        for x, lanes in zip(moved, tiles):
            if cz:
                x = pltpu.roll(x, cz % rows, 0)
                x = jnp.where(bottom if cz == 1 else top, post_ref[OPPOSITE[i], :, lanes], x)
            state_ref[i, :, lanes] = x


def settle_kernel(plan, in_ref, state_ref, post_ref, aux_ref, column_ref, link_ref, u_ref, force_ref):
    own = slice(0, plan.own)
    unpack(plan, lambda s, t: in_ref[s, :, t * LANES : (t + 1) * LANES], state_ref, own)
    column_ref[...] = bins_on_columns(plan.columns, state_ref[FIELD_CELL, 0:1, :])
    contact_blocks(plan, lambda s: in_ref[s, :, plan.width :], link_ref)
    products = (
        lambda parts: two_part_dot(parts, column_ref[...]),
        lambda parts: touching(plan, parts, link_ref),
    )
    fixed_fields(products, state_ref, aux_ref, own)
    collide_rows(plan, products, state_ref, post_ref, aux_ref, u_ref, force_ref, own)


def substeps_kernel(plan, settled_ref, collided_ref, fixed_ref, column_ref, link_ref, inner_ref, outer_ref,
                    out_ref, state_ref, post_ref, aux_ref, u_ref, force_ref, other_column_ref, other_link_ref):
    rows, columns, group, per = plan.rows, plan.columns, plan.group, plan.per_tile
    halo, own = plan.halo, plan.own
    window, layer = plan.place()
    even = lax.rem(window, 2) == 0
    first, last = window == 0, window == plan.sources - 1
    ground, ceiling = first & (layer == 0), last & (layer == plan.n_gz - 1)
    tile_row = lax.broadcasted_iota(jnp.int32, (SUBLANES, LANES), 0)
    beyond = slice(own, rows)

    def halo_tile(s, t):
        at = slice(t * LANES, (t + 1) * LANES)
        inner, outer = inner_ref[s // 2, :, at], outer_ref[s // 2, :, at]
        below = jnp.where(even, outer, inner)
        above = jnp.where(even, inner, outer)
        if s % 2:
            above = pltpu.roll(above, halo, 0)
        else:
            below = pltpu.roll(below, halo, 0)
        return jnp.where(tile_row < halo, above, below)

    unpack(plan, halo_tile, state_ref, beyond)
    other_cells = jnp.where(first, state_ref[FIELD_CELL, rows - 1 : rows, :], state_ref[FIELD_CELL, own : own + 1, :])
    other_column_ref[...] = bins_on_columns(columns, other_cells)

    def other_contacts(s):
        start = plan.width + s % 2 * LANES
        return outer_ref[s // 2, :, start : start + LANES]

    contact_blocks(plan, other_contacts, other_link_ref)

    halo_row = lax.broadcasted_iota(jnp.int32, (SUBLANES, columns), 0)
    foreign = (last & (halo_row < halo)) | (first & (halo_row >= halo))

    def both_layers(product, own_matrix, other_matrix):
        def call(parts):
            mine = product(parts, own_matrix)
            others = product([x[-SUBLANES:] for x in parts], other_matrix)
            if parts[0].shape[0] == SUBLANES:
                return [jnp.where(foreign, b, a) for a, b in zip(mine, others)]
            return [
                jnp.concatenate([a[:own], jnp.where(foreign, b, a[own:])], axis=0) for a, b in zip(mine, others)
            ]

        return call

    products = (
        both_layers(lambda x, m: two_part_dot(x, m[...]), column_ref, other_column_ref),
        both_layers(lambda x, m: touching(plan, x, m), link_ref, other_link_ref),
    )
    fixed_fields(products, state_ref, aux_ref, beyond)
    collide_rows(plan, products, state_ref, post_ref, aux_ref, u_ref, force_ref, beyond)
    stream_rows(plan, state_ref, post_ref, ground, ceiling)

    def step(_, carry):
        collide_rows(plan, products, state_ref, post_ref, aux_ref, u_ref, force_ref, slice(0, rows))
        stream_rows(plan, state_ref, post_ref, ground, ceiling)
        return carry

    lax.fori_loop(1, SUBSTEPS, step, 0)

    for t in range(plan.tiles):
        sets = [[state_ref[t * per + j, 0:own, lanes] for j in range(per)] for lanes in tile_lanes(plan)]
        for q, parts in enumerate(swap_groups(sets, group)):
            for s, part in enumerate(parts):
                out_ref[q * per + s, :, t * LANES : (t + 1) * LANES] = part


def finish_kernel(plan, in_ref, pop_ref, vel_ref, stage, sems):
    whole = 19 * plan.group // LANES
    end = 19 * plan.group
    split = whole * LANES // 2
    holders = [plan.holder(q) for q in range(plan.sources)]
    moves = {
        plan.tiles - 1: (stage.at[end : end + 3 * plan.bins], vel_ref),
        whole // 2 - 1: (stage.at[:split], pop_ref.at[:split]),
        whole - 1: (stage.at[split:end], pop_ref.at[split:]),
    }
    copies = []
    for t in (whole, whole + 1, *range(whole)):
        at = slice(t * LANES, (t + 1) * LANES)
        stage[at, :] = jnp.concatenate([in_ref[holders[q], :, at] for q in range(plan.sources)], axis=0).T
        if t in moves:
            copies.append(pltpu.make_async_copy(*moves[t], sems.at[len(copies)]))
            copies[-1].start()
    for copy in copies:
        copy.wait()


def windows_body(plan, populations, grain_velocity, grain_volume, slots, contacts, bin_cell):
    group, bins, sources = plan.group, plan.bins, plan.sources
    rows, columns, own = plan.rows, plan.columns, plan.own
    f32, bf16, i32 = jnp.float32, jnp.bfloat16, jnp.int32
    half = sources // 2

    def call(kernel, shapes, inputs, scratch=(), where=(VMEM, VMEM), aliases=None):
        if where[0] is HBM:
            inputs = [pltpu.with_memory_space_constraint(x, pltpu.HBM) for x in inputs]
        shapes = [jax.ShapeDtypeStruct(shape, kind) for shape, kind in shapes]
        return pl.pallas_call(
            lambda *refs: kernel(plan, *refs),
            out_shape=shapes,
            in_specs=[where[0]] * len(inputs),
            out_specs=[where[1]] * len(shapes),
            scratch_shapes=list(scratch),
            input_output_aliases=aliases or {},
            compiler_params=pltpu.CompilerParams(vmem_limit_bytes=VMEM_LIMIT),
        )(*inputs)

    (outgoing,) = call(
        prepare_kernel,
        [((sources, own, plan.wide), f32)],
        (
            populations.reshape(19 * group, LANES),
            grain_velocity.reshape(3 * bins, LANES),
            grain_volume,
            slots,
            contacts,
            bin_cell.reshape(1, bins),
        ),
        (
            pltpu.VMEM((plan.width, LANES), f32),
            pltpu.VMEM((bins, LANES), i32),
            pltpu.VMEM((bins, bins), i32),
            pltpu.VMEM((1, bins), i32),
            pltpu.SemaphoreType.DMA((16,)),
        ),
        (HBM, VMEM),
    )
    layer_axes, every_axis = ("gx", "gy"), ("gx", "gy", "gz")
    incoming = lax.all_to_all(outgoing, layer_axes, split_axis=0, concat_axis=0, tiled=True)
    inner, outer = call(
        edges_kernel,
        [((half, SUBLANES, plan.width), f32), ((half, SUBLANES, plan.width + 2 * LANES), f32)],
        (incoming,),
    )
    inner = lax.ppermute(inner, every_axis, plan.swaps(0))
    outer = lax.ppermute(outer, every_axis, plan.swaps(1))
    carried = [
        ((plan.fields, rows, columns), f32),
        ((19, rows, columns), f32),
        ((2, rows, columns), f32),
    ]
    moments_and_forces = (pltpu.VMEM((5, rows, columns), f32), pltpu.VMEM((3, rows, columns), f32))
    *settled, column, link = call(
        settle_kernel,
        carried + [((columns, columns), bf16), ((columns, LANES), bf16)],
        (incoming,),
        moments_and_forces,
    )
    back, *_ = call(
        substeps_kernel,
        [((sources, own, plan.width), f32)] + carried,
        (*settled, column, link, inner, outer),
        (
            *moments_and_forces,
            pltpu.VMEM((columns, columns), bf16),
            pltpu.VMEM((columns, LANES), bf16),
        ),
        aliases={0: 1, 1: 2, 2: 3},
    )
    result = lax.all_to_all(back, layer_axes, split_axis=0, concat_axis=0, tiled=True)
    fluid, velocity = call(
        finish_kernel,
        [((19 * group, LANES), f32), ((3 * bins, LANES), f32)],
        (result,),
        (pltpu.VMEM((plan.width, LANES), f32), pltpu.SemaphoreType.DMA((16,))),
        (VMEM, HBM),
    )
    return (fluid.reshape(populations.shape), velocity.reshape(grain_velocity.shape))


def body(populations, grain_velocity, grain_volume, slots, contacts, bin_cell):
    plan = Plan(
        lax.axis_size("gx"),
        lax.axis_size("gy"),
        lax.axis_size("gz"),
        populations,
        contacts,
        grain_velocity.shape[2],
    )
    arrays = (populations, grain_velocity, grain_volume, slots, contacts, bin_cell)
    if plan.fits() and contacts.shape[0] == contacts.shape[1]:
        return windows_body(plan, *arrays)
    return columns_body(*arrays)


def solution(mesh):
    placed = (
        P(None, "gx", "gy", "gz"),
        P(None, ("gx", "gy", "gz"), None),
        P(("gx", "gy", "gz"), None),
        P(("gx", "gy", "gz"), None),
        P(("gx", "gy", "gz"), None),
        P(("gx", "gy", "gz")),
    )
    return jax.shard_map(
        body,
        mesh=mesh,
        in_specs=placed,
        out_specs=(P(None, "gx", "gy", "gz"), P(None, ("gx", "gy", "gz"), None)),
        check_vma=False,
    )
```

```python
import jax
import jax.numpy as jnp
import numpy as np
from jax import lax
from jax.experimental import pallas as pl
from jax.experimental.pallas import tpu as pltpu
from jax.sharding import PartitionSpec as P

SUBSTEPS = 4


VELOCITIES = np.array(
    [
        [0, 0, 0],
        [1, 0, 0],
        [-1, 0, 0],
        [0, 1, 0],
        [0, -1, 0],
        [0, 0, 1],
        [0, 0, -1],
        [1, 1, 0],
        [-1, -1, 0],
        [1, -1, 0],
        [-1, 1, 0],
        [1, 0, 1],
        [-1, 0, -1],
        [1, 0, -1],
        [-1, 0, 1],
        [0, 1, 1],
        [0, -1, -1],
        [0, 1, -1],
        [0, -1, 1],
    ]
)
WEIGHTS = np.array([1.0 / 3.0] + [1.0 / 18.0] * 6 + [1.0 / 36.0] * 12)
OPPOSITE = [0, 2, 1, 4, 3, 6, 5, 8, 7, 10, 9, 12, 11, 14, 13, 16, 15, 18, 17]
relax_time = 0.8
contact_stiffness = 0.1
drag_factor = 2.0
gravity = 0.01


def passed_along(x, axis, by):
    length = lax.axis_size(axis)
    return lax.ppermute(x, axis, [(i, (i + by) % length) for i in range(length)])


def passed_along_2(value, axis, steps):
    count = lax.axis_size(axis)
    leading, last = (max(0, -steps), min(count, count - steps))
    return lax.ppermute(value, axis, [(source, source + steps) for source in range(leading, last)])


def moments(popul):
    density = jnp.sum(popul, axis=0)
    speed = []
    for axis in range(3):
        rising = np.array([i for i in range(19) if VELOCITIES[i, axis] == 1])
        falling = np.array([i for i in range(19) if VELOCITIES[i, axis] == -1])
        momentum = jnp.sum(popul[rising], axis=0) - jnp.sum(popul[falling], axis=0)
        speed.append(momentum / density)
    return (density, speed)


def grain_step(block, velocity, live, volume, links):
    grains = velocity.shape[2]
    bins = links.shape[1]
    groups = velocity.shape[1] // bins
    rate = drag_factor * volume * live
    drag = rate[None] * (block[:3] - velocity)
    moving = (velocity * live[None]).reshape(3, groups, bins, grains)
    pairs = links.reshape(groups, bins, bins)
    near = jnp.einsum("gkj,cgjs->cgks", pairs, moving, precision=lax.Precision.HIGHEST).reshape(
        3, -1, grains
    )
    count = jnp.einsum(
        "gkj,gjs->gks", pairs, live.reshape(groups, bins, grains), precision=lax.Precision.HIGHEST
    ).reshape(-1, grains)
    push = contact_stiffness * live[None] * (near - count[None] * velocity)
    fall = jnp.asarray([0.0, 0.0, gravity], jnp.float32).reshape(3, 1, 1) * live[None]
    updated = velocity + drag + push - fall
    forces = jnp.concatenate([-drag, (volume * live)[None]], axis=0)
    return (updated, forces)


def collide(popul, density, speed, field):
    scale = 1.0 / (1.0 + field[3])
    target = [scale * (speed[a] + relax_time * field[a] / density) for a in range(3)]
    square = target[0] * target[0] + target[1] * target[1] + target[2] * target[2]
    rows = []
    for i in range(19):
        along = jnp.zeros_like(density)
        for a in range(3):
            if VELOCITIES[i, a] != 0:
                along = along + float(VELOCITIES[i, a]) * target[a]
        equil = (
            float(WEIGHTS[i]) * density * (1.0 + 3.0 * along + 4.5 * along * along - 1.5 * square)
        )
        rows.append(popul[i] - (popul[i] - equil) / relax_time)
    return jnp.stack(rows)


def walls(moved, post):
    depth = post.shape[3]
    zpos = jnp.arange(depth)
    bottom = (zpos == 0) & (lax.axis_index("gz") == 0)
    top = (zpos == depth - 1) & (lax.axis_index("gz") == lax.axis_size("gz") - 1)
    rows = []
    for i in range(19):
        layer = moved[i]
        if VELOCITIES[i, 2] == 1:
            layer = jnp.where(bottom, post[OPPOSITE[i]], layer)
        elif VELOCITIES[i, 2] == -1:
            layer = jnp.where(top, post[OPPOSITE[i]], layer)
        rows.append(layer)
    return jnp.stack(rows)


def leaving(axis):
    rising = np.array([i for i in range(19) if VELOCITIES[i, axis] == 1])
    falling = np.array([i for i in range(19) if VELOCITIES[i, axis] == -1])
    return (rising, falling)


def stream(post):
    moved = post
    rising, falling = leaving(0)
    upper = moved[rising]
    lower = moved[falling]
    edge_up = passed_along(upper[:, -1:], "gx", 1)
    edge_down = passed_along(lower[:, :1], "gx", -1)
    moved = moved.at[rising].set(jnp.concatenate([edge_up, upper[:, :-1]], axis=1))
    moved = moved.at[falling].set(jnp.concatenate([lower[:, 1:], edge_down], axis=1))
    rising, falling = leaving(1)
    upper = moved[rising]
    lower = moved[falling]
    edge_up = passed_along(upper[:, :, -1:], "gy", 1)
    edge_down = passed_along(lower[:, :, :1], "gy", -1)
    moved = moved.at[rising].set(jnp.concatenate([edge_up, upper[:, :, :-1]], axis=2))
    moved = moved.at[falling].set(jnp.concatenate([lower[:, :, 1:], edge_down], axis=2))
    rising, falling = leaving(2)
    upper = moved[rising]
    lower = moved[falling]
    edge_up = passed_along_2(upper[:, :, :, -1:], "gz", 1)
    edge_down = passed_along_2(lower[:, :, :, :1], "gz", -1)
    moved = moved.at[rising].set(jnp.concatenate([edge_up, upper[:, :, :, :-1]], axis=3))
    moved = moved.at[falling].set(jnp.concatenate([lower[:, :, :, 1:], edge_down], axis=3))
    return walls(moved, post)


def carry_flow(outgoing):
    result = lax.all_to_all(outgoing, ("gx", "gy"), split_axis=1, concat_axis=1, tiled=True)
    return result


def carry_force(outgoing):
    result = lax.all_to_all(outgoing, ("gx", "gy"), split_axis=1, concat_axis=1, tiled=True)
    return result


def rank_within(source):
    count = source.shape[-1]
    before = jnp.arange(count)[None, :] < jnp.arange(count)[:, None]
    same = source[..., :, None] == source[..., None, :]
    return jnp.sum((same & before).astype(jnp.int32), axis=-1)


def columns_body(populations, grain_velocity, grain_volume, slots, contacts, bin_cell):
    n_gx = lax.axis_size("gx")
    n_gy = lax.axis_size("gy")
    n_gz = lax.axis_size("gz")
    sources = n_gx * n_gy
    bins = contacts.shape[1]
    grains = grain_velocity.shape[2]
    depth_x, depth_y, depth_z = (populations.shape[1], populations.shape[2], populations.shape[3])
    zblocks = depth_z // grains
    capacity = max(2, 4 * bins // sources)
    width_y = depth_y * n_gy
    column_blocks = depth_z * n_gz // grains

    def locate(cells):
        xcell = cells // (width_y * column_blocks)
        ycell = cells // column_blocks % width_y
        zblock = cells % column_blocks
        source = xcell // depth_x * n_gy + ycell // depth_y
        local = (xcell % depth_x * depth_y + ycell % depth_y) * zblocks + zblock % zblocks
        return (source, local)

    own_source, own_local = locate(bin_cell)
    own_row = own_source * capacity + rank_within(own_source)
    every = lax.all_gather(bin_cell, ("gx", "gy"), axis=0, tiled=True).reshape(sources, bins)
    all_source, all_local = locate(every)
    all_rank = rank_within(all_source)
    here = lax.axis_index("gx") * n_gy + lax.axis_index("gy")
    slot_ids = jnp.arange(capacity, dtype=jnp.int32)
    picked = (all_source == here)[:, None, :] & (all_rank[:, None, :] == slot_ids[None, :, None])
    send_column = jnp.sum(jnp.where(picked, all_local[:, None, :], 0), axis=2).reshape(-1)
    send_mask = jnp.any(picked, axis=2).reshape(-1).astype(jnp.float32)
    live = slots.astype(jnp.float32)
    links = contacts.astype(jnp.float32)
    fluid = populations
    velocity = grain_velocity
    for step in range(SUBSTEPS):
        density, speed = moments(fluid)
        flow = jnp.stack(speed + [density]).reshape(4, -1, grains)
        outgoing = jnp.take(flow, send_column, axis=1) * send_mask[None, :, None]
        incoming = carry_flow(outgoing)
        block = jnp.take(incoming, own_row, axis=1)
        velocity, forces = grain_step(block, velocity, live, grain_volume, links)
        back = jnp.zeros((4, sources * capacity, grains), jnp.float32).at[:, own_row].set(forces)
        returned = carry_force(back)
        field = jnp.zeros_like(flow).at[:, send_column].add(returned * send_mask[None, :, None])
        field = field.reshape(4, depth_x, depth_y, depth_z)
        post = collide(fluid, density, speed, field)
        fluid = stream(post)
    return (fluid, velocity)


LANES = 128
SUBLANES = 8
VMEM_LIMIT = 24 * 1024 * 1024
VMEM = pl.BlockSpec(memory_space=pltpu.VMEM)
HBM = pl.BlockSpec(memory_space=pltpu.HBM)
FIELD_V = (19, 20, 21)
FIELD_CELL = 22
FIELD_RATE = 23


class Plan:
    def __init__(self, n_gx, n_gy, n_gz, populations, contacts, grains):
        self.n_gx, self.n_gy, self.n_gz = n_gx, n_gy, n_gz
        self.dx, self.dy, self.depth = populations.shape[1:]
        self.grains = grains
        self.bins = contacts.shape[1]
        self.sources = n_gx * n_gy
        self.group = self.dx * self.dy
        self.halo = SUBSTEPS
        self.own = self.depth // self.sources
        self.rows = self.own + 2 * self.halo
        self.columns = self.sources * self.group
        self.per_tile = max(1, LANES // self.group)
        self.fields = 24
        self.tiles = self.fields // self.per_tile
        self.width = self.fields * self.group
        self.wide = self.width + LANES
        self.returned = (2 * self.tiles - 1) * LANES

    def fits(self):
        group = self.group
        return (
            self.sources % 2 == 0
            and self.depth == LANES
            and self.grains == LANES
            and self.own * self.sources == LANES
            and self.own == SUBLANES == 2 * self.halo
            and self.rows == 2 * SUBLANES
            and group == self.bins
            and group * group == SUBLANES * LANES
            and self.per_tile == self.n_gy
        )

    def along(self, window):
        gx, r = divmod(window, self.n_gy)
        return gx * self.n_gy + (self.n_gy - 1 - r if gx % 2 else r)

    def device(self, window):
        layer, local = divmod(window, self.sources)
        if layer % 2:
            local = self.sources - 1 - local
        return self.along(local) * self.n_gz + layer

    def swaps(self, start):
        count = self.n_gz * self.sources
        paired = []
        for a in range(start, count - 1, 2):
            paired += [(a, a + 1), (a + 1, a)]
        if start:
            paired += [(0, count - 1), (count - 1, 0)]
        return [(self.device(a), self.device(b)) for a, b in paired]

    def place(self):
        gx, gy, layer = (lax.axis_index(name) for name in ("gx", "gy", "gz"))
        local = gx * self.n_gy + jnp.where(lax.rem(gx, 2) == 1, self.n_gy - 1 - gy, gy)
        return jnp.where(lax.rem(layer, 2) == 1, self.sources - 1 - local, local), layer

    def holder(self, window):
        odd = lax.rem(lax.axis_index("gz"), 2) == 1
        return jnp.where(odd, self.along(self.sources - 1 - window), self.along(window))


def pick(group, parts):
    lane = lax.broadcasted_iota(jnp.int32, parts[0].shape, 1) // group
    step = 1
    while len(parts) > 1:
        odd = lane // step % 2 == 1
        parts = [jnp.where(odd, b, a) for a, b in zip(parts[::2], parts[1::2])]
        step *= 2
    return parts[0]


def turned_groups(parts, group):
    count = len(parts)
    turned = []
    for r in range(count):
        chosen = pick(group, [parts[(g + r) % count] for g in range(count)])
        turned.append(pltpu.roll(chosen, r * group, 1) if r else chosen)
    return turned


def swap_groups(sets, group):
    turned = [turned_groups(parts, group) for parts in sets]
    count = len(sets[0])
    return [[pick(group, [t[(g - j) % count] for g in range(count)]) for j in range(count)] for t in turned]


def prepare_kernel(plan, pop_ref, vel_ref, vol_ref, slot_ref, link_ref, cell_ref, out_ref,
                   pops, slots, links, cells, sems):
    group, bins, own = plan.group, plan.bins, plan.own
    whole = 19 * group // LANES
    end = plan.width
    vel_start = 19 * group
    split = whole * LANES // 2
    moves = [
        (cell_ref, cells),
        (link_ref, links),
        (slot_ref, slots),
        (vol_ref, pops.at[end - bins : end]),
        (vel_ref, pops.at[vel_start : vel_start + 3 * bins]),
        (pop_ref.at[split:], pops.at[split:vel_start]),
        (pop_ref.at[:split], pops.at[:split]),
    ]
    copies = [pltpu.make_async_copy(a, b, sems.at[i]) for i, (a, b) in enumerate(moves)]
    for copy in copies:
        copy.start()
    for copy in copies:
        copy.wait()

    cell = cells[...]
    width_y = plan.dy * plan.n_gy
    xcell = lax.div(cell, width_y * plan.n_gz)
    ycell = lax.rem(lax.div(cell, plan.n_gz), width_y)
    source = lax.div(xcell, plan.dx) * plan.n_gy + lax.div(ycell, plan.dy)
    cell = source * group + lax.rem(xcell, plan.dx) * plan.dy + lax.rem(ycell, plan.dy)
    blank = jnp.zeros((1, bins), jnp.float32)
    cell = jnp.concatenate([blank, blank, cell.astype(jnp.float32), blank], axis=1)
    packed = jnp.concatenate(
        [links[g * SUBLANES : (g + 1) * SUBLANES, :].astype(jnp.float32) for g in range(bins // SUBLANES)],
        axis=1,
    )
    holders = [plan.holder(q) for q in range(plan.sources)]
    for q in range(plan.sources):
        out_ref[q, :, plan.width :] = packed
    for t in range(plan.tiles):
        block = pops[t * LANES : (t + 1) * LANES, :]
        if t == plan.tiles - 1:
            rate = pops[end - bins : end, :] * slots[...].astype(jnp.float32)
            block = jnp.concatenate([block[: 2 * bins], rate, rate], axis=0)
        block = block.T
        if t == plan.tiles - 1:
            lane = lax.broadcasted_iota(jnp.int32, block.shape, 1) // bins
            block = jnp.where(lane == FIELD_CELL % plan.per_tile, cell, block)
        for q in range(plan.sources):
            out_ref[holders[q], :, t * LANES : (t + 1) * LANES] = block[q * own : (q + 1) * own, :]


def edges_kernel(plan, in_ref, inner_ref, outer_ref):
    window, _ = plan.place()
    even = lax.rem(window, 2) == 0
    halo = plan.halo
    low_rows = lax.broadcasted_iota(jnp.int32, (SUBLANES, LANES), 0) < halo
    for h in range(plan.sources // 2):
        for t in range(plan.tiles):
            lanes = slice(t * LANES, (t + 1) * LANES)
            a, b = in_ref[2 * h, :, lanes], in_ref[2 * h + 1, :, lanes]
            low = jnp.where(low_rows, a, pltpu.roll(b, halo, 0))
            high = jnp.where(low_rows, pltpu.roll(a, halo, 0), b)
            inner_ref[h, :, lanes] = jnp.where(even, high, low)
            outer_ref[h, :, lanes] = jnp.where(even, low, high)
        for k in range(2):
            start = plan.width + k * LANES
            outer_ref[h, :, start : start + LANES] = in_ref[2 * h + k, :, plan.width :]


def two_part_dot(parts, matrix):
    whole = jnp.concatenate(parts, axis=0)
    rest = whole - whole.astype(jnp.bfloat16).astype(jnp.float32)
    stacked = jnp.concatenate([whole, rest], axis=0).astype(jnp.bfloat16)
    out = lax.dot_general(
        stacked, matrix, (((1,), (1,)), ((), ())), preferred_element_type=jnp.float32
    )
    rows = parts[0].shape[0]
    half = rows * len(parts)
    return [
        out[i * rows : (i + 1) * rows] + out[half + i * rows : half + (i + 1) * rows]
        for i in range(len(parts))
    ]


def bins_on_columns(columns, cells):
    which = lax.broadcasted_iota(jnp.int32, (columns, columns), 0).astype(jnp.float32)
    return (which == cells).astype(jnp.float32).astype(jnp.bfloat16)


def contact_blocks(plan, packed, link_ref):
    group, per = plan.group, plan.per_tile
    lane = lax.broadcasted_iota(jnp.int32, (SUBLANES, LANES), 1) // group
    for q in range(0, plan.sources, per):
        turned = turned_groups([packed(s) for s in range(q, q + per)], group)
        for s in range(per):
            pieces = [jnp.where(lane == s, turned[(s - g) % per], 0.0) for g in range(per)]
            start = (q + s) * group
            link_ref[start : start + group, :] = jnp.concatenate(pieces, axis=0).astype(jnp.bfloat16)


def unpack(plan, tile_of, state_ref, rows):
    per = plan.per_tile
    for t in range(plan.tiles):
        sets = [[tile_of(s, t) for s in range(q, q + per)] for q in range(0, plan.sources, per)]
        for q, parts in enumerate(swap_groups(sets, plan.group)):
            for j, part in enumerate(parts):
                state_ref[t * per + j, rows, q * LANES : (q + 1) * LANES] = part


def touching(plan, parts, matrix):
    quads = plan.sources // plan.per_tile
    blocks = []
    for q in range(quads):
        at = slice(q * LANES, (q + 1) * LANES)
        blocks.append(two_part_dot([x[:, at] for x in parts], matrix[at, :]))
    return [jnp.concatenate([b[i] for b in blocks], axis=1) for i in range(len(parts))]


def tile_lanes(plan):
    return [slice(q * LANES, (q + 1) * LANES) for q in range(plan.sources // plan.per_tile)]


def on_bins(plan, fields, cells):
    tiles = tile_lanes(plan)
    cells = cells.astype(jnp.int32)
    lane, tile = lax.rem(cells, LANES), lax.div(cells, LANES)
    out = []
    for x in fields:
        pieces = []
        for to in tiles:
            found = None
            for q, at in enumerate(tiles):
                moved = jnp.take_along_axis(x[:, at], lane[:, to], axis=1, mode="promise_in_bounds")
                found = moved if found is None else jnp.where(tile[:, to] == q, moved, found)
            pieces.append(found)
        out.append(jnp.concatenate(pieces, axis=1))
    return out


def collide_rows(plan, products, state_ref, post_ref, aux_ref, u_ref, force_ref, rows, begin=False):
    to_columns, near = products
    for lanes in tile_lanes(plan):
        popul = [state_ref[i, rows, lanes] for i in range(19)]
        density = popul[0]
        for i in range(1, 19):
            density = density + popul[i]
        inverse = 1.0 / density
        u_ref[3, rows, lanes] = density
        u_ref[4, rows, lanes] = inverse
        for a in range(3):
            rising = [popul[i] for i in range(19) if VELOCITIES[i, a] == 1]
            falling = [popul[i] for i in range(19) if VELOCITIES[i, a] == -1]
            u_ref[a, rows, lanes] = (sum(rising[1:], rising[0]) - sum(falling[1:], falling[0])) * inverse
    rate = state_ref[FIELD_RATE, rows]
    live = (rate > 0.0).astype(jnp.float32)
    velocity = [state_ref[field, rows] for field in FIELD_V]
    speed = on_bins(plan, [u_ref[a, rows] for a in range(3)], state_ref[FIELD_CELL, rows])
    drags = [drag_factor * rate * (speed[a] - velocity[a]) for a in range(3)]
    moving = [velocity[a] * live for a in range(3)]
    if begin:
        *forces, solid = to_columns(drags + [rate])
        *moving, count = near(moving + [live])
        aux_ref[0, rows] = 1.0 / (1.0 + solid)
        aux_ref[1, rows] = count
    else:
        forces = to_columns(drags)
        moving = near(moving)
        count = aux_ref[1, rows]
    for a, force in enumerate(forces):
        force_ref[a, rows] = force
    for a in range(3):
        push = contact_stiffness * live * (moving[a] - count * velocity[a])
        updated = velocity[a] + drags[a] + push
        if a == 2:
            updated = updated - gravity * live
        state_ref[FIELD_V[a], rows] = updated
    keep, take = 1.0 - 1.0 / relax_time, 1.0 / relax_time
    for lanes in tile_lanes(plan):
        density, inverse = u_ref[3, rows, lanes], u_ref[4, rows, lanes]
        scale = aux_ref[0, rows, lanes]
        share = relax_time * inverse
        target = [scale * (u_ref[a, rows, lanes] - share * force_ref[a, rows, lanes]) for a in range(3)]
        square = target[0] * target[0] + target[1] * target[1] + target[2] * target[2]
        base = 1.0 - 1.5 * square
        triple = [3.0 * x for x in target]
        shares = {w: (take * float(w)) * density for w in sorted(set(WEIGHTS))}
        post_ref[0, rows, lanes] = keep * state_ref[0, rows, lanes] + shares[WEIGHTS[0]] * base
        for i in range(1, 19, 2):
            along = None
            for a in range(3):
                if VELOCITIES[i, a] != 0:
                    if along is None:
                        along = triple[a] if VELOCITIES[i, a] == 1 else -triple[a]
                    else:
                        along = along + triple[a] if VELOCITIES[i, a] == 1 else along - triple[a]
            level = base + 0.5 * (along * along)
            share_i = shares[WEIGHTS[i]]
            post_ref[i, rows, lanes] = keep * state_ref[i, rows, lanes] + share_i * (level + along)
            post_ref[i + 1, rows, lanes] = keep * state_ref[i + 1, rows, lanes] + share_i * (level - along)


def stream_rows(plan, state_ref, post_ref, ground, ceiling):
    rows, group, dx, dy = plan.rows, plan.group, plan.dx, plan.dy
    lane = lax.broadcasted_iota(jnp.int32, (rows, LANES), 1)
    row = lax.broadcasted_iota(jnp.int32, (rows, LANES), 0)
    lane_y = lax.div(lane, group) * dy + lax.rem(lane, dy)
    lane_x = lax.rem(lax.div(lane, dy), dx)
    bottom, top = ground & (row == 0), ceiling & (row == plan.own - 1)
    tiles = tile_lanes(plan)
    for i in range(19):
        cx, cy, cz = (int(c) for c in VELOCITIES[i])
        moved = [post_ref[i, :, lanes] for lanes in tiles]
        if cx or cy:
            y = lax.rem(lane_y - cy + plan.n_gy * dy, plan.n_gy * dy)
            x = lax.rem(lane_x - cx + dx, dx)
            from_lane = lax.div(y, dy) * group + x * dy + lax.rem(y, dy)
            moved = [jnp.take_along_axis(x, from_lane, axis=1, mode="promise_in_bounds") for x in moved]
        if cx:
            edge = lane_x == (0 if cx == 1 else dx - 1)
            moved = [jnp.where(edge, moved[(q - cx) % len(tiles)], moved[q]) for q in range(len(tiles))]
        for x, lanes in zip(moved, tiles):
            if cz:
                x = pltpu.roll(x, cz % rows, 0)
                x = jnp.where(bottom if cz == 1 else top, post_ref[OPPOSITE[i], :, lanes], x)
            state_ref[i, :, lanes] = x


def settle_kernel(plan, in_ref, state_ref, post_ref, aux_ref, column_ref, link_ref, u_ref, force_ref):
    own = slice(0, plan.own)
    unpack(plan, lambda s, t: in_ref[s, :, t * LANES : (t + 1) * LANES], state_ref, own)
    column_ref[...] = bins_on_columns(plan.columns, state_ref[FIELD_CELL, 0:1, :])
    contact_blocks(plan, lambda s: in_ref[s, :, plan.width :], link_ref)
    products = (
        lambda parts: two_part_dot(parts, column_ref[...]),
        lambda parts: touching(plan, parts, link_ref),
    )
    collide_rows(plan, products, state_ref, post_ref, aux_ref, u_ref, force_ref, own, True)


def substeps_kernel(plan, settled_ref, collided_ref, fixed_ref, column_ref, link_ref, inner_ref, outer_ref,
                    out_ref, state_ref, post_ref, aux_ref, u_ref, force_ref, other_column_ref, other_link_ref):
    rows, columns, group, per = plan.rows, plan.columns, plan.group, plan.per_tile
    halo, own = plan.halo, plan.own
    window, layer = plan.place()
    even = lax.rem(window, 2) == 0
    first, last = window == 0, window == plan.sources - 1
    ground, ceiling = first & (layer == 0), last & (layer == plan.n_gz - 1)
    tile_row = lax.broadcasted_iota(jnp.int32, (SUBLANES, LANES), 0)
    beyond = slice(own, rows)

    def halo_tile(s, t):
        at = slice(t * LANES, (t + 1) * LANES)
        inner, outer = inner_ref[s // 2, :, at], outer_ref[s // 2, :, at]
        below = jnp.where(even, outer, inner)
        above = jnp.where(even, inner, outer)
        if s % 2:
            above = pltpu.roll(above, halo, 0)
        else:
            below = pltpu.roll(below, halo, 0)
        return jnp.where(tile_row < halo, above, below)

    unpack(plan, halo_tile, state_ref, beyond)
    other_cells = jnp.where(first, state_ref[FIELD_CELL, rows - 1 : rows, :], state_ref[FIELD_CELL, own : own + 1, :])
    other_column_ref[...] = bins_on_columns(columns, other_cells)

    def other_contacts(s):
        start = plan.width + s % 2 * LANES
        return outer_ref[s // 2, :, start : start + LANES]

    contact_blocks(plan, other_contacts, other_link_ref)

    halo_row = lax.broadcasted_iota(jnp.int32, (SUBLANES, columns), 0)
    foreign = (last & (halo_row < halo)) | (first & (halo_row >= halo))

    def both_layers(product, own_matrix, other_matrix):
        def call(parts):
            mine = product(parts, own_matrix)
            others = product([x[-SUBLANES:] for x in parts], other_matrix)
            if parts[0].shape[0] == SUBLANES:
                return [jnp.where(foreign, b, a) for a, b in zip(mine, others)]
            return [
                jnp.concatenate([a[:own], jnp.where(foreign, b, a[own:])], axis=0) for a, b in zip(mine, others)
            ]

        return call

    products = (
        both_layers(lambda x, m: two_part_dot(x, m[...]), column_ref, other_column_ref),
        both_layers(lambda x, m: touching(plan, x, m), link_ref, other_link_ref),
    )
    collide_rows(plan, products, state_ref, post_ref, aux_ref, u_ref, force_ref, beyond, True)
    stream_rows(plan, state_ref, post_ref, ground, ceiling)

    def step(_, carry):
        collide_rows(plan, products, state_ref, post_ref, aux_ref, u_ref, force_ref, slice(0, rows))
        stream_rows(plan, state_ref, post_ref, ground, ceiling)
        return carry

    lax.fori_loop(1, SUBSTEPS, step, 0)

    first_half = lax.broadcasted_iota(jnp.int32, (halo, LANES), 1) < LANES // 2
    for t in range(plan.tiles):
        sets = [[state_ref[t * per + j, 0:own, lanes] for j in range(per)] for lanes in tile_lanes(plan)]
        for q, parts in enumerate(swap_groups(sets, group)):
            for s, part in enumerate(parts):
                low, high = part[:halo], part[halo:]
                if t == plan.tiles - 1:
                    pieces = [jnp.where(first_half, low, pltpu.roll(high, LANES // 2, 1))]
                else:
                    pieces = [low, high]
                for k, piece in enumerate(pieces):
                    start = (2 * t + k) * LANES
                    out_ref[q * per + s, :, start : start + LANES] = piece


def finish_kernel(plan, in_ref, pop_ref, vel_ref, stage, sems):
    whole = 19 * plan.group // LANES
    end = 19 * plan.group
    split = whole * LANES // 2
    holders = [plan.holder(q) for q in range(plan.sources)]
    moves = {
        plan.tiles - 1: (stage.at[end : end + 3 * plan.bins], vel_ref),
        whole // 2 - 1: (stage.at[:split], pop_ref.at[:split]),
        whole - 1: (stage.at[split:end], pop_ref.at[split:]),
    }
    copies = []
    for t in (whole, whole + 1, *range(whole)):
        pieces = []
        for holder in holders:
            start = 2 * t * LANES
            low = in_ref[holder, :, start : start + LANES]
            if t == plan.tiles - 1:
                high = pltpu.roll(low, LANES // 2, 1)
            else:
                high = in_ref[holder, :, start + LANES : start + 2 * LANES]
            pieces += [low, high]
        stage[t * LANES : (t + 1) * LANES, :] = jnp.concatenate(pieces, axis=0).T
        if t in moves:
            copies.append(pltpu.make_async_copy(*moves[t], sems.at[len(copies)]))
            copies[-1].start()
    for copy in copies:
        copy.wait()


def windows_body(plan, populations, grain_velocity, grain_volume, slots, contacts, bin_cell):
    group, bins, sources = plan.group, plan.bins, plan.sources
    rows, columns, own = plan.rows, plan.columns, plan.own
    f32, bf16, i32 = jnp.float32, jnp.bfloat16, jnp.int32
    half = sources // 2

    def call(kernel, shapes, inputs, scratch=(), where=(VMEM, VMEM), aliases=None):
        if where[0] is HBM:
            inputs = [pltpu.with_memory_space_constraint(x, pltpu.HBM) for x in inputs]
        shapes = [jax.ShapeDtypeStruct(shape, kind) for shape, kind in shapes]
        return pl.pallas_call(
            lambda *refs: kernel(plan, *refs),
            out_shape=shapes,
            in_specs=[where[0]] * len(inputs),
            out_specs=[where[1]] * len(shapes),
            scratch_shapes=list(scratch),
            input_output_aliases=aliases or {},
            compiler_params=pltpu.CompilerParams(vmem_limit_bytes=VMEM_LIMIT),
        )(*inputs)

    (outgoing,) = call(
        prepare_kernel,
        [((sources, own, plan.wide), f32)],
        (
            populations.reshape(19 * group, LANES),
            grain_velocity.reshape(3 * bins, LANES),
            grain_volume,
            slots,
            contacts,
            bin_cell.reshape(1, bins),
        ),
        (
            pltpu.VMEM((plan.width, LANES), f32),
            pltpu.VMEM((bins, LANES), i32),
            pltpu.VMEM((bins, bins), i32),
            pltpu.VMEM((1, bins), i32),
            pltpu.SemaphoreType.DMA((16,)),
        ),
        (HBM, VMEM),
    )
    layer_axes, every_axis = ("gx", "gy"), ("gx", "gy", "gz")
    incoming = lax.all_to_all(outgoing, layer_axes, split_axis=0, concat_axis=0, tiled=True)
    inner, outer = call(
        edges_kernel,
        [((half, SUBLANES, plan.width), f32), ((half, SUBLANES, plan.width + 2 * LANES), f32)],
        (incoming,),
    )
    inner = lax.ppermute(inner, every_axis, plan.swaps(0))
    outer = lax.ppermute(outer, every_axis, plan.swaps(1))
    carried = [
        ((plan.fields, rows, columns), f32),
        ((19, rows, columns), f32),
        ((2, rows, columns), f32),
    ]
    moments_and_forces = (pltpu.VMEM((5, rows, columns), f32), pltpu.VMEM((3, rows, columns), f32))
    *settled, column, link = call(
        settle_kernel,
        carried + [((columns, columns), bf16), ((columns, LANES), bf16)],
        (incoming,),
        moments_and_forces,
    )
    back, *_ = call(
        substeps_kernel,
        [((sources, plan.halo, plan.returned), f32)] + carried,
        (*settled, column, link, inner, outer),
        (
            *moments_and_forces,
            pltpu.VMEM((columns, columns), bf16),
            pltpu.VMEM((columns, LANES), bf16),
        ),
        aliases={0: 1, 1: 2, 2: 3},
    )
    result = lax.all_to_all(back, layer_axes, split_axis=0, concat_axis=0, tiled=True)
    fluid, velocity = call(
        finish_kernel,
        [((19 * group, LANES), f32), ((3 * bins, LANES), f32)],
        (result,),
        (pltpu.VMEM((plan.width, LANES), f32), pltpu.SemaphoreType.DMA((16,))),
        (VMEM, HBM),
    )
    return (fluid.reshape(populations.shape), velocity.reshape(grain_velocity.shape))


def body(populations, grain_velocity, grain_volume, slots, contacts, bin_cell):
    plan = Plan(
        lax.axis_size("gx"),
        lax.axis_size("gy"),
        lax.axis_size("gz"),
        populations,
        contacts,
        grain_velocity.shape[2],
    )
    arrays = (populations, grain_velocity, grain_volume, slots, contacts, bin_cell)
    if plan.fits() and contacts.shape[0] == contacts.shape[1]:
        return windows_body(plan, *arrays)
    return columns_body(*arrays)


def solution(mesh):
    placed = (
        P(None, "gx", "gy", "gz"),
        P(None, ("gx", "gy", "gz"), None),
        P(("gx", "gy", "gz"), None),
        P(("gx", "gy", "gz"), None),
        P(("gx", "gy", "gz"), None),
        P(("gx", "gy", "gz")),
    )
    return jax.shard_map(
        body,
        mesh=mesh,
        in_specs=placed,
        out_specs=(P(None, "gx", "gy", "gz"), P(None, ("gx", "gy", "gz"), None)),
        check_vma=False,
    )
```

```python
import jax
import jax.numpy as jnp
import numpy as np
from jax import lax
from jax.experimental import pallas as pl
from jax.experimental.pallas import tpu as pltpu
from jax.sharding import PartitionSpec as P

SUBSTEPS = 4


VELOCITIES = np.array(
    [
        [0, 0, 0],
        [1, 0, 0],
        [-1, 0, 0],
        [0, 1, 0],
        [0, -1, 0],
        [0, 0, 1],
        [0, 0, -1],
        [1, 1, 0],
        [-1, -1, 0],
        [1, -1, 0],
        [-1, 1, 0],
        [1, 0, 1],
        [-1, 0, -1],
        [1, 0, -1],
        [-1, 0, 1],
        [0, 1, 1],
        [0, -1, -1],
        [0, 1, -1],
        [0, -1, 1],
    ]
)
WEIGHTS = np.array([1.0 / 3.0] + [1.0 / 18.0] * 6 + [1.0 / 36.0] * 12)
OPPOSITE = [0, 2, 1, 4, 3, 6, 5, 8, 7, 10, 9, 12, 11, 14, 13, 16, 15, 18, 17]
relax_time = 0.8
contact_stiffness = 0.1
drag_factor = 2.0
gravity = 0.01


def passed_along(x, axis, by):
    length = lax.axis_size(axis)
    return lax.ppermute(x, axis, [(i, (i + by) % length) for i in range(length)])


def passed_along_2(value, axis, steps):
    count = lax.axis_size(axis)
    leading, last = (max(0, -steps), min(count, count - steps))
    return lax.ppermute(value, axis, [(source, source + steps) for source in range(leading, last)])


def moments(popul):
    density = jnp.sum(popul, axis=0)
    speed = []
    for axis in range(3):
        rising = np.array([i for i in range(19) if VELOCITIES[i, axis] == 1])
        falling = np.array([i for i in range(19) if VELOCITIES[i, axis] == -1])
        momentum = jnp.sum(popul[rising], axis=0) - jnp.sum(popul[falling], axis=0)
        speed.append(momentum / density)
    return (density, speed)


def grain_step(block, velocity, live, volume, links):
    grains = velocity.shape[2]
    bins = links.shape[1]
    groups = velocity.shape[1] // bins
    rate = drag_factor * volume * live
    drag = rate[None] * (block[:3] - velocity)
    moving = (velocity * live[None]).reshape(3, groups, bins, grains)
    pairs = links.reshape(groups, bins, bins)
    near = jnp.einsum("gkj,cgjs->cgks", pairs, moving, precision=lax.Precision.HIGHEST).reshape(
        3, -1, grains
    )
    count = jnp.einsum(
        "gkj,gjs->gks", pairs, live.reshape(groups, bins, grains), precision=lax.Precision.HIGHEST
    ).reshape(-1, grains)
    push = contact_stiffness * live[None] * (near - count[None] * velocity)
    fall = jnp.asarray([0.0, 0.0, gravity], jnp.float32).reshape(3, 1, 1) * live[None]
    updated = velocity + drag + push - fall
    forces = jnp.concatenate([-drag, (volume * live)[None]], axis=0)
    return (updated, forces)


def collide(popul, density, speed, field):
    scale = 1.0 / (1.0 + field[3])
    target = [scale * (speed[a] + relax_time * field[a] / density) for a in range(3)]
    square = target[0] * target[0] + target[1] * target[1] + target[2] * target[2]
    rows = []
    for i in range(19):
        along = jnp.zeros_like(density)
        for a in range(3):
            if VELOCITIES[i, a] != 0:
                along = along + float(VELOCITIES[i, a]) * target[a]
        equil = (
            float(WEIGHTS[i]) * density * (1.0 + 3.0 * along + 4.5 * along * along - 1.5 * square)
        )
        rows.append(popul[i] - (popul[i] - equil) / relax_time)
    return jnp.stack(rows)


def walls(moved, post):
    depth = post.shape[3]
    zpos = jnp.arange(depth)
    bottom = (zpos == 0) & (lax.axis_index("gz") == 0)
    top = (zpos == depth - 1) & (lax.axis_index("gz") == lax.axis_size("gz") - 1)
    rows = []
    for i in range(19):
        layer = moved[i]
        if VELOCITIES[i, 2] == 1:
            layer = jnp.where(bottom, post[OPPOSITE[i]], layer)
        elif VELOCITIES[i, 2] == -1:
            layer = jnp.where(top, post[OPPOSITE[i]], layer)
        rows.append(layer)
    return jnp.stack(rows)


def leaving(axis):
    rising = np.array([i for i in range(19) if VELOCITIES[i, axis] == 1])
    falling = np.array([i for i in range(19) if VELOCITIES[i, axis] == -1])
    return (rising, falling)


def stream(post):
    moved = post
    rising, falling = leaving(0)
    upper = moved[rising]
    lower = moved[falling]
    edge_up = passed_along(upper[:, -1:], "gx", 1)
    edge_down = passed_along(lower[:, :1], "gx", -1)
    moved = moved.at[rising].set(jnp.concatenate([edge_up, upper[:, :-1]], axis=1))
    moved = moved.at[falling].set(jnp.concatenate([lower[:, 1:], edge_down], axis=1))
    rising, falling = leaving(1)
    upper = moved[rising]
    lower = moved[falling]
    edge_up = passed_along(upper[:, :, -1:], "gy", 1)
    edge_down = passed_along(lower[:, :, :1], "gy", -1)
    moved = moved.at[rising].set(jnp.concatenate([edge_up, upper[:, :, :-1]], axis=2))
    moved = moved.at[falling].set(jnp.concatenate([lower[:, :, 1:], edge_down], axis=2))
    rising, falling = leaving(2)
    upper = moved[rising]
    lower = moved[falling]
    edge_up = passed_along_2(upper[:, :, :, -1:], "gz", 1)
    edge_down = passed_along_2(lower[:, :, :, :1], "gz", -1)
    moved = moved.at[rising].set(jnp.concatenate([edge_up, upper[:, :, :, :-1]], axis=3))
    moved = moved.at[falling].set(jnp.concatenate([lower[:, :, :, 1:], edge_down], axis=3))
    return walls(moved, post)


def carry_flow(outgoing):
    result = lax.all_to_all(outgoing, ("gx", "gy"), split_axis=1, concat_axis=1, tiled=True)
    return result


def carry_force(outgoing):
    result = lax.all_to_all(outgoing, ("gx", "gy"), split_axis=1, concat_axis=1, tiled=True)
    return result


def rank_within(source):
    count = source.shape[-1]
    before = jnp.arange(count)[None, :] < jnp.arange(count)[:, None]
    same = source[..., :, None] == source[..., None, :]
    return jnp.sum((same & before).astype(jnp.int32), axis=-1)


def columns_body(populations, grain_velocity, grain_volume, slots, contacts, bin_cell):
    n_gx = lax.axis_size("gx")
    n_gy = lax.axis_size("gy")
    n_gz = lax.axis_size("gz")
    sources = n_gx * n_gy
    bins = contacts.shape[1]
    grains = grain_velocity.shape[2]
    depth_x, depth_y, depth_z = (populations.shape[1], populations.shape[2], populations.shape[3])
    zblocks = depth_z // grains
    capacity = max(2, 4 * bins // sources)
    width_y = depth_y * n_gy
    column_blocks = depth_z * n_gz // grains

    def locate(cells):
        xcell = cells // (width_y * column_blocks)
        ycell = cells // column_blocks % width_y
        zblock = cells % column_blocks
        source = xcell // depth_x * n_gy + ycell // depth_y
        local = (xcell % depth_x * depth_y + ycell % depth_y) * zblocks + zblock % zblocks
        return (source, local)

    own_source, own_local = locate(bin_cell)
    own_row = own_source * capacity + rank_within(own_source)
    every = lax.all_gather(bin_cell, ("gx", "gy"), axis=0, tiled=True).reshape(sources, bins)
    all_source, all_local = locate(every)
    all_rank = rank_within(all_source)
    here = lax.axis_index("gx") * n_gy + lax.axis_index("gy")
    slot_ids = jnp.arange(capacity, dtype=jnp.int32)
    picked = (all_source == here)[:, None, :] & (all_rank[:, None, :] == slot_ids[None, :, None])
    send_column = jnp.sum(jnp.where(picked, all_local[:, None, :], 0), axis=2).reshape(-1)
    send_mask = jnp.any(picked, axis=2).reshape(-1).astype(jnp.float32)
    live = slots.astype(jnp.float32)
    links = contacts.astype(jnp.float32)
    fluid = populations
    velocity = grain_velocity
    for step in range(SUBSTEPS):
        density, speed = moments(fluid)
        flow = jnp.stack(speed + [density]).reshape(4, -1, grains)
        outgoing = jnp.take(flow, send_column, axis=1) * send_mask[None, :, None]
        incoming = carry_flow(outgoing)
        block = jnp.take(incoming, own_row, axis=1)
        velocity, forces = grain_step(block, velocity, live, grain_volume, links)
        back = jnp.zeros((4, sources * capacity, grains), jnp.float32).at[:, own_row].set(forces)
        returned = carry_force(back)
        field = jnp.zeros_like(flow).at[:, send_column].add(returned * send_mask[None, :, None])
        field = field.reshape(4, depth_x, depth_y, depth_z)
        post = collide(fluid, density, speed, field)
        fluid = stream(post)
    return (fluid, velocity)


LANES = 128
SUBLANES = 8
VMEM_LIMIT = 24 * 1024 * 1024
VMEM = pl.BlockSpec(memory_space=pltpu.VMEM)
HBM = pl.BlockSpec(memory_space=pltpu.HBM)
FIELD_V = (19, 20, 21)
FIELD_CELL = 22
FIELD_RATE = 23


class Plan:
    def __init__(self, n_gx, n_gy, n_gz, populations, contacts, grains):
        self.n_gx, self.n_gy, self.n_gz = n_gx, n_gy, n_gz
        self.dx, self.dy, self.depth = populations.shape[1:]
        self.grains = grains
        self.bins = contacts.shape[1]
        self.sources = n_gx * n_gy
        self.group = self.dx * self.dy
        self.halo = SUBSTEPS
        self.own = self.depth // self.sources
        self.rows = self.own + 2 * self.halo
        self.columns = self.sources * self.group
        self.per_tile = max(1, LANES // self.group)
        self.fields = 24
        self.tiles = self.fields // self.per_tile
        self.width = self.fields * self.group
        self.wide = (2 * self.tiles + 1) * LANES
        self.returned = (2 * self.tiles - 1) * LANES

    def fits(self):
        group = self.group
        return (
            self.sources % 2 == 0
            and self.depth == LANES
            and self.grains == LANES
            and self.own * self.sources == LANES
            and self.own == SUBLANES == 2 * self.halo
            and self.rows == 2 * SUBLANES
            and group == self.bins
            and group * group == SUBLANES * LANES
            and self.per_tile == self.n_gy
        )

    def along(self, window):
        gx, r = divmod(window, self.n_gy)
        return gx * self.n_gy + (self.n_gy - 1 - r if gx % 2 else r)

    def device(self, window):
        layer, local = divmod(window, self.sources)
        if layer % 2:
            local = self.sources - 1 - local
        return self.along(local) * self.n_gz + layer

    def swaps(self, start):
        count = self.n_gz * self.sources
        paired = []
        for a in range(start, count - 1, 2):
            paired += [(a, a + 1), (a + 1, a)]
        if start:
            paired += [(0, count - 1), (count - 1, 0)]
        return [(self.device(a), self.device(b)) for a, b in paired]

    def place(self):
        gx, gy, layer = (lax.axis_index(name) for name in ("gx", "gy", "gz"))
        local = gx * self.n_gy + jnp.where(lax.rem(gx, 2) == 1, self.n_gy - 1 - gy, gy)
        return jnp.where(lax.rem(layer, 2) == 1, self.sources - 1 - local, local), layer

    def holder(self, window):
        odd = lax.rem(lax.axis_index("gz"), 2) == 1
        return jnp.where(odd, self.along(self.sources - 1 - window), self.along(window))


def pick(group, parts):
    lane = lax.broadcasted_iota(jnp.int32, parts[0].shape, 1) // group
    step = 1
    while len(parts) > 1:
        odd = lane // step % 2 == 1
        parts = [jnp.where(odd, b, a) for a, b in zip(parts[::2], parts[1::2])]
        step *= 2
    return parts[0]


def turned_groups(parts, group):
    count = len(parts)
    turned = []
    for r in range(count):
        chosen = pick(group, [parts[(g + r) % count] for g in range(count)])
        turned.append(pltpu.roll(chosen, r * group, 1) if r else chosen)
    return turned


def swap_groups(sets, group):
    turned = [turned_groups(parts, group) for parts in sets]
    count = len(sets[0])
    return [[pick(group, [t[(g - j) % count] for g in range(count)]) for j in range(count)] for t in turned]


def prepare_kernel(plan, pop_ref, vel_ref, vol_ref, slot_ref, link_ref, cell_ref, out_ref,
                   pops, slots, links, cells, sems):
    group, bins, own, halo = plan.group, plan.bins, plan.own, plan.halo
    whole = 19 * group // LANES
    end = plan.width
    vel_start = 19 * group
    split = whole * LANES // 2
    moves = [
        (cell_ref, cells),
        (link_ref, links),
        (slot_ref, slots),
        (vol_ref, pops.at[end - bins : end]),
        (vel_ref, pops.at[vel_start : vel_start + 3 * bins]),
        (pop_ref.at[split:], pops.at[split:vel_start]),
        (pop_ref.at[:split], pops.at[:split]),
    ]
    copies = [pltpu.make_async_copy(a, b, sems.at[i]) for i, (a, b) in enumerate(moves)]
    for copy in copies:
        copy.start()
    for copy in copies:
        copy.wait()

    cell = cells[...]
    width_y = plan.dy * plan.n_gy
    xcell = lax.div(cell, width_y * plan.n_gz)
    ycell = lax.rem(lax.div(cell, plan.n_gz), width_y)
    source = lax.div(xcell, plan.dx) * plan.n_gy + lax.div(ycell, plan.dy)
    cell = source * group + lax.rem(xcell, plan.dx) * plan.dy + lax.rem(ycell, plan.dy)
    blank = jnp.zeros((1, bins), jnp.float32)
    cell = jnp.concatenate([blank, blank, cell.astype(jnp.float32), blank], axis=1)
    packed = jnp.concatenate(
        [links[g * SUBLANES : (g + 1) * SUBLANES, :].astype(jnp.float32) for g in range(bins // SUBLANES)],
        axis=1,
    )
    holders = [plan.holder(q) for q in range(plan.sources)]
    for q in range(plan.sources):
        part = q % 2 * halo
        out_ref[holders[q], :, 2 * plan.width :] = packed[part : part + halo, :]
    for t in range(plan.tiles):
        block = pops[t * LANES : (t + 1) * LANES, :]
        if t == plan.tiles - 1:
            rate = pops[end - bins : end, :] * slots[...].astype(jnp.float32)
            block = jnp.concatenate([block[: 2 * bins], rate, rate], axis=0)
        block = block.T
        if t == plan.tiles - 1:
            lane = lax.broadcasted_iota(jnp.int32, block.shape, 1) // bins
            block = jnp.where(lane == FIELD_CELL % plan.per_tile, cell, block)
        for q in range(plan.sources):
            for k in range(2):
                start, row = (2 * t + k) * LANES, q * own + k * halo
                out_ref[holders[q], :, start : start + LANES] = block[row : row + halo, :]


def half_tile(ref, s, t, k):
    start = (2 * t + k) * LANES
    return ref[s, :, start : start + LANES]


def edges_kernel(plan, in_ref, inner_ref, outer_ref):
    window, _ = plan.place()
    even = lax.rem(window, 2) == 0
    for s in range(plan.sources):
        for t in range(plan.tiles):
            lanes = slice(t * LANES, (t + 1) * LANES)
            low, high = half_tile(in_ref, s, t, 0), half_tile(in_ref, s, t, 1)
            inner_ref[s, :, lanes] = jnp.where(even, high, low)
            outer_ref[s, :, lanes] = jnp.where(even, low, high)
        inner_ref[s, :, plan.width :] = half_tile(in_ref, s, plan.tiles, 0)


def two_part_dot(parts, matrix):
    whole = jnp.concatenate(parts, axis=0)
    rest = whole - whole.astype(jnp.bfloat16).astype(jnp.float32)
    stacked = jnp.concatenate([whole, rest], axis=0).astype(jnp.bfloat16)
    out = lax.dot_general(
        stacked, matrix, (((1,), (1,)), ((), ())), preferred_element_type=jnp.float32
    )
    rows = parts[0].shape[0]
    half = rows * len(parts)
    return [
        out[i * rows : (i + 1) * rows] + out[half + i * rows : half + (i + 1) * rows]
        for i in range(len(parts))
    ]


def bins_on_columns(columns, cells):
    which = lax.broadcasted_iota(jnp.int32, (columns, columns), 0).astype(jnp.float32)
    return (which == cells).astype(jnp.float32).astype(jnp.bfloat16)


def contact_blocks(plan, packed, link_ref):
    group, per = plan.group, plan.per_tile
    lane = lax.broadcasted_iota(jnp.int32, (SUBLANES, LANES), 1) // group
    for q in range(0, plan.sources, per):
        turned = turned_groups([packed(s) for s in range(q, q + per)], group)
        for s in range(per):
            pieces = [jnp.where(lane == s, turned[(s - g) % per], 0.0) for g in range(per)]
            start = (q + s) * group
            link_ref[start : start + group, :] = jnp.concatenate(pieces, axis=0).astype(jnp.bfloat16)


def unpack(plan, tile_of, state_ref, rows):
    per = plan.per_tile
    for t in range(plan.tiles):
        sets = [[tile_of(s, t) for s in range(q, q + per)] for q in range(0, plan.sources, per)]
        for q, parts in enumerate(swap_groups(sets, plan.group)):
            for j, part in enumerate(parts):
                state_ref[t * per + j, rows, q * LANES : (q + 1) * LANES] = part


def touching(plan, parts, matrix):
    quads = plan.sources // plan.per_tile
    blocks = []
    for q in range(quads):
        at = slice(q * LANES, (q + 1) * LANES)
        blocks.append(two_part_dot([x[:, at] for x in parts], matrix[at, :]))
    return [jnp.concatenate([b[i] for b in blocks], axis=1) for i in range(len(parts))]


def tile_lanes(plan):
    return [slice(q * LANES, (q + 1) * LANES) for q in range(plan.sources // plan.per_tile)]


def on_bins(plan, fields, cells):
    tiles = tile_lanes(plan)
    cells = cells.astype(jnp.int32)
    lane, tile = lax.rem(cells, LANES), lax.div(cells, LANES)
    out = []
    for x in fields:
        pieces = []
        for to in tiles:
            found = None
            for q, at in enumerate(tiles):
                moved = jnp.take_along_axis(x[:, at], lane[:, to], axis=1, mode="promise_in_bounds")
                found = moved if found is None else jnp.where(tile[:, to] == q, moved, found)
            pieces.append(found)
        out.append(jnp.concatenate(pieces, axis=1))
    return out


def collide_rows(plan, to_columns, state_ref, post_ref, aux_ref, u_ref, force_ref, rows, begin=False):
    for lanes in tile_lanes(plan):
        popul = [state_ref[i, rows, lanes] for i in range(19)]
        density = popul[0]
        for i in range(1, 19):
            density = density + popul[i]
        inverse = 1.0 / density
        u_ref[3, rows, lanes] = density
        u_ref[4, rows, lanes] = inverse
        for a in range(3):
            rising = [popul[i] for i in range(19) if VELOCITIES[i, a] == 1]
            falling = [popul[i] for i in range(19) if VELOCITIES[i, a] == -1]
            u_ref[a, rows, lanes] = (sum(rising[1:], rising[0]) - sum(falling[1:], falling[0])) * inverse
    rate = state_ref[FIELD_RATE, rows]
    velocity = [state_ref[field, rows] for field in FIELD_V]
    speed = on_bins(plan, [u_ref[a, rows] for a in range(3)], state_ref[FIELD_CELL, rows])
    drags = [drag_factor * rate * (speed[a] - velocity[a]) for a in range(3)]
    if begin:
        *forces, solid = to_columns(drags + [rate])
        aux_ref[0, rows] = 1.0 / (1.0 + solid)
    else:
        forces = to_columns(drags)
    for a, force in enumerate(forces):
        force_ref[a, rows] = force
    keep, take = 1.0 - 1.0 / relax_time, 1.0 / relax_time
    for lanes in tile_lanes(plan):
        density, inverse = u_ref[3, rows, lanes], u_ref[4, rows, lanes]
        scale = aux_ref[0, rows, lanes]
        share = relax_time * inverse
        target = [scale * (u_ref[a, rows, lanes] - share * force_ref[a, rows, lanes]) for a in range(3)]
        square = target[0] * target[0] + target[1] * target[1] + target[2] * target[2]
        base = 1.0 - 1.5 * square
        triple = [3.0 * x for x in target]
        shares = {w: (take * float(w)) * density for w in sorted(set(WEIGHTS))}
        post_ref[0, rows, lanes] = keep * state_ref[0, rows, lanes] + shares[WEIGHTS[0]] * base
        for i in range(1, 19, 2):
            along = None
            for a in range(3):
                if VELOCITIES[i, a] != 0:
                    if along is None:
                        along = triple[a] if VELOCITIES[i, a] == 1 else -triple[a]
                    else:
                        along = along + triple[a] if VELOCITIES[i, a] == 1 else along - triple[a]
            level = base + 0.5 * (along * along)
            share_i = shares[WEIGHTS[i]]
            post_ref[i, rows, lanes] = keep * state_ref[i, rows, lanes] + share_i * (level + along)
            post_ref[i + 1, rows, lanes] = keep * state_ref[i + 1, rows, lanes] + share_i * (level - along)
    return drags


def move_grains(near, state_ref, aux_ref, rows, drags, begin=False):
    live = (state_ref[FIELD_RATE, rows] > 0.0).astype(jnp.float32)
    velocity = [state_ref[field, rows] for field in FIELD_V]
    moving = [velocity[a] * live for a in range(3)]
    if begin:
        *moving, count = near(moving + [live])
        aux_ref[1, rows] = count
    else:
        moving = near(moving)
        count = aux_ref[1, rows]
    for a in range(3):
        push = contact_stiffness * live * (moving[a] - count * velocity[a])
        updated = velocity[a] + drags[a] + push
        if a == 2:
            updated = updated - gravity * live
        state_ref[FIELD_V[a], rows] = updated


def stream_rows(plan, state_ref, post_ref):
    window, layer = plan.place()
    ground = (window == 0) & (layer == 0)
    ceiling = (window == plan.sources - 1) & (layer == plan.n_gz - 1)
    rows, group, dx, dy = plan.rows, plan.group, plan.dx, plan.dy
    lane = lax.broadcasted_iota(jnp.int32, (rows, LANES), 1)
    row = lax.broadcasted_iota(jnp.int32, (rows, LANES), 0)
    lane_y = lax.div(lane, group) * dy + lax.rem(lane, dy)
    lane_x = lax.rem(lax.div(lane, dy), dx)
    bottom, top = ground & (row == 0), ceiling & (row == plan.own - 1)
    tiles = tile_lanes(plan)
    for i in range(19):
        cx, cy, cz = (int(c) for c in VELOCITIES[i])
        moved = [post_ref[i, :, lanes] for lanes in tiles]
        if cx or cy:
            y = lax.rem(lane_y - cy + plan.n_gy * dy, plan.n_gy * dy)
            x = lax.rem(lane_x - cx + dx, dx)
            from_lane = lax.div(y, dy) * group + x * dy + lax.rem(y, dy)
            moved = [jnp.take_along_axis(x, from_lane, axis=1, mode="promise_in_bounds") for x in moved]
        if cx:
            edge = lane_x == (0 if cx == 1 else dx - 1)
            moved = [jnp.where(edge, moved[(q - cx) % len(tiles)], moved[q]) for q in range(len(tiles))]
        for x, lanes in zip(moved, tiles):
            if cz:
                x = pltpu.roll(x, cz % rows, 0)
                x = jnp.where(bottom if cz == 1 else top, post_ref[OPPOSITE[i], :, lanes], x)
            state_ref[i, :, lanes] = x


def settle_kernel(plan, in_ref, state_ref, post_ref, aux_ref, column_ref, u_ref, force_ref):
    own = slice(0, plan.own)

    def own_tile(s, t):
        return jnp.concatenate([half_tile(in_ref, s, t, 0), half_tile(in_ref, s, t, 1)], axis=0)

    unpack(plan, own_tile, state_ref, own)
    column_ref[...] = bins_on_columns(plan.columns, state_ref[FIELD_CELL, 0:1, :])
    drags = collide_rows(
        plan,
        lambda parts: two_part_dot(parts, column_ref[...]),
        state_ref, post_ref, aux_ref, u_ref, force_ref, own, True,
    )
    for a in range(3):
        aux_ref[2 + a, own] = drags[a]


def contact_kernel(plan, in_ref, inner_ref, settled_ref, fixed_ref, state_ref, aux_ref, link_ref, packed_ref):
    window, _ = plan.place()
    even = lax.rem(window, 2) == 0
    own = slice(0, plan.own)

    def packed(s):
        mine, sibling = half_tile(in_ref, s, plan.tiles, 0), inner_ref[s, :, plan.width :]
        return jnp.concatenate([jnp.where(even, mine, sibling), jnp.where(even, sibling, mine)], axis=0)

    for s in range(plan.sources):
        packed_ref[s] = packed(s)
    contact_blocks(plan, lambda s: packed_ref[s], link_ref)
    drags = [aux_ref[2 + a, own] for a in range(3)]
    move_grains(lambda parts: touching(plan, parts, link_ref), state_ref, aux_ref, own, drags, True)


def both_layers(plan, product, own_matrix, other_matrix):
    window, _ = plan.place()
    halo_row = lax.broadcasted_iota(jnp.int32, (SUBLANES, plan.columns), 0)
    last, first = window == plan.sources - 1, window == 0
    foreign = (last & (halo_row < plan.halo)) | (first & (halo_row >= plan.halo))
    own = plan.own

    def call(parts):
        mine = product(parts, own_matrix)
        others = product([x[-SUBLANES:] for x in parts], other_matrix)
        if parts[0].shape[0] == SUBLANES:
            return [jnp.where(foreign, b, a) for a, b in zip(mine, others)]
        return [jnp.concatenate([a[:own], jnp.where(foreign, b, a[own:])], axis=0) for a, b in zip(mine, others)]

    return call


def columns_of(plan, column_ref, other_column_ref):
    return both_layers(plan, lambda x, m: two_part_dot(x, m[...]), column_ref, other_column_ref)


def halo_kernel(plan, settled_ref, collided_ref, fixed_ref, column_ref, inner_ref, outer_ref,
                state_ref, post_ref, aux_ref, other_column_ref, u_ref, force_ref):
    rows, own = plan.rows, plan.own
    window, _ = plan.place()
    even = lax.rem(window, 2) == 0
    beyond = slice(own, rows)

    def halo_tile(s, t):
        at = slice(t * LANES, (t + 1) * LANES)
        inner, outer = inner_ref[s, :, at], outer_ref[s, :, at]
        return jnp.concatenate([jnp.where(even, inner, outer), jnp.where(even, outer, inner)], axis=0)

    unpack(plan, halo_tile, state_ref, beyond)
    other_cells = jnp.where(window == 0, state_ref[FIELD_CELL, rows - 1 : rows, :], state_ref[FIELD_CELL, own : own + 1, :])
    other_column_ref[...] = bins_on_columns(plan.columns, other_cells)
    to_columns = columns_of(plan, column_ref, other_column_ref)
    drags = collide_rows(plan, to_columns, state_ref, post_ref, aux_ref, u_ref, force_ref, beyond, True)
    for a in range(3):
        aux_ref[2 + a, beyond] = drags[a]
    stream_rows(plan, state_ref, post_ref)


def substeps_kernel(plan, settled_ref, fixed_ref, column_ref, other_column_ref, link_ref, packed_ref,
                    out_ref, state_ref, aux_ref, post_ref, u_ref, force_ref, other_link_ref):
    rows, own, halo, group, per = plan.rows, plan.own, plan.halo, plan.group, plan.per_tile
    beyond = slice(own, rows)
    contact_blocks(plan, lambda s: packed_ref[s], other_link_ref)
    to_columns = columns_of(plan, column_ref, other_column_ref)
    near = both_layers(plan, lambda x, m: touching(plan, x, m), link_ref, other_link_ref)
    move_grains(near, state_ref, aux_ref, beyond, [aux_ref[2 + a, beyond] for a in range(3)], True)
    refs = (state_ref, post_ref, aux_ref, u_ref, force_ref)

    def step(_, carry):
        drags = collide_rows(plan, to_columns, *refs, slice(0, rows))
        move_grains(near, state_ref, aux_ref, slice(0, rows), drags)
        stream_rows(plan, state_ref, post_ref)
        return carry

    lax.fori_loop(1, SUBSTEPS, step, 0)

    first_half = lax.broadcasted_iota(jnp.int32, (halo, LANES), 1) < LANES // 2
    for t in range(plan.tiles):
        sets = [[state_ref[t * per + j, 0:own, lanes] for j in range(per)] for lanes in tile_lanes(plan)]
        for q, parts in enumerate(swap_groups(sets, group)):
            for s, part in enumerate(parts):
                low, high = part[:halo], part[halo:]
                if t == plan.tiles - 1:
                    pieces = [jnp.where(first_half, low, pltpu.roll(high, LANES // 2, 1))]
                else:
                    pieces = [low, high]
                for k, piece in enumerate(pieces):
                    start = (2 * t + k) * LANES
                    out_ref[q * per + s, :, start : start + LANES] = piece


def finish_kernel(plan, in_ref, pop_ref, vel_ref, stage, sems):
    whole = 19 * plan.group // LANES
    end = 19 * plan.group
    split = whole * LANES // 2
    holders = [plan.holder(q) for q in range(plan.sources)]
    moves = {
        plan.tiles - 1: (stage.at[end : end + 3 * plan.bins], vel_ref),
        whole // 2 - 1: (stage.at[:split], pop_ref.at[:split]),
        whole - 1: (stage.at[split:end], pop_ref.at[split:]),
    }
    copies = []
    for t in (whole, whole + 1, *range(whole)):
        pieces = []
        for holder in holders:
            start = 2 * t * LANES
            low = in_ref[holder, :, start : start + LANES]
            if t == plan.tiles - 1:
                high = pltpu.roll(low, LANES // 2, 1)
            else:
                high = in_ref[holder, :, start + LANES : start + 2 * LANES]
            pieces += [low, high]
        stage[t * LANES : (t + 1) * LANES, :] = jnp.concatenate(pieces, axis=0).T
        if t in moves:
            copies.append(pltpu.make_async_copy(*moves[t], sems.at[len(copies)]))
            copies[-1].start()
    for copy in copies:
        copy.wait()


def windows_body(plan, populations, grain_velocity, grain_volume, slots, contacts, bin_cell):
    group, bins, sources = plan.group, plan.bins, plan.sources
    rows, columns, own = plan.rows, plan.columns, plan.own
    f32, bf16, i32 = jnp.float32, jnp.bfloat16, jnp.int32
    halo = plan.halo

    def call(kernel, shapes, inputs, scratch=(), where=(VMEM, VMEM), aliases=None):
        if where[0] is HBM:
            inputs = [pltpu.with_memory_space_constraint(x, pltpu.HBM) for x in inputs]
        shapes = [jax.ShapeDtypeStruct(shape, kind) for shape, kind in shapes]
        return pl.pallas_call(
            lambda *refs: kernel(plan, *refs),
            out_shape=shapes,
            in_specs=[where[0]] * len(inputs),
            out_specs=[where[1]] * len(shapes),
            scratch_shapes=list(scratch),
            input_output_aliases=aliases or {},
            compiler_params=pltpu.CompilerParams(vmem_limit_bytes=VMEM_LIMIT),
        )(*inputs)

    (outgoing,) = call(
        prepare_kernel,
        [((sources, halo, plan.wide), f32)],
        (
            populations.reshape(19 * group, LANES),
            grain_velocity.reshape(3 * bins, LANES),
            grain_volume,
            slots,
            contacts,
            bin_cell.reshape(1, bins),
        ),
        (
            pltpu.VMEM((plan.width, LANES), f32),
            pltpu.VMEM((bins, LANES), i32),
            pltpu.VMEM((bins, bins), i32),
            pltpu.VMEM((1, bins), i32),
            pltpu.SemaphoreType.DMA((16,)),
        ),
        (HBM, VMEM),
    )
    layer_axes, every_axis = ("gx", "gy"), ("gx", "gy", "gz")
    incoming = lax.all_to_all(outgoing, layer_axes, split_axis=0, concat_axis=0, tiled=True)
    inner, outer = call(
        edges_kernel,
        [((sources, halo, plan.width + LANES), f32), ((sources, halo, plan.width), f32)],
        (incoming,),
    )
    inner = lax.ppermute(inner, every_axis, plan.swaps(0))
    outer = lax.ppermute(outer, every_axis, plan.swaps(1))
    carried = [
        ((plan.fields, rows, columns), f32),
        ((19, rows, columns), f32),
        ((5, rows, columns), f32),
    ]
    moments_and_forces = (pltpu.VMEM((5, rows, columns), f32), pltpu.VMEM((3, rows, columns), f32))
    state, post, aux, column = call(
        settle_kernel,
        carried + [((columns, columns), bf16)],
        (incoming,),
        moments_and_forces,
    )
    state, aux, link, packed = call(
        contact_kernel,
        [carried[0], carried[2], ((columns, LANES), bf16), ((sources, SUBLANES, LANES), f32)],
        (incoming, inner, state, aux),
        aliases={2: 0, 3: 1},
    )
    packed = lax.ppermute(packed, every_axis, plan.swaps(1))
    state, _, aux, other_column = call(
        halo_kernel,
        carried + [((columns, columns), bf16)],
        (state, post, aux, column, inner, outer),
        moments_and_forces,
        aliases={0: 0, 1: 1, 2: 2},
    )
    back, *_ = call(
        substeps_kernel,
        [((sources, halo, plan.returned), f32), carried[0], carried[2]],
        (state, aux, column, other_column, link, packed),
        (
            pltpu.VMEM((19, rows, columns), f32),
            *moments_and_forces,
            pltpu.VMEM((columns, LANES), bf16),
        ),
        aliases={0: 1, 1: 2},
    )
    result = lax.all_to_all(back, layer_axes, split_axis=0, concat_axis=0, tiled=True)
    fluid, velocity = call(
        finish_kernel,
        [((19 * group, LANES), f32), ((3 * bins, LANES), f32)],
        (result,),
        (pltpu.VMEM((plan.width, LANES), f32), pltpu.SemaphoreType.DMA((16,))),
        (VMEM, HBM),
    )
    return (fluid.reshape(populations.shape), velocity.reshape(grain_velocity.shape))


def body(populations, grain_velocity, grain_volume, slots, contacts, bin_cell):
    plan = Plan(
        lax.axis_size("gx"),
        lax.axis_size("gy"),
        lax.axis_size("gz"),
        populations,
        contacts,
        grain_velocity.shape[2],
    )
    arrays = (populations, grain_velocity, grain_volume, slots, contacts, bin_cell)
    if plan.fits() and contacts.shape[0] == contacts.shape[1]:
        return windows_body(plan, *arrays)
    return columns_body(*arrays)


def solution(mesh):
    placed = (
        P(None, "gx", "gy", "gz"),
        P(None, ("gx", "gy", "gz"), None),
        P(("gx", "gy", "gz"), None),
        P(("gx", "gy", "gz"), None),
        P(("gx", "gy", "gz"), None),
        P(("gx", "gy", "gz")),
    )
    return jax.shard_map(
        body,
        mesh=mesh,
        in_specs=placed,
        out_specs=(P(None, "gx", "gy", "gz"), P(None, ("gx", "gy", "gz"), None)),
        check_vma=False,
    )
```

```python
import functools
import jax
import jax.numpy as jnp
import numpy as np
from jax import lax
from jax.experimental import pallas as pl
from jax.experimental.pallas import tpu as pltpu
from jax.sharding import PartitionSpec as P

SUBSTEPS = 4


VELOCITIES = np.array(
    [
        [0, 0, 0],
        [1, 0, 0],
        [-1, 0, 0],
        [0, 1, 0],
        [0, -1, 0],
        [0, 0, 1],
        [0, 0, -1],
        [1, 1, 0],
        [-1, -1, 0],
        [1, -1, 0],
        [-1, 1, 0],
        [1, 0, 1],
        [-1, 0, -1],
        [1, 0, -1],
        [-1, 0, 1],
        [0, 1, 1],
        [0, -1, -1],
        [0, 1, -1],
        [0, -1, 1],
    ]
)
WEIGHTS = np.array([1.0 / 3.0] + [1.0 / 18.0] * 6 + [1.0 / 36.0] * 12)
OPPOSITE = [0, 2, 1, 4, 3, 6, 5, 8, 7, 10, 9, 12, 11, 14, 13, 16, 15, 18, 17]
relax_time = 0.8
contact_stiffness = 0.1
drag_factor = 2.0
gravity = 0.01


def passed_along(x, axis, by):
    length = lax.axis_size(axis)
    return lax.ppermute(x, axis, [(i, (i + by) % length) for i in range(length)])


def passed_along_2(value, axis, steps):
    count = lax.axis_size(axis)
    leading, last = (max(0, -steps), min(count, count - steps))
    return lax.ppermute(value, axis, [(source, source + steps) for source in range(leading, last)])


def moments(popul):
    density = jnp.sum(popul, axis=0)
    speed = []
    for axis in range(3):
        rising = np.array([i for i in range(19) if VELOCITIES[i, axis] == 1])
        falling = np.array([i for i in range(19) if VELOCITIES[i, axis] == -1])
        momentum = jnp.sum(popul[rising], axis=0) - jnp.sum(popul[falling], axis=0)
        speed.append(momentum / density)
    return (density, speed)


def grain_step(block, velocity, live, volume, links):
    grains = velocity.shape[2]
    bins = links.shape[1]
    groups = velocity.shape[1] // bins
    rate = drag_factor * volume * live
    drag = rate[None] * (block[:3] - velocity)
    moving = (velocity * live[None]).reshape(3, groups, bins, grains)
    pairs = links.reshape(groups, bins, bins)
    near = jnp.einsum("gkj,cgjs->cgks", pairs, moving, precision=lax.Precision.HIGHEST).reshape(
        3, -1, grains
    )
    count = jnp.einsum(
        "gkj,gjs->gks", pairs, live.reshape(groups, bins, grains), precision=lax.Precision.HIGHEST
    ).reshape(-1, grains)
    push = contact_stiffness * live[None] * (near - count[None] * velocity)
    fall = jnp.asarray([0.0, 0.0, gravity], jnp.float32).reshape(3, 1, 1) * live[None]
    updated = velocity + drag + push - fall
    forces = jnp.concatenate([-drag, (volume * live)[None]], axis=0)
    return (updated, forces)


def collide(popul, density, speed, field):
    scale = 1.0 / (1.0 + field[3])
    target = [scale * (speed[a] + relax_time * field[a] / density) for a in range(3)]
    square = target[0] * target[0] + target[1] * target[1] + target[2] * target[2]
    rows = []
    for i in range(19):
        along = jnp.zeros_like(density)
        for a in range(3):
            if VELOCITIES[i, a] != 0:
                along = along + float(VELOCITIES[i, a]) * target[a]
        equil = (
            float(WEIGHTS[i]) * density * (1.0 + 3.0 * along + 4.5 * along * along - 1.5 * square)
        )
        rows.append(popul[i] - (popul[i] - equil) / relax_time)
    return jnp.stack(rows)


def walls(moved, post):
    depth = post.shape[3]
    zpos = jnp.arange(depth)
    bottom = (zpos == 0) & (lax.axis_index("gz") == 0)
    top = (zpos == depth - 1) & (lax.axis_index("gz") == lax.axis_size("gz") - 1)
    rows = []
    for i in range(19):
        layer = moved[i]
        if VELOCITIES[i, 2] == 1:
            layer = jnp.where(bottom, post[OPPOSITE[i]], layer)
        elif VELOCITIES[i, 2] == -1:
            layer = jnp.where(top, post[OPPOSITE[i]], layer)
        rows.append(layer)
    return jnp.stack(rows)


def leaving(axis):
    rising = np.array([i for i in range(19) if VELOCITIES[i, axis] == 1])
    falling = np.array([i for i in range(19) if VELOCITIES[i, axis] == -1])
    return (rising, falling)


def stream(post):
    moved = post
    rising, falling = leaving(0)
    upper = moved[rising]
    lower = moved[falling]
    edge_up = passed_along(upper[:, -1:], "gx", 1)
    edge_down = passed_along(lower[:, :1], "gx", -1)
    moved = moved.at[rising].set(jnp.concatenate([edge_up, upper[:, :-1]], axis=1))
    moved = moved.at[falling].set(jnp.concatenate([lower[:, 1:], edge_down], axis=1))
    rising, falling = leaving(1)
    upper = moved[rising]
    lower = moved[falling]
    edge_up = passed_along(upper[:, :, -1:], "gy", 1)
    edge_down = passed_along(lower[:, :, :1], "gy", -1)
    moved = moved.at[rising].set(jnp.concatenate([edge_up, upper[:, :, :-1]], axis=2))
    moved = moved.at[falling].set(jnp.concatenate([lower[:, :, 1:], edge_down], axis=2))
    rising, falling = leaving(2)
    upper = moved[rising]
    lower = moved[falling]
    edge_up = passed_along_2(upper[:, :, :, -1:], "gz", 1)
    edge_down = passed_along_2(lower[:, :, :, :1], "gz", -1)
    moved = moved.at[rising].set(jnp.concatenate([edge_up, upper[:, :, :, :-1]], axis=3))
    moved = moved.at[falling].set(jnp.concatenate([lower[:, :, :, 1:], edge_down], axis=3))
    return walls(moved, post)


def carry_flow(outgoing):
    result = lax.all_to_all(outgoing, ("gx", "gy"), split_axis=1, concat_axis=1, tiled=True)
    return result


def carry_force(outgoing):
    result = lax.all_to_all(outgoing, ("gx", "gy"), split_axis=1, concat_axis=1, tiled=True)
    return result


def rank_within(source):
    count = source.shape[-1]
    before = jnp.arange(count)[None, :] < jnp.arange(count)[:, None]
    same = source[..., :, None] == source[..., None, :]
    return jnp.sum((same & before).astype(jnp.int32), axis=-1)


def columns_body(populations, grain_velocity, grain_volume, slots, contacts, bin_cell):
    n_gx = lax.axis_size("gx")
    n_gy = lax.axis_size("gy")
    n_gz = lax.axis_size("gz")
    sources = n_gx * n_gy
    bins = contacts.shape[1]
    grains = grain_velocity.shape[2]
    depth_x, depth_y, depth_z = (populations.shape[1], populations.shape[2], populations.shape[3])
    zblocks = depth_z // grains
    capacity = max(2, 4 * bins // sources)
    width_y = depth_y * n_gy
    column_blocks = depth_z * n_gz // grains

    def locate(cells):
        xcell = cells // (width_y * column_blocks)
        ycell = cells // column_blocks % width_y
        zblock = cells % column_blocks
        source = xcell // depth_x * n_gy + ycell // depth_y
        local = (xcell % depth_x * depth_y + ycell % depth_y) * zblocks + zblock % zblocks
        return (source, local)

    own_source, own_local = locate(bin_cell)
    own_row = own_source * capacity + rank_within(own_source)
    every = lax.all_gather(bin_cell, ("gx", "gy"), axis=0, tiled=True).reshape(sources, bins)
    all_source, all_local = locate(every)
    all_rank = rank_within(all_source)
    here = lax.axis_index("gx") * n_gy + lax.axis_index("gy")
    slot_ids = jnp.arange(capacity, dtype=jnp.int32)
    picked = (all_source == here)[:, None, :] & (all_rank[:, None, :] == slot_ids[None, :, None])
    send_column = jnp.sum(jnp.where(picked, all_local[:, None, :], 0), axis=2).reshape(-1)
    send_mask = jnp.any(picked, axis=2).reshape(-1).astype(jnp.float32)
    live = slots.astype(jnp.float32)
    links = contacts.astype(jnp.float32)
    fluid = populations
    velocity = grain_velocity
    for step in range(SUBSTEPS):
        density, speed = moments(fluid)
        flow = jnp.stack(speed + [density]).reshape(4, -1, grains)
        outgoing = jnp.take(flow, send_column, axis=1) * send_mask[None, :, None]
        incoming = carry_flow(outgoing)
        block = jnp.take(incoming, own_row, axis=1)
        velocity, forces = grain_step(block, velocity, live, grain_volume, links)
        back = jnp.zeros((4, sources * capacity, grains), jnp.float32).at[:, own_row].set(forces)
        returned = carry_force(back)
        field = jnp.zeros_like(flow).at[:, send_column].add(returned * send_mask[None, :, None])
        field = field.reshape(4, depth_x, depth_y, depth_z)
        post = collide(fluid, density, speed, field)
        fluid = stream(post)
    return (fluid, velocity)


LANES = 128
SUBLANES = 8
VMEM_LIMIT = 24 * 1024 * 1024
VMEM = pl.BlockSpec(memory_space=pltpu.VMEM)
HBM = pl.BlockSpec(memory_space=pltpu.HBM)
FIELD_V = (19, 20, 21)
FIELD_CELL = 22
FIELD_RATE = 23


class Plan:
    def __init__(self, n_gx, n_gy, n_gz, populations, contacts, grains):
        self.n_gx, self.n_gy, self.n_gz = n_gx, n_gy, n_gz
        self.dx, self.dy, self.depth = populations.shape[1:]
        self.grains = grains
        self.bins = contacts.shape[1]
        self.sources = n_gx * n_gy
        self.group = self.dx * self.dy
        self.halo = SUBSTEPS
        self.own = self.depth // self.sources
        self.rows = self.own + 2 * self.halo
        self.columns = self.sources * self.group
        self.per_tile = max(1, LANES // self.group)
        self.fields = 24
        self.tiles = self.fields // self.per_tile
        self.width = self.fields * self.group
        self.wide = (2 * self.tiles + 1) * LANES
        self.returned = (2 * self.tiles - 1) * LANES

    def fits(self):
        group = self.group
        return (
            self.sources % 2 == 0
            and self.depth == LANES
            and self.grains == LANES
            and self.own * self.sources == LANES
            and self.own == SUBLANES == 2 * self.halo
            and self.rows == 2 * SUBLANES
            and group == self.bins
            and group * group == SUBLANES * LANES
            and self.per_tile == self.n_gy
        )

    def along(self, window):
        gx, r = divmod(window, self.n_gy)
        return gx * self.n_gy + (self.n_gy - 1 - r if gx % 2 else r)

    def device(self, window):
        layer, local = divmod(window, self.sources)
        if layer % 2:
            local = self.sources - 1 - local
        return self.along(local) * self.n_gz + layer

    def swaps(self, start):
        count = self.n_gz * self.sources
        paired = []
        for a in range(start, count - 1, 2):
            paired += [(a, a + 1), (a + 1, a)]
        if start:
            paired += [(0, count - 1), (count - 1, 0)]
        return [(self.device(a), self.device(b)) for a, b in paired]

    def place(self):
        gx, gy, layer = (lax.axis_index(name) for name in ("gx", "gy", "gz"))
        local = gx * self.n_gy + jnp.where(lax.rem(gx, 2) == 1, self.n_gy - 1 - gy, gy)
        return jnp.where(lax.rem(layer, 2) == 1, self.sources - 1 - local, local), layer

    def holder(self, window):
        odd = lax.rem(lax.axis_index("gz"), 2) == 1
        return jnp.where(odd, self.along(self.sources - 1 - window), self.along(window))


def pick(group, parts):
    lane = lax.broadcasted_iota(jnp.int32, parts[0].shape, 1) // group
    step = 1
    while len(parts) > 1:
        odd = lane // step % 2 == 1
        parts = [jnp.where(odd, b, a) for a, b in zip(parts[::2], parts[1::2])]
        step *= 2
    return parts[0]


def turned_groups(parts, group):
    count = len(parts)
    turned = []
    for r in range(count):
        chosen = pick(group, [parts[(g + r) % count] for g in range(count)])
        turned.append(pltpu.roll(chosen, r * group, 1) if r else chosen)
    return turned


def swap_groups(sets, group):
    turned = [turned_groups(parts, group) for parts in sets]
    count = len(sets[0])
    return [[pick(group, [t[(g - j) % count] for g in range(count)]) for j in range(count)] for t in turned]


def prepare_kernel(plan, pop_ref, vel_ref, vol_ref, slot_ref, link_ref, cell_ref, out_ref,
                   pops, slots, links, cells, sems):
    group, bins, own, halo = plan.group, plan.bins, plan.own, plan.halo
    whole = 19 * group // LANES
    end = plan.width
    vel_start = 19 * group
    split = whole * LANES // 2
    moves = [
        (cell_ref, cells),
        (link_ref, links),
        (slot_ref, slots),
        (vol_ref, pops.at[end - bins : end]),
        (vel_ref, pops.at[vel_start : vel_start + 3 * bins]),
        (pop_ref.at[split:], pops.at[split:vel_start]),
        (pop_ref.at[:split], pops.at[:split]),
    ]
    copies = [pltpu.make_async_copy(a, b, sems.at[i]) for i, (a, b) in enumerate(moves)]
    for copy in copies:
        copy.start()
    for copy in copies:
        copy.wait()

    cell = cells[...]
    width_y = plan.dy * plan.n_gy
    xcell = lax.div(cell, width_y * plan.n_gz)
    ycell = lax.rem(lax.div(cell, plan.n_gz), width_y)
    source = lax.div(xcell, plan.dx) * plan.n_gy + lax.div(ycell, plan.dy)
    cell = source * group + lax.rem(xcell, plan.dx) * plan.dy + lax.rem(ycell, plan.dy)
    blank = jnp.zeros((1, bins), jnp.float32)
    cell = jnp.concatenate([blank, blank, cell.astype(jnp.float32), blank], axis=1)
    packed = jnp.concatenate(
        [links[g * SUBLANES : (g + 1) * SUBLANES, :].astype(jnp.float32) for g in range(bins // SUBLANES)],
        axis=1,
    )
    holders = [plan.holder(q) for q in range(plan.sources)]
    for q in range(plan.sources):
        part = q % 2 * halo
        out_ref[holders[q], :, 2 * plan.width :] = packed[part : part + halo, :]
    for t in range(plan.tiles):
        block = pops[t * LANES : (t + 1) * LANES, :]
        if t == plan.tiles - 1:
            rate = pops[end - bins : end, :] * slots[...].astype(jnp.float32)
            block = jnp.concatenate([block[: 2 * bins], rate, rate], axis=0)
        block = block.T
        if t == plan.tiles - 1:
            lane = lax.broadcasted_iota(jnp.int32, block.shape, 1) // bins
            block = jnp.where(lane == FIELD_CELL % plan.per_tile, cell, block)
        for q in range(plan.sources):
            for k in range(2):
                start, row = (2 * t + k) * LANES, q * own + k * halo
                out_ref[holders[q], :, start : start + LANES] = block[row : row + halo, :]


def half_tile(ref, s, t, k):
    start = (2 * t + k) * LANES
    return ref[s, :, start : start + LANES]


def edges_kernel(plan, in_ref, inner_ref, outer_ref):
    window, _ = plan.place()
    even = lax.rem(window, 2) == 0
    for s in range(plan.sources):
        for t in range(plan.tiles):
            lanes = slice(t * LANES, (t + 1) * LANES)
            low, high = half_tile(in_ref, s, t, 0), half_tile(in_ref, s, t, 1)
            inner_ref[s, :, lanes] = jnp.where(even, high, low)
            outer_ref[s, :, lanes] = jnp.where(even, low, high)
        inner_ref[s, :, plan.width :] = half_tile(in_ref, s, plan.tiles, 0)


def two_part_dot(parts, matrix):
    whole = jnp.concatenate(parts, axis=0)
    rest = whole - whole.astype(jnp.bfloat16).astype(jnp.float32)
    stacked = jnp.concatenate([whole, rest], axis=0).astype(jnp.bfloat16)
    out = lax.dot_general(
        stacked, matrix, (((1,), (1,)), ((), ())), preferred_element_type=jnp.float32
    )
    rows = parts[0].shape[0]
    half = rows * len(parts)
    return [
        out[i * rows : (i + 1) * rows] + out[half + i * rows : half + (i + 1) * rows]
        for i in range(len(parts))
    ]


def bins_on_columns(columns, cells):
    which = lax.broadcasted_iota(jnp.int32, (columns, columns), 0).astype(jnp.float32)
    return (which == cells).astype(jnp.float32).astype(jnp.bfloat16)


def contact_blocks(plan, packed, link_ref):
    group, per = plan.group, plan.per_tile
    lane = lax.broadcasted_iota(jnp.int32, (SUBLANES, LANES), 1) // group
    for q in range(0, plan.sources, per):
        turned = turned_groups([packed(s) for s in range(q, q + per)], group)
        for s in range(per):
            pieces = [jnp.where(lane == s, turned[(s - g) % per], 0.0) for g in range(per)]
            start = (q + s) * group
            link_ref[start : start + group, :] = jnp.concatenate(pieces, axis=0).astype(jnp.bfloat16)


def unpack(plan, tile_of, state_ref, rows):
    per = plan.per_tile
    for t in range(plan.tiles):
        sets = [[tile_of(s, t) for s in range(q, q + per)] for q in range(0, plan.sources, per)]
        for q, parts in enumerate(swap_groups(sets, plan.group)):
            for j, part in enumerate(parts):
                state_ref[t * per + j, rows, q * LANES : (q + 1) * LANES] = part


def touching(plan, parts, matrix):
    quads = plan.sources // plan.per_tile
    blocks = []
    for q in range(quads):
        at = slice(q * LANES, (q + 1) * LANES)
        blocks.append(two_part_dot([x[:, at] for x in parts], matrix[at, :]))
    return [jnp.concatenate([b[i] for b in blocks], axis=1) for i in range(len(parts))]


def tile_lanes(plan):
    return [slice(q * LANES, (q + 1) * LANES) for q in range(plan.sources // plan.per_tile)]


def on_bins(plan, fields, cells):
    tiles = tile_lanes(plan)
    cells = cells.astype(jnp.int32)
    lane, tile = lax.rem(cells, LANES), lax.div(cells, LANES)
    out = []
    for x in fields:
        pieces = []
        for to in tiles:
            found = None
            for q, at in enumerate(tiles):
                moved = jnp.take_along_axis(x[:, at], lane[:, to], axis=1, mode="promise_in_bounds")
                found = moved if found is None else jnp.where(tile[:, to] == q, moved, found)
            pieces.append(found)
        out.append(jnp.concatenate(pieces, axis=1))
    return out


def collide_rows(plan, to_columns, state_ref, post_ref, aux_ref, u_ref, force_ref, rows, begin=False):
    for lanes in tile_lanes(plan):
        popul = [state_ref[i, rows, lanes] for i in range(19)]
        density = popul[0]
        for i in range(1, 19):
            density = density + popul[i]
        inverse = 1.0 / density
        u_ref[3, rows, lanes] = density
        u_ref[4, rows, lanes] = inverse
        for a in range(3):
            rising = [popul[i] for i in range(19) if VELOCITIES[i, a] == 1]
            falling = [popul[i] for i in range(19) if VELOCITIES[i, a] == -1]
            u_ref[a, rows, lanes] = (sum(rising[1:], rising[0]) - sum(falling[1:], falling[0])) * inverse
    rate = state_ref[FIELD_RATE, rows]
    velocity = [state_ref[field, rows] for field in FIELD_V]
    speed = on_bins(plan, [u_ref[a, rows] for a in range(3)], state_ref[FIELD_CELL, rows])
    drags = [drag_factor * rate * (speed[a] - velocity[a]) for a in range(3)]
    if begin:
        *forces, solid = to_columns(drags + [rate])
        aux_ref[0, rows] = 1.0 / (1.0 + solid)
    else:
        forces = to_columns(drags)
    for a, force in enumerate(forces):
        force_ref[a, rows] = force
    keep, take = 1.0 - 1.0 / relax_time, 1.0 / relax_time
    for lanes in tile_lanes(plan):
        density, inverse = u_ref[3, rows, lanes], u_ref[4, rows, lanes]
        scale = aux_ref[0, rows, lanes]
        share = relax_time * inverse
        target = [scale * (u_ref[a, rows, lanes] - share * force_ref[a, rows, lanes]) for a in range(3)]
        square = target[0] * target[0] + target[1] * target[1] + target[2] * target[2]
        base = 1.0 - 1.5 * square
        triple = [3.0 * x for x in target]
        shares = {w: (take * float(w)) * density for w in sorted(set(WEIGHTS))}
        post_ref[0, rows, lanes] = keep * state_ref[0, rows, lanes] + shares[WEIGHTS[0]] * base
        for i in range(1, 19, 2):
            along = None
            for a in range(3):
                if VELOCITIES[i, a] != 0:
                    if along is None:
                        along = triple[a] if VELOCITIES[i, a] == 1 else -triple[a]
                    else:
                        along = along + triple[a] if VELOCITIES[i, a] == 1 else along - triple[a]
            level = base + 0.5 * (along * along)
            share_i = shares[WEIGHTS[i]]
            post_ref[i, rows, lanes] = keep * state_ref[i, rows, lanes] + share_i * (level + along)
            post_ref[i + 1, rows, lanes] = keep * state_ref[i + 1, rows, lanes] + share_i * (level - along)
    return drags


def move_grains(near, state_ref, aux_ref, rows, drags, begin=False):
    live = (state_ref[FIELD_RATE, rows] > 0.0).astype(jnp.float32)
    velocity = [state_ref[field, rows] for field in FIELD_V]
    moving = [velocity[a] * live for a in range(3)]
    if begin:
        *moving, count = near(moving + [live])
        aux_ref[1, rows] = count
    else:
        moving = near(moving)
        count = aux_ref[1, rows]
    for a in range(3):
        push = contact_stiffness * live * (moving[a] - count * velocity[a])
        updated = velocity[a] + drags[a] + push
        if a == 2:
            updated = updated - gravity * live
        state_ref[FIELD_V[a], rows] = updated


def stream_rows(plan, state_ref, post_ref, keep=None):
    window, layer = plan.place()
    ground = (window == 0) & (layer == 0)
    ceiling = (window == plan.sources - 1) & (layer == plan.n_gz - 1)
    rows, group, dx, dy = plan.rows, plan.group, plan.dx, plan.dy
    lane = lax.broadcasted_iota(jnp.int32, (rows, LANES), 1)
    row = lax.broadcasted_iota(jnp.int32, (rows, LANES), 0)
    lane_y = lax.div(lane, group) * dy + lax.rem(lane, dy)
    lane_x = lax.rem(lax.div(lane, dy), dx)
    bottom, top = ground & (row == 0), ceiling & (row == plan.own - 1)
    tiles = tile_lanes(plan)
    for i in range(19):
        cx, cy, cz = (int(c) for c in VELOCITIES[i])
        take = rows if cz or keep is None else keep
        moved = [post_ref[i, :take, lanes] for lanes in tiles]
        if cx or cy:
            y = lax.rem(lane_y - cy + plan.n_gy * dy, plan.n_gy * dy)
            x = lax.rem(lane_x - cx + dx, dx)
            from_lane = lax.div(y, dy) * group + x * dy + lax.rem(y, dy)
            from_lane = from_lane[:take]
            moved = [jnp.take_along_axis(x, from_lane, axis=1, mode="promise_in_bounds") for x in moved]
        if cx:
            edge = lane_x[:take] == (0 if cx == 1 else dx - 1)
            moved = [jnp.where(edge, moved[(q - cx) % len(tiles)], moved[q]) for q in range(len(tiles))]
        for x, lanes in zip(moved, tiles):
            if cz:
                x = pltpu.roll(x, cz % rows, 0)
                x = jnp.where(bottom if cz == 1 else top, post_ref[OPPOSITE[i], :, lanes], x)
            state_ref[i, :keep, lanes] = x[:keep]


def settle_kernel(plan, in_ref, state_ref, post_ref, aux_ref, column_ref, u_ref, force_ref):
    own = slice(0, plan.own)

    def own_tile(s, t):
        return jnp.concatenate([half_tile(in_ref, s, t, 0), half_tile(in_ref, s, t, 1)], axis=0)

    unpack(plan, own_tile, state_ref, own)
    column_ref[...] = bins_on_columns(plan.columns, state_ref[FIELD_CELL, 0:1, :])
    drags = collide_rows(
        plan,
        lambda parts: two_part_dot(parts, column_ref[...]),
        state_ref, post_ref, aux_ref, u_ref, force_ref, own, True,
    )
    for a in range(3):
        aux_ref[2 + a, own] = drags[a]


def contact_kernel(plan, in_ref, inner_ref, settled_ref, fixed_ref, state_ref, aux_ref, link_ref, packed_ref):
    window, _ = plan.place()
    even = lax.rem(window, 2) == 0
    own = slice(0, plan.own)

    def packed(s):
        mine, sibling = half_tile(in_ref, s, plan.tiles, 0), inner_ref[s, :, plan.width :]
        return jnp.concatenate([jnp.where(even, mine, sibling), jnp.where(even, sibling, mine)], axis=0)

    for s in range(plan.sources):
        packed_ref[s] = packed(s)
    contact_blocks(plan, lambda s: packed_ref[s], link_ref)
    drags = [aux_ref[2 + a, own] for a in range(3)]
    move_grains(lambda parts: touching(plan, parts, link_ref), state_ref, aux_ref, own, drags, True)


def both_layers(plan, product, own_matrix, other_matrix):
    window, _ = plan.place()
    halo_row = lax.broadcasted_iota(jnp.int32, (SUBLANES, plan.columns), 0)
    last, first = window == plan.sources - 1, window == 0
    foreign = (last & (halo_row < plan.halo)) | (first & (halo_row >= plan.halo))
    own = plan.own

    def call(parts):
        mine = product(parts, own_matrix)
        others = product([x[-SUBLANES:] for x in parts], other_matrix)
        if parts[0].shape[0] == SUBLANES:
            return [jnp.where(foreign, b, a) for a, b in zip(mine, others)]
        return [jnp.concatenate([a[:own], jnp.where(foreign, b, a[own:])], axis=0) for a, b in zip(mine, others)]

    return call


def columns_of(plan, column_ref, other_column_ref):
    return both_layers(plan, lambda x, m: two_part_dot(x, m[...]), column_ref, other_column_ref)


def halo_kernel(plan, settled_ref, collided_ref, fixed_ref, column_ref, inner_ref, outer_ref,
                state_ref, post_ref, aux_ref, other_column_ref, u_ref, force_ref):
    rows, own = plan.rows, plan.own
    window, _ = plan.place()
    even = lax.rem(window, 2) == 0
    beyond = slice(own, rows)

    def halo_tile(s, t):
        at = slice(t * LANES, (t + 1) * LANES)
        inner, outer = inner_ref[s, :, at], outer_ref[s, :, at]
        return jnp.concatenate([jnp.where(even, inner, outer), jnp.where(even, outer, inner)], axis=0)

    unpack(plan, halo_tile, state_ref, beyond)
    other_cells = jnp.where(window == 0, state_ref[FIELD_CELL, rows - 1 : rows, :], state_ref[FIELD_CELL, own : own + 1, :])
    other_column_ref[...] = bins_on_columns(plan.columns, other_cells)
    to_columns = columns_of(plan, column_ref, other_column_ref)
    drags = collide_rows(plan, to_columns, state_ref, post_ref, aux_ref, u_ref, force_ref, beyond, True)
    for a in range(3):
        aux_ref[2 + a, beyond] = drags[a]
    stream_rows(plan, state_ref, post_ref)


def substeps_kernel(plan, settled_ref, fixed_ref, column_ref, other_column_ref, link_ref, packed_ref,
                    out_ref, state_ref, aux_ref, post_ref, u_ref, force_ref, other_link_ref):
    rows, own, halo, group, per = plan.rows, plan.own, plan.halo, plan.group, plan.per_tile
    beyond = slice(own, rows)
    contact_blocks(plan, lambda s: packed_ref[s], other_link_ref)
    to_columns = columns_of(plan, column_ref, other_column_ref)
    near = both_layers(plan, lambda x, m: touching(plan, x, m), link_ref, other_link_ref)
    move_grains(near, state_ref, aux_ref, beyond, [aux_ref[2 + a, beyond] for a in range(3)], True)
    refs = (state_ref, post_ref, aux_ref, u_ref, force_ref)

    everywhere, mine = slice(0, rows), slice(0, own)
    for step in range(1, SUBSTEPS):
        drags = collide_rows(plan, to_columns, *refs, everywhere)
        if step < SUBSTEPS - 1:
            move_grains(near, state_ref, aux_ref, everywhere, drags)
            stream_rows(plan, state_ref, post_ref)
        else:
            own_near = functools.partial(touching, plan, matrix=link_ref)
            move_grains(own_near, state_ref, aux_ref, mine, [d[mine] for d in drags])
            stream_rows(plan, state_ref, post_ref, own)

    first_half = lax.broadcasted_iota(jnp.int32, (halo, LANES), 1) < LANES // 2
    for t in range(plan.tiles):
        sets = [[state_ref[t * per + j, 0:own, lanes] for j in range(per)] for lanes in tile_lanes(plan)]
        for q, parts in enumerate(swap_groups(sets, group)):
            for s, part in enumerate(parts):
                low, high = part[:halo], part[halo:]
                if t == plan.tiles - 1:
                    pieces = [jnp.where(first_half, low, pltpu.roll(high, LANES // 2, 1))]
                else:
                    pieces = [low, high]
                for k, piece in enumerate(pieces):
                    start = (2 * t + k) * LANES
                    out_ref[q * per + s, :, start : start + LANES] = piece


def finish_kernel(plan, in_ref, pop_ref, vel_ref, stage, sems):
    whole = 19 * plan.group // LANES
    end = 19 * plan.group
    split = whole * LANES // 2
    holders = [plan.holder(q) for q in range(plan.sources)]
    moves = {
        plan.tiles - 1: (stage.at[end : end + 3 * plan.bins], vel_ref),
        whole // 2 - 1: (stage.at[:split], pop_ref.at[:split]),
        whole - 1: (stage.at[split:end], pop_ref.at[split:]),
    }
    copies = []
    for t in (whole, whole + 1, *range(whole)):
        pieces = []
        for holder in holders:
            start = 2 * t * LANES
            low = in_ref[holder, :, start : start + LANES]
            if t == plan.tiles - 1:
                high = pltpu.roll(low, LANES // 2, 1)
            else:
                high = in_ref[holder, :, start + LANES : start + 2 * LANES]
            pieces += [low, high]
        stage[t * LANES : (t + 1) * LANES, :] = jnp.concatenate(pieces, axis=0).T
        if t in moves:
            copies.append(pltpu.make_async_copy(*moves[t], sems.at[len(copies)]))
            copies[-1].start()
    for copy in copies:
        copy.wait()


def windows_body(plan, populations, grain_velocity, grain_volume, slots, contacts, bin_cell):
    group, bins, sources = plan.group, plan.bins, plan.sources
    rows, columns, own = plan.rows, plan.columns, plan.own
    f32, bf16, i32 = jnp.float32, jnp.bfloat16, jnp.int32
    halo = plan.halo

    def call(kernel, shapes, inputs, scratch=(), where=(VMEM, VMEM), aliases=None):
        if where[0] is HBM:
            inputs = [pltpu.with_memory_space_constraint(x, pltpu.HBM) for x in inputs]
        shapes = [jax.ShapeDtypeStruct(shape, kind) for shape, kind in shapes]
        return pl.pallas_call(
            lambda *refs: kernel(plan, *refs),
            out_shape=shapes,
            in_specs=[where[0]] * len(inputs),
            out_specs=[where[1]] * len(shapes),
            scratch_shapes=list(scratch),
            input_output_aliases=aliases or {},
            compiler_params=pltpu.CompilerParams(vmem_limit_bytes=VMEM_LIMIT),
        )(*inputs)

    (outgoing,) = call(
        prepare_kernel,
        [((sources, halo, plan.wide), f32)],
        (
            populations.reshape(19 * group, LANES),
            grain_velocity.reshape(3 * bins, LANES),
            grain_volume,
            slots,
            contacts,
            bin_cell.reshape(1, bins),
        ),
        (
            pltpu.VMEM((plan.width, LANES), f32),
            pltpu.VMEM((bins, LANES), i32),
            pltpu.VMEM((bins, bins), i32),
            pltpu.VMEM((1, bins), i32),
            pltpu.SemaphoreType.DMA((16,)),
        ),
        (HBM, VMEM),
    )
    layer_axes, every_axis = ("gx", "gy"), ("gx", "gy", "gz")
    incoming = lax.all_to_all(outgoing, layer_axes, split_axis=0, concat_axis=0, tiled=True)
    inner, outer = call(
        edges_kernel,
        [((sources, halo, plan.width + LANES), f32), ((sources, halo, plan.width), f32)],
        (incoming,),
    )
    inner = lax.ppermute(inner, every_axis, plan.swaps(0))
    outer = lax.ppermute(outer, every_axis, plan.swaps(1))
    carried = [
        ((plan.fields, rows, columns), f32),
        ((19, rows, columns), f32),
        ((5, rows, columns), f32),
    ]
    moments_and_forces = (pltpu.VMEM((5, rows, columns), f32), pltpu.VMEM((3, rows, columns), f32))
    state, post, aux, column = call(
        settle_kernel,
        carried + [((columns, columns), bf16)],
        (incoming,),
        moments_and_forces,
    )
    state, aux, link, packed = call(
        contact_kernel,
        [carried[0], carried[2], ((columns, LANES), bf16), ((sources, SUBLANES, LANES), f32)],
        (incoming, inner, state, aux),
        aliases={2: 0, 3: 1},
    )
    packed = lax.ppermute(packed, every_axis, plan.swaps(1))
    state, _, aux, other_column = call(
        halo_kernel,
        carried + [((columns, columns), bf16)],
        (state, post, aux, column, inner, outer),
        moments_and_forces,
        aliases={0: 0, 1: 1, 2: 2},
    )
    back, *_ = call(
        substeps_kernel,
        [((sources, halo, plan.returned), f32), carried[0], carried[2]],
        (state, aux, column, other_column, link, packed),
        (
            pltpu.VMEM((19, rows, columns), f32),
            *moments_and_forces,
            pltpu.VMEM((columns, LANES), bf16),
        ),
        aliases={0: 1, 1: 2},
    )
    result = lax.all_to_all(back, layer_axes, split_axis=0, concat_axis=0, tiled=True)
    fluid, velocity = call(
        finish_kernel,
        [((19 * group, LANES), f32), ((3 * bins, LANES), f32)],
        (result,),
        (pltpu.VMEM((plan.width, LANES), f32), pltpu.SemaphoreType.DMA((16,))),
        (VMEM, HBM),
    )
    return (fluid.reshape(populations.shape), velocity.reshape(grain_velocity.shape))


def body(populations, grain_velocity, grain_volume, slots, contacts, bin_cell):
    plan = Plan(
        lax.axis_size("gx"),
        lax.axis_size("gy"),
        lax.axis_size("gz"),
        populations,
        contacts,
        grain_velocity.shape[2],
    )
    arrays = (populations, grain_velocity, grain_volume, slots, contacts, bin_cell)
    if plan.fits() and contacts.shape[0] == contacts.shape[1]:
        return windows_body(plan, *arrays)
    return columns_body(*arrays)


def solution(mesh):
    placed = (
        P(None, "gx", "gy", "gz"),
        P(None, ("gx", "gy", "gz"), None),
        P(("gx", "gy", "gz"), None),
        P(("gx", "gy", "gz"), None),
        P(("gx", "gy", "gz"), None),
        P(("gx", "gy", "gz")),
    )
    return jax.shard_map(
        body,
        mesh=mesh,
        in_specs=placed,
        out_specs=(P(None, "gx", "gy", "gz"), P(None, ("gx", "gy", "gz"), None)),
        check_vma=False,
    )
```

```python
import functools
import jax
import jax.numpy as jnp
import numpy as np
from jax import lax
from jax.experimental import pallas as pl
from jax.experimental.pallas import tpu as pltpu
from jax.sharding import PartitionSpec as P

SUBSTEPS = 4


VELOCITIES = np.array(
    [
        [0, 0, 0],
        [1, 0, 0],
        [-1, 0, 0],
        [0, 1, 0],
        [0, -1, 0],
        [0, 0, 1],
        [0, 0, -1],
        [1, 1, 0],
        [-1, -1, 0],
        [1, -1, 0],
        [-1, 1, 0],
        [1, 0, 1],
        [-1, 0, -1],
        [1, 0, -1],
        [-1, 0, 1],
        [0, 1, 1],
        [0, -1, -1],
        [0, 1, -1],
        [0, -1, 1],
    ]
)
WEIGHTS = np.array([1.0 / 3.0] + [1.0 / 18.0] * 6 + [1.0 / 36.0] * 12)
OPPOSITE = [0, 2, 1, 4, 3, 6, 5, 8, 7, 10, 9, 12, 11, 14, 13, 16, 15, 18, 17]
relax_time = 0.8
contact_stiffness = 0.1
drag_factor = 2.0
gravity = 0.01


def passed_along(x, axis, by):
    length = lax.axis_size(axis)
    return lax.ppermute(x, axis, [(i, (i + by) % length) for i in range(length)])


def passed_along_2(value, axis, steps):
    count = lax.axis_size(axis)
    leading, last = (max(0, -steps), min(count, count - steps))
    return lax.ppermute(value, axis, [(source, source + steps) for source in range(leading, last)])


def moments(popul):
    density = jnp.sum(popul, axis=0)
    speed = []
    for axis in range(3):
        rising = np.array([i for i in range(19) if VELOCITIES[i, axis] == 1])
        falling = np.array([i for i in range(19) if VELOCITIES[i, axis] == -1])
        momentum = jnp.sum(popul[rising], axis=0) - jnp.sum(popul[falling], axis=0)
        speed.append(momentum / density)
    return (density, speed)


def grain_step(block, velocity, live, volume, links):
    grains = velocity.shape[2]
    bins = links.shape[1]
    groups = velocity.shape[1] // bins
    rate = drag_factor * volume * live
    drag = rate[None] * (block[:3] - velocity)
    moving = (velocity * live[None]).reshape(3, groups, bins, grains)
    pairs = links.reshape(groups, bins, bins)
    near = jnp.einsum("gkj,cgjs->cgks", pairs, moving, precision=lax.Precision.HIGHEST).reshape(
        3, -1, grains
    )
    count = jnp.einsum(
        "gkj,gjs->gks", pairs, live.reshape(groups, bins, grains), precision=lax.Precision.HIGHEST
    ).reshape(-1, grains)
    push = contact_stiffness * live[None] * (near - count[None] * velocity)
    fall = jnp.asarray([0.0, 0.0, gravity], jnp.float32).reshape(3, 1, 1) * live[None]
    updated = velocity + drag + push - fall
    forces = jnp.concatenate([-drag, (volume * live)[None]], axis=0)
    return (updated, forces)


def collide(popul, density, speed, field):
    scale = 1.0 / (1.0 + field[3])
    target = [scale * (speed[a] + relax_time * field[a] / density) for a in range(3)]
    square = target[0] * target[0] + target[1] * target[1] + target[2] * target[2]
    rows = []
    for i in range(19):
        along = jnp.zeros_like(density)
        for a in range(3):
            if VELOCITIES[i, a] != 0:
                along = along + float(VELOCITIES[i, a]) * target[a]
        equil = (
            float(WEIGHTS[i]) * density * (1.0 + 3.0 * along + 4.5 * along * along - 1.5 * square)
        )
        rows.append(popul[i] - (popul[i] - equil) / relax_time)
    return jnp.stack(rows)


def walls(moved, post):
    depth = post.shape[3]
    zpos = jnp.arange(depth)
    bottom = (zpos == 0) & (lax.axis_index("gz") == 0)
    top = (zpos == depth - 1) & (lax.axis_index("gz") == lax.axis_size("gz") - 1)
    rows = []
    for i in range(19):
        layer = moved[i]
        if VELOCITIES[i, 2] == 1:
            layer = jnp.where(bottom, post[OPPOSITE[i]], layer)
        elif VELOCITIES[i, 2] == -1:
            layer = jnp.where(top, post[OPPOSITE[i]], layer)
        rows.append(layer)
    return jnp.stack(rows)


def leaving(axis):
    rising = np.array([i for i in range(19) if VELOCITIES[i, axis] == 1])
    falling = np.array([i for i in range(19) if VELOCITIES[i, axis] == -1])
    return (rising, falling)


def stream(post):
    moved = post
    rising, falling = leaving(0)
    upper = moved[rising]
    lower = moved[falling]
    edge_up = passed_along(upper[:, -1:], "gx", 1)
    edge_down = passed_along(lower[:, :1], "gx", -1)
    moved = moved.at[rising].set(jnp.concatenate([edge_up, upper[:, :-1]], axis=1))
    moved = moved.at[falling].set(jnp.concatenate([lower[:, 1:], edge_down], axis=1))
    rising, falling = leaving(1)
    upper = moved[rising]
    lower = moved[falling]
    edge_up = passed_along(upper[:, :, -1:], "gy", 1)
    edge_down = passed_along(lower[:, :, :1], "gy", -1)
    moved = moved.at[rising].set(jnp.concatenate([edge_up, upper[:, :, :-1]], axis=2))
    moved = moved.at[falling].set(jnp.concatenate([lower[:, :, 1:], edge_down], axis=2))
    rising, falling = leaving(2)
    upper = moved[rising]
    lower = moved[falling]
    edge_up = passed_along_2(upper[:, :, :, -1:], "gz", 1)
    edge_down = passed_along_2(lower[:, :, :, :1], "gz", -1)
    moved = moved.at[rising].set(jnp.concatenate([edge_up, upper[:, :, :, :-1]], axis=3))
    moved = moved.at[falling].set(jnp.concatenate([lower[:, :, :, 1:], edge_down], axis=3))
    return walls(moved, post)


def carry_flow(outgoing):
    result = lax.all_to_all(outgoing, ("gx", "gy"), split_axis=1, concat_axis=1, tiled=True)
    return result


def carry_force(outgoing):
    result = lax.all_to_all(outgoing, ("gx", "gy"), split_axis=1, concat_axis=1, tiled=True)
    return result


def rank_within(source):
    count = source.shape[-1]
    before = jnp.arange(count)[None, :] < jnp.arange(count)[:, None]
    same = source[..., :, None] == source[..., None, :]
    return jnp.sum((same & before).astype(jnp.int32), axis=-1)


def columns_body(populations, grain_velocity, grain_volume, slots, contacts, bin_cell):
    n_gx = lax.axis_size("gx")
    n_gy = lax.axis_size("gy")
    n_gz = lax.axis_size("gz")
    sources = n_gx * n_gy
    bins = contacts.shape[1]
    grains = grain_velocity.shape[2]
    depth_x, depth_y, depth_z = (populations.shape[1], populations.shape[2], populations.shape[3])
    zblocks = depth_z // grains
    capacity = max(2, 4 * bins // sources)
    width_y = depth_y * n_gy
    column_blocks = depth_z * n_gz // grains

    def locate(cells):
        xcell = cells // (width_y * column_blocks)
        ycell = cells // column_blocks % width_y
        zblock = cells % column_blocks
        source = xcell // depth_x * n_gy + ycell // depth_y
        local = (xcell % depth_x * depth_y + ycell % depth_y) * zblocks + zblock % zblocks
        return (source, local)

    own_source, _ = locate(bin_cell)
    own_row = own_source * capacity + rank_within(own_source)
    every = lax.all_gather(bin_cell, ("gx", "gy"), axis=0, tiled=True).reshape(sources, bins)
    all_source, all_local = locate(every)
    all_rank = rank_within(all_source)
    here = lax.axis_index("gx") * n_gy + lax.axis_index("gy")
    slot_ids = jnp.arange(capacity, dtype=jnp.int32)
    picked = (all_source == here)[:, None, :] & (all_rank[:, None, :] == slot_ids[None, :, None])
    send_column = jnp.sum(jnp.where(picked, all_local[:, None, :], 0), axis=2).reshape(-1)
    send_mask = jnp.any(picked, axis=2).reshape(-1).astype(jnp.float32)
    live = slots.astype(jnp.float32)
    links = contacts.astype(jnp.float32)
    fluid = populations
    velocity = grain_velocity
    for _ in range(SUBSTEPS):
        density, speed = moments(fluid)
        flow = jnp.stack(speed + [density]).reshape(4, -1, grains)
        outgoing = jnp.take(flow, send_column, axis=1) * send_mask[None, :, None]
        incoming = carry_flow(outgoing)
        block = jnp.take(incoming, own_row, axis=1)
        velocity, forces = grain_step(block, velocity, live, grain_volume, links)
        back = jnp.zeros((4, sources * capacity, grains), jnp.float32).at[:, own_row].set(forces)
        returned = carry_force(back)
        field = jnp.zeros_like(flow).at[:, send_column].add(returned * send_mask[None, :, None])
        field = field.reshape(4, depth_x, depth_y, depth_z)
        post = collide(fluid, density, speed, field)
        fluid = stream(post)
    return (fluid, velocity)


LANES = 128
SUBLANES = 8
VMEM_LIMIT = 24 * 1024 * 1024
VMEM = pl.BlockSpec(memory_space=pltpu.VMEM)
HBM = pl.BlockSpec(memory_space=pltpu.HBM)
FIELD_V = (19, 20, 21)
FIELD_CELL = 22
FIELD_RATE = 23


class Plan:
    def __init__(self, n_gx, n_gy, n_gz, populations, contacts, grains):
        self.n_gx, self.n_gy, self.n_gz = n_gx, n_gy, n_gz
        self.dx, self.dy, self.depth = populations.shape[1:]
        self.grains = grains
        self.bins = contacts.shape[1]
        self.sources = n_gx * n_gy
        self.group = self.dx * self.dy
        self.halo = SUBSTEPS
        self.own = self.depth // self.sources
        self.rows = self.own + 2 * self.halo
        self.columns = self.sources * self.group
        self.per_tile = max(1, LANES // self.group)
        self.fields = 24
        self.tiles = self.fields // self.per_tile
        self.width = self.fields * self.group
        self.wide = (2 * self.tiles + 1) * LANES
        self.returned = (2 * self.tiles - 1) * LANES

    def fits(self):
        group = self.group
        return (
            self.sources % 2 == 0
            and self.depth == LANES
            and self.grains == LANES
            and self.own * self.sources == LANES
            and self.own == SUBLANES == 2 * self.halo
            and self.rows == 2 * SUBLANES
            and group == self.bins
            and group * group == SUBLANES * LANES
            and self.per_tile == self.n_gy
        )

    def along(self, window):
        gx, r = divmod(window, self.n_gy)
        return gx * self.n_gy + (self.n_gy - 1 - r if gx % 2 else r)

    def device(self, window):
        layer, local = divmod(window, self.sources)
        if layer % 2:
            local = self.sources - 1 - local
        return self.along(local) * self.n_gz + layer

    def swaps(self, start):
        count = self.n_gz * self.sources
        paired = []
        for a in range(start, count - 1, 2):
            paired += [(a, a + 1), (a + 1, a)]
        if start:
            paired += [(0, count - 1), (count - 1, 0)]
        return [(self.device(a), self.device(b)) for a, b in paired]

    def place(self):
        gx, gy, layer = (lax.axis_index(name) for name in ("gx", "gy", "gz"))
        local = gx * self.n_gy + jnp.where(lax.rem(gx, 2) == 1, self.n_gy - 1 - gy, gy)
        return jnp.where(lax.rem(layer, 2) == 1, self.sources - 1 - local, local), layer

    def holder(self, window):
        odd = lax.rem(lax.axis_index("gz"), 2) == 1
        return jnp.where(odd, self.along(self.sources - 1 - window), self.along(window))


def pick(group, parts):
    lane = lax.broadcasted_iota(jnp.int32, parts[0].shape, 1) // group
    step = 1
    while len(parts) > 1:
        odd = lane // step % 2 == 1
        parts = [jnp.where(odd, b, a) for a, b in zip(parts[::2], parts[1::2])]
        step *= 2
    return parts[0]


def turned_groups(parts, group):
    count = len(parts)
    turned = []
    for r in range(count):
        chosen = pick(group, [parts[(g + r) % count] for g in range(count)])
        turned.append(pltpu.roll(chosen, r * group, 1) if r else chosen)
    return turned


def swap_groups(sets, group):
    turned = [turned_groups(parts, group) for parts in sets]
    count = len(sets[0])
    return [[pick(group, [t[(g - j) % count] for g in range(count)]) for j in range(count)] for t in turned]


def prepare_kernel(plan, pop_ref, vel_ref, vol_ref, slot_ref, link_ref, cell_ref, out_ref,
                   pops, slots, links, cells, sems):
    group, bins, own, halo = plan.group, plan.bins, plan.own, plan.halo
    whole = 19 * group // LANES
    end = plan.width
    vel_start = 19 * group
    split = whole * LANES // 2
    moves = [
        (cell_ref, cells),
        (link_ref, links),
        (slot_ref, slots),
        (vol_ref, pops.at[end - bins : end]),
        (vel_ref, pops.at[vel_start : vel_start + 3 * bins]),
        (pop_ref.at[split:], pops.at[split:vel_start]),
        (pop_ref.at[:split], pops.at[:split]),
    ]
    copies = [pltpu.make_async_copy(a, b, sems.at[i]) for i, (a, b) in enumerate(moves)]
    for copy in copies:
        copy.start()
    for copy in copies:
        copy.wait()

    cell = cells[...]
    width_y = plan.dy * plan.n_gy
    xcell = lax.div(cell, width_y * plan.n_gz)
    ycell = lax.rem(lax.div(cell, plan.n_gz), width_y)
    source = lax.div(xcell, plan.dx) * plan.n_gy + lax.div(ycell, plan.dy)
    cell = source * group + lax.rem(xcell, plan.dx) * plan.dy + lax.rem(ycell, plan.dy)
    blank = jnp.zeros((1, bins), jnp.float32)
    cell = jnp.concatenate([blank, blank, cell.astype(jnp.float32), blank], axis=1)
    packed = jnp.concatenate(
        [links[g * SUBLANES : (g + 1) * SUBLANES, :].astype(jnp.float32) for g in range(bins // SUBLANES)],
        axis=1,
    )
    holders = [plan.holder(q) for q in range(plan.sources)]
    for q in range(plan.sources):
        part = q % 2 * halo
        out_ref[holders[q], :, 2 * plan.width :] = packed[part : part + halo, :]
    for t in range(plan.tiles):
        block = pops[t * LANES : (t + 1) * LANES, :]
        if t == plan.tiles - 1:
            rate = pops[end - bins : end, :] * slots[...].astype(jnp.float32)
            block = jnp.concatenate([block[: 2 * bins], rate, rate], axis=0)
        block = block.T
        if t == plan.tiles - 1:
            lane = lax.broadcasted_iota(jnp.int32, block.shape, 1) // bins
            block = jnp.where(lane == FIELD_CELL % plan.per_tile, cell, block)
        for q in range(plan.sources):
            for k in range(2):
                start, row = (2 * t + k) * LANES, q * own + k * halo
                out_ref[holders[q], :, start : start + LANES] = block[row : row + halo, :]


def half_tile(ref, s, t, k):
    start = (2 * t + k) * LANES
    return ref[s, :, start : start + LANES]


def edges_kernel(plan, in_ref, inner_ref, outer_ref):
    window, _ = plan.place()
    even = lax.rem(window, 2) == 0
    for s in range(plan.sources):
        for t in range(plan.tiles):
            lanes = slice(t * LANES, (t + 1) * LANES)
            low, high = half_tile(in_ref, s, t, 0), half_tile(in_ref, s, t, 1)
            inner_ref[s, :, lanes] = jnp.where(even, high, low)
            outer_ref[s, :, lanes] = jnp.where(even, low, high)
        inner_ref[s, :, plan.width :] = half_tile(in_ref, s, plan.tiles, 0)


def two_part_dot(parts, matrix):
    whole = jnp.concatenate(parts, axis=0)
    rest = whole - whole.astype(jnp.bfloat16).astype(jnp.float32)
    stacked = jnp.concatenate([whole, rest], axis=0).astype(jnp.bfloat16)
    out = lax.dot_general(
        stacked, matrix, (((1,), (1,)), ((), ())), preferred_element_type=jnp.float32
    )
    rows = parts[0].shape[0]
    half = rows * len(parts)
    return [
        out[i * rows : (i + 1) * rows] + out[half + i * rows : half + (i + 1) * rows]
        for i in range(len(parts))
    ]


def bins_on_columns(columns, cells):
    which = lax.broadcasted_iota(jnp.int32, (columns, columns), 0).astype(jnp.float32)
    return (which == cells).astype(jnp.float32).astype(jnp.bfloat16)


def contact_blocks(plan, packed, link_ref):
    group, per = plan.group, plan.per_tile
    lane = lax.broadcasted_iota(jnp.int32, (SUBLANES, LANES), 1) // group
    for q in range(0, plan.sources, per):
        turned = turned_groups([packed(s) for s in range(q, q + per)], group)
        for s in range(per):
            pieces = [jnp.where(lane == s, turned[(s - g) % per], 0.0) for g in range(per)]
            start = (q + s) * group
            link_ref[start : start + group, :] = jnp.concatenate(pieces, axis=0).astype(jnp.bfloat16)


def unpack(plan, tile_of, state_ref, rows):
    per = plan.per_tile
    for t in range(plan.tiles):
        sets = [[tile_of(s, t) for s in range(q, q + per)] for q in range(0, plan.sources, per)]
        for q, parts in enumerate(swap_groups(sets, plan.group)):
            for j, part in enumerate(parts):
                state_ref[t * per + j, rows, q * LANES : (q + 1) * LANES] = part


def touching(plan, parts, matrix):
    quads = plan.sources // plan.per_tile
    blocks = []
    for q in range(quads):
        at = slice(q * LANES, (q + 1) * LANES)
        blocks.append(two_part_dot([x[:, at] for x in parts], matrix[at, :]))
    return [jnp.concatenate([b[i] for b in blocks], axis=1) for i in range(len(parts))]


def tile_lanes(plan):
    return [slice(q * LANES, (q + 1) * LANES) for q in range(plan.sources // plan.per_tile)]


def on_bins(plan, fields, cells):
    tiles = tile_lanes(plan)
    cells = cells.astype(jnp.int32)
    lane, tile = lax.rem(cells, LANES), lax.div(cells, LANES)
    out = []
    for x in fields:
        pieces = []
        for to in tiles:
            found = None
            for q, at in enumerate(tiles):
                moved = jnp.take_along_axis(x[:, at], lane[:, to], axis=1, mode="promise_in_bounds")
                found = moved if found is None else jnp.where(tile[:, to] == q, moved, found)
            pieces.append(found)
        out.append(jnp.concatenate(pieces, axis=1))
    return out


def collide_rows(plan, to_columns, state_ref, post_ref, aux_ref, u_ref, force_ref, rows, begin=False):
    for lanes in tile_lanes(plan):
        popul = [state_ref[i, rows, lanes] for i in range(19)]
        density = popul[0]
        for i in range(1, 19):
            density = density + popul[i]
        inverse = 1.0 / density
        u_ref[3, rows, lanes] = density
        u_ref[4, rows, lanes] = inverse
        for a in range(3):
            rising = [popul[i] for i in range(19) if VELOCITIES[i, a] == 1]
            falling = [popul[i] for i in range(19) if VELOCITIES[i, a] == -1]
            u_ref[a, rows, lanes] = (sum(rising[1:], rising[0]) - sum(falling[1:], falling[0])) * inverse
    rate = state_ref[FIELD_RATE, rows]
    velocity = [state_ref[field, rows] for field in FIELD_V]
    speed = on_bins(plan, [u_ref[a, rows] for a in range(3)], state_ref[FIELD_CELL, rows])
    drags = [drag_factor * rate * (speed[a] - velocity[a]) for a in range(3)]
    if begin:
        *forces, solid = to_columns(drags + [rate])
        aux_ref[0, rows] = 1.0 / (1.0 + solid)
    else:
        forces = to_columns(drags)
    for a, force in enumerate(forces):
        force_ref[a, rows] = force
    keep, take = 1.0 - 1.0 / relax_time, 1.0 / relax_time
    for lanes in tile_lanes(plan):
        density, inverse = u_ref[3, rows, lanes], u_ref[4, rows, lanes]
        scale = aux_ref[0, rows, lanes]
        share = relax_time * inverse
        target = [scale * (u_ref[a, rows, lanes] - share * force_ref[a, rows, lanes]) for a in range(3)]
        square = target[0] * target[0] + target[1] * target[1] + target[2] * target[2]
        base = 1.0 - 1.5 * square
        triple = [3.0 * x for x in target]
        shares = {w: (take * float(w)) * density for w in sorted(set(WEIGHTS))}
        post_ref[0, rows, lanes] = keep * state_ref[0, rows, lanes] + shares[WEIGHTS[0]] * base
        for i in range(1, 19, 2):
            along = None
            for a in range(3):
                if VELOCITIES[i, a] != 0:
                    if along is None:
                        along = triple[a] if VELOCITIES[i, a] == 1 else -triple[a]
                    else:
                        along = along + triple[a] if VELOCITIES[i, a] == 1 else along - triple[a]
            level = base + 0.5 * (along * along)
            share_i = shares[WEIGHTS[i]]
            post_ref[i, rows, lanes] = keep * state_ref[i, rows, lanes] + share_i * (level + along)
            post_ref[i + 1, rows, lanes] = keep * state_ref[i + 1, rows, lanes] + share_i * (level - along)
    return drags


def move_grains(near, state_ref, aux_ref, rows, drags, begin=False):
    live = (state_ref[FIELD_RATE, rows] > 0.0).astype(jnp.float32)
    velocity = [state_ref[field, rows] for field in FIELD_V]
    moving = [velocity[a] * live for a in range(3)]
    if begin:
        *moving, count = near(moving + [live])
        aux_ref[1, rows] = count
    else:
        moving = near(moving)
        count = aux_ref[1, rows]
    for a in range(3):
        push = contact_stiffness * live * (moving[a] - count * velocity[a])
        updated = velocity[a] + drags[a] + push
        if a == 2:
            updated = updated - gravity * live
        state_ref[FIELD_V[a], rows] = updated


def stream_rows(plan, state_ref, post_ref, keep=None):
    window, layer = plan.place()
    ground = (window == 0) & (layer == 0)
    ceiling = (window == plan.sources - 1) & (layer == plan.n_gz - 1)
    rows, group, dx, dy = plan.rows, plan.group, plan.dx, plan.dy
    lane = lax.broadcasted_iota(jnp.int32, (rows, LANES), 1)
    row = lax.broadcasted_iota(jnp.int32, (rows, LANES), 0)
    lane_y = lax.div(lane, group) * dy + lax.rem(lane, dy)
    lane_x = lax.rem(lax.div(lane, dy), dx)
    bottom, top = ground & (row == 0), ceiling & (row == plan.own - 1)
    tiles = tile_lanes(plan)
    for i in range(19):
        cx, cy, cz = (int(c) for c in VELOCITIES[i])
        take = rows if cz or keep is None else keep
        moved = [post_ref[i, :take, lanes] for lanes in tiles]
        if cx or cy:
            y = lax.rem(lane_y - cy + plan.n_gy * dy, plan.n_gy * dy)
            x = lax.rem(lane_x - cx + dx, dx)
            from_lane = lax.div(y, dy) * group + x * dy + lax.rem(y, dy)
            from_lane = from_lane[:take]
            moved = [jnp.take_along_axis(x, from_lane, axis=1, mode="promise_in_bounds") for x in moved]
        if cx:
            edge = lane_x[:take] == (0 if cx == 1 else dx - 1)
            moved = [jnp.where(edge, moved[(q - cx) % len(tiles)], moved[q]) for q in range(len(tiles))]
        for x, lanes in zip(moved, tiles):
            if cz:
                x = pltpu.roll(x, cz % rows, 0)
                x = jnp.where(bottom if cz == 1 else top, post_ref[OPPOSITE[i], :, lanes], x)
            state_ref[i, :keep, lanes] = x[:keep]


def settle_kernel(plan, in_ref, state_ref, post_ref, aux_ref, column_ref, u_ref, force_ref):
    own = slice(0, plan.own)

    def own_tile(s, t):
        return jnp.concatenate([half_tile(in_ref, s, t, 0), half_tile(in_ref, s, t, 1)], axis=0)

    unpack(plan, own_tile, state_ref, own)
    column_ref[...] = bins_on_columns(plan.columns, state_ref[FIELD_CELL, 0:1, :])
    drags = collide_rows(
        plan,
        lambda parts: two_part_dot(parts, column_ref[...]),
        state_ref, post_ref, aux_ref, u_ref, force_ref, own, True,
    )
    for a in range(3):
        aux_ref[2 + a, own] = drags[a]


def pack_kernel(plan, in_ref, inner_ref, packed_ref):
    window, _ = plan.place()
    even = lax.rem(window, 2) == 0
    for s in range(plan.sources):
        mine, sibling = half_tile(in_ref, s, plan.tiles, 0), inner_ref[s, :, plan.width :]
        packed_ref[s] = jnp.concatenate([jnp.where(even, mine, sibling), jnp.where(even, sibling, mine)], axis=0)


def contact_kernel(plan, packed_ref, settled_ref, fixed_ref, state_ref, aux_ref, link_ref):
    own = slice(0, plan.own)
    contact_blocks(plan, lambda s: packed_ref[s], link_ref)
    drags = [aux_ref[2 + a, own] for a in range(3)]
    move_grains(lambda parts: touching(plan, parts, link_ref), state_ref, aux_ref, own, drags, True)


def both_layers(plan, product, own_matrix, other_matrix):
    window, _ = plan.place()
    halo_row = lax.broadcasted_iota(jnp.int32, (SUBLANES, plan.columns), 0)
    last, first = window == plan.sources - 1, window == 0
    foreign = (last & (halo_row < plan.halo)) | (first & (halo_row >= plan.halo))
    own = plan.own

    def call(parts):
        mine = product(parts, own_matrix)
        others = product([x[-SUBLANES:] for x in parts], other_matrix)
        if parts[0].shape[0] == SUBLANES:
            return [jnp.where(foreign, b, a) for a, b in zip(mine, others)]
        return [jnp.concatenate([a[:own], jnp.where(foreign, b, a[own:])], axis=0) for a, b in zip(mine, others)]

    return call


def columns_of(plan, column_ref, other_column_ref):
    return both_layers(plan, lambda x, m: two_part_dot(x, m[...]), column_ref, other_column_ref)


def halo_kernel(plan, settled_ref, collided_ref, fixed_ref, column_ref, inner_ref, outer_ref,
                state_ref, post_ref, aux_ref, other_column_ref, u_ref, force_ref):
    rows, own = plan.rows, plan.own
    window, _ = plan.place()
    even = lax.rem(window, 2) == 0
    beyond = slice(own, rows)

    def halo_tile(s, t):
        at = slice(t * LANES, (t + 1) * LANES)
        inner, outer = inner_ref[s, :, at], outer_ref[s, :, at]
        return jnp.concatenate([jnp.where(even, inner, outer), jnp.where(even, outer, inner)], axis=0)

    unpack(plan, halo_tile, state_ref, beyond)
    other_cells = jnp.where(window == 0, state_ref[FIELD_CELL, rows - 1 : rows, :], state_ref[FIELD_CELL, own : own + 1, :])
    other_column_ref[...] = bins_on_columns(plan.columns, other_cells)
    to_columns = columns_of(plan, column_ref, other_column_ref)
    drags = collide_rows(plan, to_columns, state_ref, post_ref, aux_ref, u_ref, force_ref, beyond, True)
    for a in range(3):
        aux_ref[2 + a, beyond] = drags[a]
    stream_rows(plan, state_ref, post_ref)


def substeps_kernel(plan, settled_ref, fixed_ref, column_ref, other_column_ref, link_ref, packed_ref,
                    out_ref, state_ref, aux_ref, post_ref, u_ref, force_ref, other_link_ref):
    rows, own, halo, group, per = plan.rows, plan.own, plan.halo, plan.group, plan.per_tile
    beyond = slice(own, rows)
    contact_blocks(plan, lambda s: packed_ref[s], other_link_ref)
    to_columns = columns_of(plan, column_ref, other_column_ref)
    near = both_layers(plan, lambda x, m: touching(plan, x, m), link_ref, other_link_ref)
    move_grains(near, state_ref, aux_ref, beyond, [aux_ref[2 + a, beyond] for a in range(3)], True)
    refs = (state_ref, post_ref, aux_ref, u_ref, force_ref)

    everywhere, mine = slice(0, rows), slice(0, own)
    for step in range(1, SUBSTEPS):
        drags = collide_rows(plan, to_columns, *refs, everywhere)
        if step < SUBSTEPS - 1:
            move_grains(near, state_ref, aux_ref, everywhere, drags)
            stream_rows(plan, state_ref, post_ref)
        else:
            own_near = functools.partial(touching, plan, matrix=link_ref)
            move_grains(own_near, state_ref, aux_ref, mine, [d[mine] for d in drags])
            stream_rows(plan, state_ref, post_ref, own)

    first_half = lax.broadcasted_iota(jnp.int32, (halo, LANES), 1) < LANES // 2
    for t in range(plan.tiles):
        sets = [[state_ref[t * per + j, 0:own, lanes] for j in range(per)] for lanes in tile_lanes(plan)]
        for q, parts in enumerate(swap_groups(sets, group)):
            for s, part in enumerate(parts):
                low, high = part[:halo], part[halo:]
                if t == plan.tiles - 1:
                    pieces = [jnp.where(first_half, low, pltpu.roll(high, LANES // 2, 1))]
                else:
                    pieces = [low, high]
                for k, piece in enumerate(pieces):
                    start = (2 * t + k) * LANES
                    out_ref[q * per + s, :, start : start + LANES] = piece


def finish_kernel(plan, in_ref, pop_ref, vel_ref, stage, sems):
    whole = 19 * plan.group // LANES
    end = 19 * plan.group
    split = whole * LANES // 2
    holders = [plan.holder(q) for q in range(plan.sources)]
    moves = {
        plan.tiles - 1: (stage.at[end : end + 3 * plan.bins], vel_ref),
        whole // 2 - 1: (stage.at[:split], pop_ref.at[:split]),
        whole - 1: (stage.at[split:end], pop_ref.at[split:]),
    }
    copies = []
    for t in (whole, whole + 1, *range(whole)):
        pieces = []
        for holder in holders:
            start = 2 * t * LANES
            low = in_ref[holder, :, start : start + LANES]
            if t == plan.tiles - 1:
                high = pltpu.roll(low, LANES // 2, 1)
            else:
                high = in_ref[holder, :, start + LANES : start + 2 * LANES]
            pieces += [low, high]
        stage[t * LANES : (t + 1) * LANES, :] = jnp.concatenate(pieces, axis=0).T
        if t in moves:
            copies.append(pltpu.make_async_copy(*moves[t], sems.at[len(copies)]))
            copies[-1].start()
    for copy in copies:
        copy.wait()


def windows_body(plan, populations, grain_velocity, grain_volume, slots, contacts, bin_cell):
    group, bins, sources = plan.group, plan.bins, plan.sources
    rows, columns = plan.rows, plan.columns
    f32, bf16, i32 = jnp.float32, jnp.bfloat16, jnp.int32
    halo = plan.halo

    def call(kernel, shapes, inputs, scratch=(), where=(VMEM, VMEM), aliases=None):
        if where[0] is HBM:
            inputs = [pltpu.with_memory_space_constraint(x, pltpu.HBM) for x in inputs]
        shapes = [jax.ShapeDtypeStruct(shape, kind) for shape, kind in shapes]
        return pl.pallas_call(
            lambda *refs: kernel(plan, *refs),
            out_shape=shapes,
            in_specs=[where[0]] * len(inputs),
            out_specs=[where[1]] * len(shapes),
            scratch_shapes=list(scratch),
            input_output_aliases=aliases or {},
            compiler_params=pltpu.CompilerParams(vmem_limit_bytes=VMEM_LIMIT),
        )(*inputs)

    (outgoing,) = call(
        prepare_kernel,
        [((sources, halo, plan.wide), f32)],
        (
            populations.reshape(19 * group, LANES),
            grain_velocity.reshape(3 * bins, LANES),
            grain_volume,
            slots,
            contacts,
            bin_cell.reshape(1, bins),
        ),
        (
            pltpu.VMEM((plan.width, LANES), f32),
            pltpu.VMEM((bins, LANES), i32),
            pltpu.VMEM((bins, bins), i32),
            pltpu.VMEM((1, bins), i32),
            pltpu.SemaphoreType.DMA((16,)),
        ),
        (HBM, VMEM),
    )
    layer_axes, every_axis = ("gx", "gy"), ("gx", "gy", "gz")
    incoming = lax.all_to_all(outgoing, layer_axes, split_axis=0, concat_axis=0, tiled=True)
    inner, outer = call(
        edges_kernel,
        [((sources, halo, plan.width + LANES), f32), ((sources, halo, plan.width), f32)],
        (incoming,),
    )
    outer = lax.ppermute(outer, every_axis, plan.swaps(1))
    inner = lax.ppermute(inner, every_axis, plan.swaps(0))
    carried = [
        ((plan.fields, rows, columns), f32),
        ((19, rows, columns), f32),
        ((5, rows, columns), f32),
    ]
    moments_and_forces = (pltpu.VMEM((5, rows, columns), f32), pltpu.VMEM((3, rows, columns), f32))
    state, post, aux, column = call(
        settle_kernel,
        carried + [((columns, columns), bf16)],
        (incoming,),
        moments_and_forces,
    )
    (contacts_here,) = call(pack_kernel, [((sources, SUBLANES, LANES), f32)], (incoming, inner))
    packed = lax.ppermute(contacts_here, every_axis, plan.swaps(1))
    state, aux, link = call(
        contact_kernel,
        [carried[0], carried[2], ((columns, LANES), bf16)],
        (contacts_here, state, aux),
        aliases={1: 0, 2: 1},
    )
    state, _, aux, other_column = call(
        halo_kernel,
        carried + [((columns, columns), bf16)],
        (state, post, aux, column, inner, outer),
        moments_and_forces,
        aliases={0: 0, 1: 1, 2: 2},
    )
    back, *_ = call(
        substeps_kernel,
        [((sources, halo, plan.returned), f32), carried[0], carried[2]],
        (state, aux, column, other_column, link, packed),
        (
            pltpu.VMEM((19, rows, columns), f32),
            *moments_and_forces,
            pltpu.VMEM((columns, LANES), bf16),
        ),
        aliases={0: 1, 1: 2},
    )
    result = lax.all_to_all(back, layer_axes, split_axis=0, concat_axis=0, tiled=True)
    fluid, velocity = call(
        finish_kernel,
        [((19 * group, LANES), f32), ((3 * bins, LANES), f32)],
        (result,),
        (pltpu.VMEM((plan.width, LANES), f32), pltpu.SemaphoreType.DMA((16,))),
        (VMEM, HBM),
    )
    return (fluid.reshape(populations.shape), velocity.reshape(grain_velocity.shape))


def body(populations, grain_velocity, grain_volume, slots, contacts, bin_cell):
    plan = Plan(
        lax.axis_size("gx"),
        lax.axis_size("gy"),
        lax.axis_size("gz"),
        populations,
        contacts,
        grain_velocity.shape[2],
    )
    arrays = (populations, grain_velocity, grain_volume, slots, contacts, bin_cell)
    if plan.fits() and contacts.shape[0] == contacts.shape[1]:
        return windows_body(plan, *arrays)
    return columns_body(*arrays)


def solution(mesh):
    placed = (
        P(None, "gx", "gy", "gz"),
        P(None, ("gx", "gy", "gz"), None),
        P(("gx", "gy", "gz"), None),
        P(("gx", "gy", "gz"), None),
        P(("gx", "gy", "gz"), None),
        P(("gx", "gy", "gz")),
    )
    return jax.shard_map(
        body,
        mesh=mesh,
        in_specs=placed,
        out_specs=(P(None, "gx", "gy", "gz"), P(None, ("gx", "gy", "gz"), None)),
        check_vma=False,
    )
```
